512 devices in a mesh: section: 2 (over z_lo), batch: 16 (over z_hi, x), tensor: 16 (over y, core).
Axes of the slice: x: 4, y: 8, z: 8 (z_hi: 4, z_lo: 2; z = z_hi * 2 + z_lo), core: 2. Of those that a mesh axis runs over, the one named last changes fastest.
Arguments:
- tokens: bfloat16 [4096, 4096], P('batch', ('section', 'tensor')), may hold values from -950 to 950, as said below
- nb_ids: int32 [128, 128], P('batch'), may hold values from 0 to 15999
- nb_index: int32 [64, 2], P('batch'), may hold values from 0 to 7
- table: bfloat16 [16000, 4096], P('batch', ('section', 'tensor')), may hold values from -950 to 950, as said below
- norm_gains: float32 [2, 4096], replicated, may hold values from 0.1 to 1.9
- projections: bfloat16 [2, 2, 4096, 4096], P(None, None, None, ('section', 'tensor')), may hold values from -0.5 to 0.5, as said below
Outputs:
- mixed: bfloat16 [4096, 4096], P('batch', ('section', 'tensor'))
The draws below stay inside these ranges and needn't reach their ends.
Inputs may be any that keep to these rules, and one draw needn't show every extreme that they name: tokens: entries of order one to some hundreds, of both signs. table: entries of order one to some hundreds, of both signs. projections: entries of order D ** -0.5, of both signs.
All inputs are finite; a program needn't handle non-finite values.
Results may differ from the reference program's by a relative error of at most 0.019.
Values may be sent and summed in bfloat16 or wider, within the bound.
No kernel may reach another device: no remote copies, remote signals or barrier semaphores. Data moves between devices by JAX's collectives and lax.ppermute only.
A program may use at most 64 MiB of HBM per device.

```python
import math
import jax
import jax.numpy as jnp
import numpy as np
from jax import lax

D = 4096
HEADS = 32
HEAD_DIM = 128
SPAN = 64
NEIGH = 2
NLEN = 128
SPANS = 4
NBLK = 8
TOKENS = 4096
VOCAB = 16000
N_BATCH = 16


def spread_rows(key, rows, cols):
    first, second, third = jax.random.split(key, 3)
    base = jnp.clip(jax.random.normal(first, (rows, cols), jnp.float32), -4.0, 4.0)
    column = jnp.exp(jax.random.uniform(second, (1, cols), jnp.float32, 0.0, math.log(10.0)))
    row_scale = jnp.exp(jax.random.uniform(third, (rows, 1), jnp.float32, 0.0, math.log(10.0)))
    return base * column * row_scale


def draw_tokens(key, part):
    return spread_rows(jax.random.fold_in(key, 11), TOKENS, D).astype(jnp.bfloat16)


def draw_table(key, part):
    return spread_rows(jax.random.fold_in(key, 23), VOCAB, D).astype(jnp.bfloat16)


def draw_projections(key, part):
    inner = jax.random.fold_in(key, 37)
    base = jnp.clip(jax.random.normal(inner, (2, 2, D, D), jnp.float32), -4.0, 4.0)
    factor = jnp.array([[1.0, 1.0], [1.0, 8.0]], jnp.float32).reshape(2, 2, 1, 1)
    return (base * factor / math.sqrt(D)).astype(jnp.bfloat16)


def plant(values, own_key, least, largest):
    spot = [jax.random.randint(jax.random.fold_in(own_key, axis), (), 0, length) for axis, length in enumerate(values.shape)]
    longest = values.shape.index(max(values.shape))
    next_to = spot[:longest] + [(spot[longest] + 1) % values.shape[longest]] + spot[longest + 1:]
    return values.at[tuple(spot)].set(least).at[tuple(next_to)].set(largest)


def cumulative_ranks(number_of, lean):
    loads = [(1 << 20) // math.isqrt(grade ** lean) + 1 for grade in range(1, number_of + 1)]
    deviation = 1 + sum(loads) // (1 << 30)
    return np.cumsum(np.array([max(1, weight // deviation) for weight in loads]))


def skewed_ids(key, dims, amount, slope):
    listing = cumulative_ranks(amount, slope)
    lot = jax.random.randint(jax.random.fold_in(key, 1), dims, 0, int(listing[amount - 1]))
    grade = jnp.searchsorted(jnp.asarray(listing, jnp.int32), lot, side="right")
    return jax.random.permutation(jax.random.fold_in(key, 2), amount)[grade].astype(jnp.int32)


def setup_inputs(seed: int = 0) -> dict:
    splits = jax.random.split(jax.random.key(seed), 7)
    return {
        "tokens": draw_tokens(jax.random.fold_in(splits[6], 71), 0),
        "nb_ids": plant(skewed_ids(splits[1], (N_BATCH * NBLK, NLEN), VOCAB, 2), jax.random.fold_in(splits[1], 3), 0, VOCAB - 1).astype(jnp.int32),
        "nb_index": plant(jax.random.randint(splits[2], (N_BATCH * SPANS, NEIGH), 0, NBLK), jax.random.fold_in(splits[2], 1), 0, NBLK - 1).astype(jnp.int32),
        "table": draw_table(jax.random.fold_in(splits[6], 71), 0),
        "norm_gains": jnp.clip(1.0 + 0.18 * jax.random.normal(splits[4], (2, D), jnp.float32), 0.1, 1.9),
        "projections": draw_projections(jax.random.fold_in(splits[6], 71), 0),
    }


def rms_norm(values, gain):
    wide = values.astype(jnp.float32)
    square = lax.optimization_barrier(jnp.mean(wide * wide, axis=-1, keepdims=True))
    return (wide * jax.lax.rsqrt(square + 1e-06) * gain).astype(jnp.bfloat16)

def reference(tokens, nb_ids, nb_index, table, norm_gains, projections):
    embedded = jnp.take(table, nb_ids.reshape(-1), axis=0)
    encoded = rms_norm(embedded, norm_gains[0])
    keys = jnp.dot(encoded, projections[0, 0], preferred_element_type=jnp.float32).astype(jnp.bfloat16)
    values = jnp.dot(encoded, projections[0, 1], preferred_element_type=jnp.float32).astype(jnp.bfloat16)
    normed = rms_norm(tokens, norm_gains[1])
    queries = jnp.dot(normed, projections[1, 0], preferred_element_type=jnp.float32).astype(jnp.bfloat16)
    groups = TOKENS // SPAN
    query_blocks = queries.reshape(groups, SPAN, HEADS, HEAD_DIM).astype(jnp.float32)
    owner = jnp.arange(groups, dtype=jnp.int32) // SPANS
    blocks = (nb_index + owner[:, None] * NBLK).astype(jnp.int32)
    key_blocks = keys.reshape(N_BATCH * NBLK, NLEN, HEADS, HEAD_DIM)
    value_blocks = values.reshape(N_BATCH * NBLK, NLEN, HEADS, HEAD_DIM)
    chosen_keys = key_blocks[blocks].reshape(groups, NEIGH * NLEN, HEADS, HEAD_DIM).astype(jnp.float32)
    chosen_values = value_blocks[blocks].reshape(groups, NEIGH * NLEN, HEADS, HEAD_DIM).astype(jnp.float32)
    scores = jnp.einsum('cqhd,ckhd->chqk', query_blocks, chosen_keys) * (1.0 / math.sqrt(HEAD_DIM))
    expo = jnp.exp(scores)
    weights = (expo / lax.optimization_barrier(jnp.sum(expo, axis=-1, keepdims=True))).astype(jnp.bfloat16)
    attended = jnp.einsum('chqk,ckhd->cqhd', weights.astype(jnp.float32), chosen_values)
    attended = attended.astype(jnp.bfloat16).reshape(TOKENS, D)
    return jnp.dot(attended, projections[1, 1].T, preferred_element_type=jnp.float32).astype(jnp.bfloat16)
```

```python
import functools
import math

import jax
import jax.numpy as jnp
from jax import lax
from jax.experimental import pallas as pl
from jax.experimental.pallas import tpu as pltpu
from jax.sharding import Mesh
from jax.sharding import PartitionSpec as P

HEAD_DIM = 128
SPAN = 64
ROWS = 72
SLOTS = 1024
SHARD = 1000
EPS = 1e-06
SCALE = math.log2(math.e) / math.sqrt(HEAD_DIM)
F32 = jnp.float32
BF16 = jnp.bfloat16


def dot(a, b, dims):
    return lax.dot_general(a, b, (dims, ((), ())), preferred_element_type=F32)


def diagonal(shape):
    row = lax.broadcasted_iota(jnp.int32, shape, len(shape) - 2)
    lane = lax.broadcasted_iota(jnp.int32, shape, len(shape) - 1)
    return row == lane % SPAN


def sums_to_row(column):
    row = jnp.sum(jnp.where(diagonal((SPAN, 128)), column, 0.0), axis=0, keepdims=True)
    upper = row.astype(BF16).astype(F32)
    lane = lax.broadcasted_iota(jnp.int32, (1, 128), 1)
    return jnp.where(lane < SPAN, upper, row - upper)


def row_to_sums(row):
    return jnp.sum(jnp.where(diagonal((SPAN, 128)), row, 0.0), axis=1, keepdims=True)


def key_value_kernel(x_ref, gain_ref, wk_ref, wv_ref, keys_ref, values_ref, acc_ref, square_ref):
    step = pl.program_id(0)

    @pl.when(step == 0)
    def _():
        acc_ref[...] = jnp.zeros_like(acc_ref)
        square_ref[...] = jnp.zeros_like(square_ref)

    wide = [x_ref[i].astype(F32) for i in range(2)]
    square_ref[...] += wide[0] * wide[0] + wide[1] * wide[1]
    scaled = [(wide[i] * gain_ref[0, i : i + 1, :]).astype(BF16) for i in range(2)]
    lhs = jnp.concatenate(scaled, axis=1)
    rhs = jnp.concatenate([wk_ref[...], wv_ref[...]], axis=1)
    acc_ref[...] += dot(lhs, rhs, ((1,), (0,)))

    @pl.when(step == pl.num_programs(0) - 1)
    def _():
        mean = jnp.sum(square_ref[...], axis=1, keepdims=True) * (1.0 / 4096)
        out = (acc_ref[...] * lax.rsqrt(mean + EPS)).astype(BF16)
        keys_ref[...] = out[:, :HEAD_DIM]
        values_ref[...] = out[:, HEAD_DIM:]


def project_rows(x, gain, wk, wv):
    blocks, rows, cols = x.shape
    weight = pl.BlockSpec((2 * cols, HEAD_DIM), lambda i: (i, 0))
    whole = pl.BlockSpec((rows, HEAD_DIM), lambda i: (0, 0))
    return pl.pallas_call(
        key_value_kernel,
        grid=(blocks // 2,),
        in_specs=[
            pl.BlockSpec((2, rows, cols), lambda i: (i, 0, 0)),
            pl.BlockSpec((1, 2, cols), lambda i: (i, 0, 0)),
            weight,
            weight,
        ],
        out_specs=[whole, whole],
        out_shape=[jax.ShapeDtypeStruct((rows, HEAD_DIM), BF16)] * 2,
        scratch_shapes=[pltpu.VMEM((rows, 2 * HEAD_DIM), F32), pltpu.VMEM((rows, cols), F32)],
        name="project_rows",
    )(x, gain.reshape(blocks // 2, 2, cols), wk, wv)


def attend_kernel(q_ref, keys_ref, values_ref, count_ref, out_ref):
    bias = jnp.log2(count_ref[0].astype(F32))
    scores = dot(q_ref[...], keys_ref[...], ((1,), (1,)))
    spread = jnp.broadcast_to(bias[:, None, :], (4, SPAN, SLOTS)).reshape(4 * SPAN, SLOTS)
    expo = jnp.exp2(scores * SCALE + spread)
    total = jnp.sum(expo, axis=1, keepdims=True)
    inverse = jnp.where(total > 0.0, 1.0 / total, 0.0)
    weights = (expo * inverse).astype(BF16)
    part = dot(weights, values_ref[...], ((1,), (0,))).astype(BF16)
    for j in range(4):
        rows = slice(j * SPAN, (j + 1) * SPAN)
        out_ref[0, j // 2, 0, j % 2, :SPAN, :] = part[rows]
        tail = jnp.broadcast_to(sums_to_row(total[rows]), (ROWS - SPAN, 128))
        out_ref[0, j // 2, 0, j % 2, SPAN:, :] = tail.astype(BF16)


def attend(queries, keys, values, counts):
    whole = pl.BlockSpec((SLOTS, HEAD_DIM), lambda i: (0, 0))
    return pl.pallas_call(
        attend_kernel,
        grid=(16,),
        in_specs=[
            pl.BlockSpec((4 * SPAN, HEAD_DIM), lambda i: (i, 0)),
            whole,
            whole,
            pl.BlockSpec((1, 4, SLOTS), lambda i: (i, 0, 0)),
        ],
        out_specs=pl.BlockSpec(
            (1, 2, 1, 2, ROWS, HEAD_DIM), lambda i: (i % 4, 0, i // 4, 0, 0, 0)
        ),
        out_shape=jax.ShapeDtypeStruct((4, 2, 4, 2, ROWS, HEAD_DIM), BF16),
        name="attend",
    )(queries, keys, values, counts)


def merge(parts):
    sums = [row_to_sums(p[SPAN : SPAN + 1, :].astype(F32)) for p in parts]
    total = functools.reduce(jnp.add, sums)
    mixed = functools.reduce(
        jnp.add, [p[:SPAN, :].astype(F32) * (s / total) for p, s in zip(parts, sums)]
    )
    return mixed, total


def merge_kernel(in_ref, out_ref):
    for j in range(in_ref.shape[1]):
        parts = [in_ref[k, j] for k in range(in_ref.shape[0])]
        sums = [row_to_sums(p[SPAN : SPAN + 1, :].astype(F32)) for p in parts]
        total = functools.reduce(jnp.add, sums)
        inverse = jnp.where(total > 0.0, 1.0 / total, 0.0)
        mixed = functools.reduce(
            jnp.add, [p[:SPAN, :].astype(F32) * (s * inverse) for p, s in zip(parts, sums)]
        )
        out_ref[j, :SPAN, :] = mixed.astype(BF16)
        out_ref[j, SPAN:, :] = jnp.broadcast_to(sums_to_row(total), (ROWS - SPAN, 128)).astype(BF16)


def merge_shards(parts):
    shards, count = parts.shape[:2]
    step = 4
    return pl.pallas_call(
        merge_kernel,
        grid=(count // step,),
        in_specs=[pl.BlockSpec((shards, step, ROWS, HEAD_DIM), lambda i: (0, i, 0, 0))],
        out_specs=pl.BlockSpec((step, ROWS, HEAD_DIM), lambda i: (i, 0, 0)),
        out_shape=jax.ShapeDtypeStruct((count, ROWS, HEAD_DIM), BF16),
        name="merge_shards",
    )(parts)


def mix_kernel(place_ref, parts_ref, w0_ref, w1_ref, w2_ref, w3_ref, out_ref, att_ref):
    @pl.when(pl.program_id(0) == 0)
    def _():
        for s in range(2):
            for c in range(2):
                mixed, _ = merge([parts_ref[s, z, c] for z in range(4)])
                att_ref[2 * s + c] = mixed.astype(BF16)

    place = place_ref[0]
    acc = None
    for k, ref in enumerate((w0_ref, w1_ref, w2_ref, w3_ref)):
        term = dot(att_ref[place ^ k], ref[...], ((1,), (1,)))
        acc = term if acc is None else acc + term
    for d in range(out_ref.shape[0]):
        out_ref[d] = acc[:, d * HEAD_DIM : (d + 1) * HEAD_DIM].astype(BF16)


def mix(place, parts, weights):
    step = 8
    weight = pl.BlockSpec((step * HEAD_DIM, HEAD_DIM), lambda i, *_: (i, 0))
    return pl.pallas_call(
        mix_kernel,
        grid_spec=pltpu.PrefetchScalarGridSpec(
            num_scalar_prefetch=1,
            grid=(32 // step,),
            in_specs=[
                pl.BlockSpec((2, 4, 2, ROWS, HEAD_DIM), lambda i, *_: (0, 0, 0, 0, 0)),
                weight,
                weight,
                weight,
                weight,
            ],
            out_specs=pl.BlockSpec((step, SPAN, HEAD_DIM), lambda i, *_: (i, 0, 0)),
            scratch_shapes=[pltpu.VMEM((4, SPAN, HEAD_DIM), BF16)],
        ),
        out_shape=jax.ShapeDtypeStruct((32, SPAN, HEAD_DIM), BF16),
        name="mix",
    )(place, parts, *weights)


def swap(value, axis):
    return lax.ppermute(value, axis, [(0, 1), (1, 0)])


def multiplicities(nb_ids, nb_index):
    place = nb_ids % SHARD
    upper = (nb_ids // SHARD) * 32 + place // 32
    one_upper = (upper[:, :, None] == jnp.arange(512)).astype(BF16)
    one_lower = ((place % 32)[:, :, None] == jnp.arange(32)).astype(BF16)
    per_block = jnp.einsum("nip,niq->npq", one_upper, one_lower, preferred_element_type=F32)
    pick = jnp.sum((nb_index[:, :, None] == jnp.arange(8)).astype(F32), axis=1)
    counts = jnp.einsum("gn,npq->gpq", pick.astype(BF16), per_block.astype(BF16), preferred_element_type=F32)
    return counts.reshape(4, 16, SLOTS).transpose(1, 0, 2).astype(BF16)


def on_device(tokens, nb_ids, nb_index, table, norm_gains, projections):
    group = ("s", "y", "c")
    core = lax.axis_index("c")
    place = lax.axis_index("s") * 2 + core
    padded = jnp.pad(table, ((0, SLOTS - SHARD), (0, 0)))
    rows = lax.all_gather(padded, group, axis=0)

    halves = jnp.broadcast_to(tokens.reshape(1, 1, 2, 128, 128), (2, 8, 2, 128, 128))
    full_tokens = lax.all_to_all(halves.reshape(32, 128, 128), group, 0, 0)
    wq = projections[1, 0]
    wq_other = swap(wq, "c")
    wide = full_tokens.astype(F32)
    mean = jnp.sum(wide * wide, axis=(0, 2)) * (1.0 / 4096)
    normed = wide * lax.rsqrt(mean + EPS)[None, :, None] * norm_gains[1].reshape(32, 1, 128)
    normed = normed.astype(BF16).transpose(1, 0, 2).reshape(128, 4096)
    own = jnp.dot(normed, wq, preferred_element_type=F32).astype(BF16)
    other = jnp.dot(normed, wq_other, preferred_element_type=F32).astype(BF16)
    pair = jnp.where(core == 0, jnp.stack([own, other]), jnp.stack([other, own]))
    spread = jnp.broadcast_to(pair[None], (16, 2, 128, 128)).reshape(32, 128, 128)
    queries = lax.all_to_all(spread, ("zh", "x", "c"), 0, 0).reshape(4096, HEAD_DIM)
    counts = lax.all_to_all(multiplicities(nb_ids, nb_index), ("zh", "x"), 0, 0)

    wo = projections[1, 1]
    wo_section = swap(wo, "s")
    wo_all = (wo, swap(wo, "c"), wo_section, swap(wo_section, "c"))

    keys, values = project_rows(rows, norm_gains[0], projections[0, 0], projections[0, 1])
    parts = attend(queries, keys, values, counts)
    parts = lax.all_to_all(parts, "x", 0, 0)
    merged = merge_shards(parts.reshape(4, 16, ROWS, HEAD_DIM))
    merged = lax.all_to_all(merged, ("s", "zh", "c"), 0, 0)
    out = mix(place.reshape(1), merged.reshape(2, 4, 2, ROWS, HEAD_DIM), wo_all)
    out = lax.all_to_all(out, group, 0, 0)
    out = jnp.sum(out.reshape(2, 8, 2, SPAN, HEAD_DIM).astype(F32), axis=1)
    return out.astype(BF16).reshape(4 * SPAN, HEAD_DIM)


def solution(mesh):
    fine = Mesh(mesh.devices.reshape(2, 4, 4, 8, 2), ("s", "zh", "x", "y", "c"))
    batch, cols = ("zh", "x"), ("s", "y", "c")
    return jax.shard_map(
        on_device,
        mesh=fine,
        in_specs=(
            P(batch, cols),
            P(batch, None),
            P(batch, None),
            P(batch, cols),
            P(),
            P(None, None, None, cols),
        ),
        out_specs=P(batch, cols),
        check_vma=False,
    )
```

```python
import functools
import math

import jax
import jax.numpy as jnp
from jax import lax
from jax.experimental import pallas as pl
from jax.experimental.pallas import tpu as pltpu
from jax.sharding import Mesh
from jax.sharding import PartitionSpec as P

HEAD_DIM = 128
SPAN = 64
ROWS = 72
SHARD = 1000
HALF = 512
ROWS_IN = HALF + 128
OFFSETS = (0, 7, 1, 6, 2, 5, 3, 4)
EPS = 1e-06
SCALE = math.log2(math.e) / math.sqrt(HEAD_DIM)
F32 = jnp.float32
BF16 = jnp.bfloat16


def dot(a, b, dims):
    return lax.dot_general(a, b, (dims, ((), ())), preferred_element_type=F32)


def diagonal(shape):
    row = lax.broadcasted_iota(jnp.int32, shape, len(shape) - 2)
    lane = lax.broadcasted_iota(jnp.int32, shape, len(shape) - 1)
    return row == lane % SPAN


def sums_to_row(column):
    row = jnp.sum(jnp.where(diagonal((SPAN, 128)), column, 0.0), axis=0, keepdims=True)
    upper = row.astype(BF16).astype(F32)
    lane = lax.broadcasted_iota(jnp.int32, (1, 128), 1)
    return jnp.where(lane < SPAN, upper, row - upper)


def row_to_sums(row):
    return jnp.sum(jnp.where(diagonal((SPAN, 128)), row, 0.0), axis=1, keepdims=True)


def column_to_row(column):
    square = (128, 128)
    same = lax.broadcasted_iota(jnp.int32, square, 0) == lax.broadcasted_iota(jnp.int32, square, 1)
    return jnp.sum(jnp.where(same, column, 0.0), axis=0, keepdims=True)


def row_to_column(row):
    square = (128, 128)
    same = lax.broadcasted_iota(jnp.int32, square, 0) == lax.broadcasted_iota(jnp.int32, square, 1)
    return jnp.sum(jnp.where(same, row, 0.0), axis=1, keepdims=True)


def project_kernel(where_ref, *refs):
    near, far = refs[:7], refs[7:9]
    gain_ref = refs[9]
    weights = refs[10:14]
    keep_ref, keep_q_ref, squares_ref, send_ref, lhs_ref = refs[14:]
    core, here = where_ref[0], where_ref[1]
    square = jnp.zeros((ROWS_IN, 128), F32)
    for ref, offset in zip((*near, None), OFFSETS):
        source = (here + offset) % 8
        for i in range(2):
            if ref is None:
                x = jnp.concatenate([far[0][i], far[1][i]], axis=0)
            else:
                x = ref[i]
            wide = x.astype(F32)
            square = square + wide * wide
            gain = gain_ref[source, i]
            rows = wide[:HALF] * gain[0:1], wide[HALF:] * gain[1:2]
            lanes = slice(i * 128, (i + 1) * 128)
            lhs_ref[source, :HALF, lanes] = rows[0].astype(BF16)
            lhs_ref[source, HALF:, lanes] = rows[1].astype(BF16)
    sums = jnp.sum(square, axis=1, keepdims=True)
    tail = [column_to_row(sums[k * 128 : (k + 1) * 128]) for k in range(5)]
    squares = jnp.concatenate(tail + [jnp.zeros((3, 128), F32)], axis=0)
    squares_ref[...] = squares
    upper = squares.astype(BF16)
    send_ref[0, HALF + 64 :, :] = upper
    send_ref[1, HALF + 64 :, :] = (squares - upper.astype(F32)).astype(BF16)
    send_ref[2, HALF + 64 :, :] = upper
    send_ref[3, HALF + 64 :, :] = upper
    lhs = jnp.concatenate([lhs_ref[y] for y in range(8)], axis=1)
    for m, ref in enumerate(weights):
        head = core ^ (m % 2)
        pair = jnp.concatenate([ref[1], ref[2]], axis=1)
        both = dot(lhs[:HALF], pair, ((1,), (0,)))
        query = dot(lhs[HALF:], ref[0], ((1,), (0,)))
        if m < 2:
            keep_ref[head, 0] = both[:, :128]
            keep_ref[head, 1] = both[:, 128:]
            keep_q_ref[head] = query
        else:
            for i in range(2):
                send_ref[2 * head + i, :HALF, :] = both[:, i * 128 : (i + 1) * 128].astype(BF16)
                send_ref[2 * head + i, HALF : HALF + 64, :] = query[i * 64 : (i + 1) * 64].astype(BF16)


def project(where, blocks, far, gains, weights):
    vmem = pl.BlockSpec(memory_space=pltpu.VMEM)
    return pl.pallas_call(
        project_kernel,
        in_specs=[pl.BlockSpec(memory_space=pltpu.SMEM)] + [vmem] * 14,
        out_specs=[vmem] * 4,
        out_shape=[
            jax.ShapeDtypeStruct((2, 2, HALF, 128), F32),
            jax.ShapeDtypeStruct((2, 128, 128), F32),
            jax.ShapeDtypeStruct((8, 128), F32),
            jax.ShapeDtypeStruct((4, HALF + 72, 128), BF16),
        ],
        scratch_shapes=[pltpu.VMEM((8, ROWS_IN, 256), BF16)],
        name="project",
    )(where, *blocks, *far, gains, *weights)


def finish_kernel(keep_ref, keep_q_ref, squares_ref, other_ref, count_ref, kv_ref, q_ref):
    ours = squares_ref[...]
    theirs = other_ref[0, HALF + 64 :, :].astype(F32) + other_ref[1, HALF + 64 :, :].astype(F32)
    rate = lax.rsqrt((ours + theirs) * (1.0 / 4096) + EPS)
    for head in range(2):
        for k in range(4):
            rows = slice(k * 128, (k + 1) * 128)
            column = row_to_column(rate[k : k + 1])
            for i in range(2):
                total = keep_ref[head, i, rows] + other_ref[2 * head + i, rows, :].astype(F32)
                value = (total * column).astype(BF16)
                for x in range(4):
                    kv_ref[x, head, i, rows] = value
        column = row_to_column(rate[4:5])
        for i in range(2):
            rows = slice(i * 64, (i + 1) * 64)
            total = keep_q_ref[head, rows] + other_ref[2 * head + i, HALF : HALF + 64, :].astype(F32)
            value = (total * column[rows]).astype(BF16)
            for z in range(4):
                q_ref[z, head, rows] = value
        for z in range(4):
            q_ref[z, head, 128:] = count_ref[z]


def finish(keep, keep_q, squares, other, counts):
    vmem = pl.BlockSpec(memory_space=pltpu.VMEM)
    return pl.pallas_call(
        finish_kernel,
        in_specs=[vmem] * 5,
        out_specs=[vmem] * 2,
        out_shape=[
            jax.ShapeDtypeStruct((4, 2, 2, HALF, 128), BF16),
            jax.ShapeDtypeStruct((4, 2, 192, 128), BF16),
        ],
        name="finish",
    )(keep, keep_q, squares, other, counts)


def attend_kernel(q_ref, kv_ref, count_ref, out_ref, expo_ref):
    queries = jnp.concatenate([q_ref[0, 0], q_ref[0, 1]], axis=0)
    total = jnp.zeros((4 * SPAN, 128), F32)
    for k in range(8):
        x, c = divmod(k, 2)
        lanes = slice(k * HALF, (k + 1) * HALF)
        bias = jnp.log2(count_ref[0, :, lanes].astype(F32))
        spread = jnp.broadcast_to(bias[:, None, :], (4, SPAN, HALF)).reshape(4 * SPAN, HALF)
        scores = dot(queries, kv_ref[x, c, 0], ((1,), (1,)))
        expo = jnp.exp2(scores * SCALE + spread)
        expo_ref[:, lanes] = expo
        for i in range(HALF // 128):
            total = total + expo[:, i * 128 : (i + 1) * 128]
    total = jnp.sum(total, axis=1, keepdims=True)
    inverse = jnp.where(total > 0.0, 1.0 / total, 0.0)
    weights = (expo_ref[...] * inverse).astype(BF16)
    values = jnp.concatenate([kv_ref[k // 2, k % 2, 1] for k in range(8)], axis=0)
    part = dot(weights, values, ((1,), (0,))).astype(BF16)
    for j in range(4):
        rows = slice(j * SPAN, (j + 1) * SPAN)
        out_ref[j // 2, 0, j % 2, :SPAN, :] = part[rows]
        tail = jnp.broadcast_to(sums_to_row(total[rows]), (ROWS - SPAN, 128))
        out_ref[j // 2, 0, j % 2, SPAN:, :] = tail.astype(BF16)


def attend(queries, key_values, counts):
    return pl.pallas_call(
        attend_kernel,
        grid=(4,),
        in_specs=[
            pl.BlockSpec((1, 2, 128, HEAD_DIM), lambda i: (i, 0, 0, 0)),
            pl.BlockSpec((4, 2, 2, HALF, HEAD_DIM), lambda i: (0, 0, 0, 0, 0)),
            pl.BlockSpec((1, 4, 8 * HALF), lambda i: (i, 0, 0)),
        ],
        out_specs=pl.BlockSpec((2, 1, 2, ROWS, HEAD_DIM), lambda i: (0, i, 0, 0, 0)),
        out_shape=jax.ShapeDtypeStruct((2, 4, 2, ROWS, HEAD_DIM), BF16),
        scratch_shapes=[pltpu.VMEM((4 * SPAN, 8 * HALF), F32)],
        name="attend",
    )(queries, key_values, counts)


def merge(parts):
    sums = [row_to_sums(p[SPAN : SPAN + 1, :].astype(F32)) for p in parts]
    total = functools.reduce(jnp.add, sums)
    mixed = functools.reduce(
        jnp.add, [p[:SPAN, :].astype(F32) * (s / total) for p, s in zip(parts, sums)]
    )
    return mixed, total


def mix_kernel(place_ref, parts_ref, w0_ref, w1_ref, w2_ref, w3_ref, out_ref, att_ref):
    @pl.when(pl.program_id(0) == 0)
    def _():
        for s in range(2):
            for c in range(2):
                mixed, _ = merge([parts_ref[s, z, c] for z in range(4)])
                att_ref[2 * s + c] = mixed.astype(BF16)

    place = place_ref[0]
    acc = None
    for k, ref in enumerate((w0_ref, w1_ref, w2_ref, w3_ref)):
        term = dot(att_ref[place ^ k], ref[...], ((1,), (1,)))
        acc = term if acc is None else acc + term
    for d in range(out_ref.shape[0]):
        out_ref[d] = acc[:, d * HEAD_DIM : (d + 1) * HEAD_DIM].astype(BF16)


def mix(place, parts, weights):
    step = 8
    weight = pl.BlockSpec((step * HEAD_DIM, HEAD_DIM), lambda i, *_: (i, 0))
    return pl.pallas_call(
        mix_kernel,
        grid_spec=pltpu.PrefetchScalarGridSpec(
            num_scalar_prefetch=1,
            grid=(32 // step,),
            in_specs=[
                pl.BlockSpec((2, 4, 2, ROWS, HEAD_DIM), lambda i, *_: (0, 0, 0, 0, 0)),
                weight,
                weight,
                weight,
                weight,
            ],
            out_specs=pl.BlockSpec((step, SPAN, HEAD_DIM), lambda i, *_: (i, 0, 0)),
            scratch_shapes=[pltpu.VMEM((4, SPAN, HEAD_DIM), BF16)],
        ),
        out_shape=jax.ShapeDtypeStruct((32, SPAN, HEAD_DIM), BF16),
        name="mix",
    )(place, parts, *weights)


def swap(value, axis):
    return lax.ppermute(value, axis, [(0, 1), (1, 0)])


def multiplicities(nb_ids, nb_index):
    place = nb_ids % SHARD
    place = jnp.where(place < HALF, place, place + (2 * HALF - SHARD))
    upper = (nb_ids // SHARD) * 32 + place // 32
    one_upper = (upper[:, :, None] == jnp.arange(512)).astype(BF16)
    one_lower = ((place % 32)[:, :, None] == jnp.arange(32)).astype(BF16)
    per_block = jnp.einsum("nip,niq->npq", one_upper, one_lower, preferred_element_type=F32)
    pick = jnp.sum((nb_index[:, :, None] == jnp.arange(8)).astype(F32), axis=1)
    counts = jnp.einsum(
        "gn,npq->gpq", pick.astype(BF16), per_block.astype(BF16), preferred_element_type=F32
    )
    return counts.astype(BF16)


def half_of(table, tokens, core):
    rows = lax.dynamic_slice_in_dim(table, core * (SHARD - HALF), HALF)
    return jnp.concatenate([rows, lax.dynamic_slice_in_dim(tokens, core * 128, 128)], axis=0)


def on_device(tokens, nb_ids, nb_index, table, norm_gains, projections):
    core, section, here = lax.axis_index("c"), lax.axis_index("s"), lax.axis_index("y")

    own = half_of(table, tokens, core)
    got = swap(half_of(table, tokens, 1 - core), "c")
    chunk = jnp.where(core == 0, jnp.stack([own, got]), jnp.stack([got, own]))
    ahead = [(i, (i + 1) % 8) for i in range(8)]
    back = [(i, (i - 1) % 8) for i in range(8)]
    blocks, up, down = [chunk], chunk, chunk
    for _ in range(3):
        up, down = lax.ppermute(up, "y", ahead), lax.ppermute(down, "y", back)
        blocks += [up, down]
    cut = ROWS_IN // 2
    far = (lax.ppermute(up[:, :cut], "y", ahead), lax.ppermute(down[:, cut:], "y", back))

    stacked = jnp.stack([projections[1, 0], projections[0, 0], projections[0, 1]])
    mine = lax.dynamic_slice_in_dim(stacked, section * 2048, 2048, axis=1)
    across = swap(lax.dynamic_slice_in_dim(stacked, (1 - section) * 2048, 2048, axis=1), "s")
    weights = (mine, swap(mine, "c"), across, swap(across, "c"))
    wo = projections[1, 1]
    wo_section = swap(wo, "s")
    wo_all = (wo, swap(wo, "c"), wo_section, swap(wo_section, "c"))

    gains = lax.dynamic_slice_in_dim(norm_gains, section * 2048, 2048, axis=1)
    gains = gains.reshape(2, 8, 2, 128).transpose(1, 2, 0, 3)
    counts = multiplicities(nb_ids, nb_index).reshape(2, 2, 4, 4 * 1024)
    counts = lax.dynamic_index_in_dim(counts, core, 0, keepdims=False)
    counts = counts.transpose(1, 0, 2).reshape(4, 64, 128)

    where = jnp.stack([core, here]).astype(jnp.int32)
    keep, keep_q, squares, send = project(where, blocks, far, gains, weights)
    key_values, queries = finish(keep, keep_q, squares, swap(send, "s"), counts)
    queries = lax.all_to_all(queries.reshape(8, 192, 128), ("zh", "c"), 0, 0)
    queries = queries.reshape(4, 2, 192, 128)
    counts = queries[:, :, 128:].reshape(4, 4, 8 * HALF)
    key_values = lax.all_to_all(key_values.reshape(8, 2, HALF, 128), ("x", "c"), 0, 0)
    parts = attend(queries, key_values.reshape(4, 2, 2, HALF, 128), counts)
    parts = lax.all_to_all(parts.reshape(16, ROWS, HEAD_DIM), ("s", "zh", "c"), 0, 0)
    place = (section * 2 + core).astype(jnp.int32).reshape(1)
    out = mix(place, parts.reshape(2, 4, 2, ROWS, HEAD_DIM), wo_all)
    out = lax.all_to_all(out, ("s", "y", "c"), 0, 0)
    out = jnp.sum(out.reshape(2, 8, 2, SPAN, HEAD_DIM).astype(F32), axis=1)
    return out.astype(BF16).reshape(4 * SPAN, HEAD_DIM)


def solution(mesh):
    fine = Mesh(mesh.devices.reshape(2, 4, 4, 8, 2), ("s", "zh", "x", "y", "c"))
    batch, cols = ("zh", "x"), ("s", "y", "c")
    return jax.shard_map(
        on_device,
        mesh=fine,
        in_specs=(
            P(batch, cols),
            P(batch, None),
            P(batch, None),
            P(batch, cols),
            P(),
            P(None, None, None, cols),
        ),
        out_specs=P(batch, cols),
        check_vma=False,
    )
```

```python
import functools
import math

import jax
import jax.numpy as jnp
from jax import lax
from jax.experimental import pallas as pl
from jax.experimental.pallas import tpu as pltpu
from jax.sharding import Mesh
from jax.sharding import PartitionSpec as P

HEAD_DIM = 128
SPAN = 64
ROWS = 72
SHARD = 1000
HALF = 512
ROWS_IN = HALF + 128
EPS = 1e-06
SCALE = math.log2(math.e) / math.sqrt(HEAD_DIM)
F32 = jnp.float32
BF16 = jnp.bfloat16


def dot(a, b, dims):
    return lax.dot_general(a, b, (dims, ((), ())), preferred_element_type=F32)


def diagonal(shape):
    row = lax.broadcasted_iota(jnp.int32, shape, len(shape) - 2)
    lane = lax.broadcasted_iota(jnp.int32, shape, len(shape) - 1)
    return row == lane % SPAN


def sums_to_row(column):
    row = jnp.sum(jnp.where(diagonal((SPAN, 128)), column, 0.0), axis=0, keepdims=True)
    upper = row.astype(BF16).astype(F32)
    lane = lax.broadcasted_iota(jnp.int32, (1, 128), 1)
    return jnp.where(lane < SPAN, upper, row - upper)


def row_to_sums(row):
    return jnp.sum(jnp.where(diagonal((SPAN, 128)), row, 0.0), axis=1, keepdims=True)


def column_to_row(column):
    square = (128, 128)
    same = lax.broadcasted_iota(jnp.int32, square, 0) == lax.broadcasted_iota(jnp.int32, square, 1)
    return jnp.sum(jnp.where(same, column, 0.0), axis=0, keepdims=True)


def row_to_column(row):
    square = (128, 128)
    same = lax.broadcasted_iota(jnp.int32, square, 0) == lax.broadcasted_iota(jnp.int32, square, 1)
    return jnp.sum(jnp.where(same, row, 0.0), axis=1, keepdims=True)


def far_kernel(source_ref, b0_ref, b1_ref, b2_ref, b3_ref, b4_ref, gain_ref, w_ref, lhs_ref, squares_ref, send_ref):
    square = jnp.zeros((ROWS_IN, 128), F32)
    pieces = [b0_ref, b1_ref]
    for ref in (b2_ref, b3_ref, b4_ref):
        pieces += [ref.at[0], ref.at[1]]
    for k, ref in enumerate(pieces):
        source = source_ref[k]
        for i in range(2):
            wide = ref[i].astype(F32)
            square = square + wide * wide
            gain = gain_ref[source, i]
            lanes = slice(i * 128, (i + 1) * 128)
            lhs_ref[source, :HALF, lanes] = (wide[:HALF] * gain[0:1]).astype(BF16)
            lhs_ref[source, HALF:, lanes] = (wide[HALF:] * gain[1:2]).astype(BF16)
    sums = jnp.sum(square, axis=1, keepdims=True)
    tail = [column_to_row(sums[k * 128 : (k + 1) * 128]) for k in range(5)]
    squares = jnp.concatenate(tail + [jnp.zeros((3, 128), F32)], axis=0)
    squares_ref[...] = squares
    upper = squares.astype(BF16)
    send_ref[0, HALF + 64 :, :] = upper
    send_ref[1, HALF + 64 :, :] = (squares - upper.astype(F32)).astype(BF16)
    product(lhs_ref, w_ref, send_ref)


def product(lhs_ref, w_ref, send_ref):
    lhs = jnp.concatenate([lhs_ref[y] for y in range(8)], axis=1)
    pair = jnp.concatenate([w_ref[0], w_ref[1]], axis=1)
    both = dot(lhs[:HALF], pair, ((1,), (0,)))
    query = dot(lhs[HALF:], w_ref[2], ((1,), (0,)))
    for i in range(2):
        send_ref[i, :HALF, :] = both[:, i * 128 : (i + 1) * 128].astype(BF16)
        send_ref[i, HALF : HALF + 64, :] = query[i * 64 : (i + 1) * 64].astype(BF16)


def project_far(source, blocks, gains, weight):
    vmem = pl.BlockSpec(memory_space=pltpu.VMEM)
    return pl.pallas_call(
        far_kernel,
        in_specs=[pl.BlockSpec(memory_space=pltpu.SMEM)] + [vmem] * 7,
        out_specs=[vmem] * 3,
        out_shape=[
            jax.ShapeDtypeStruct((8, ROWS_IN, 256), BF16),
            jax.ShapeDtypeStruct((8, 128), F32),
            jax.ShapeDtypeStruct((2, HALF + 72, 128), BF16),
        ],
        name="project_far",
    )(source, *blocks, gains, weight)


def project_diagonal(lhs, weight):
    vmem = pl.BlockSpec(memory_space=pltpu.VMEM)
    return pl.pallas_call(
        product,
        in_specs=[vmem] * 2,
        out_specs=vmem,
        out_shape=jax.ShapeDtypeStruct((2, HALF + 64, 128), BF16),
        name="project_diagonal",
    )(lhs, weight)


def near_kernel(lhs_ref, w0_ref, w1_ref, keep_ref, keep_q_ref):
    lhs = jnp.concatenate([lhs_ref[y] for y in range(8)], axis=1)
    for m, ref in enumerate((w0_ref, w1_ref)):
        pair = jnp.concatenate([ref[0], ref[1]], axis=1)
        both = dot(lhs[:HALF], pair, ((1,), (0,)))
        keep_ref[m, 0] = both[:, :128]
        keep_ref[m, 1] = both[:, 128:]
        keep_q_ref[m] = dot(lhs[HALF:], ref[2], ((1,), (0,)))


def project_near(lhs, weights):
    vmem = pl.BlockSpec(memory_space=pltpu.VMEM)
    return pl.pallas_call(
        near_kernel,
        in_specs=[vmem] * 3,
        out_specs=[vmem] * 2,
        out_shape=[
            jax.ShapeDtypeStruct((2, 2, HALF, 128), F32),
            jax.ShapeDtypeStruct((2, 128, 128), F32),
        ],
        name="project_near",
    )(lhs, *weights)


def finish_kernel(source_ref, keep_ref, keep_q_ref, squares_ref, first_ref, second_ref, count_ref, own_ref, give_ref, q_ref):
    core = source_ref[8]
    ours = squares_ref[...]
    theirs = first_ref[0, HALF + 64 :, :].astype(F32) + first_ref[1, HALF + 64 :, :].astype(F32)
    rate = lax.rsqrt((ours + theirs) * (1.0 / 4096) + EPS)
    for m, (ref, other_ref) in enumerate(((own_ref, first_ref), (give_ref, second_ref))):
        head = core ^ m
        for k in range(4):
            rows = slice(k * 128, (k + 1) * 128)
            column = row_to_column(rate[k : k + 1])
            for i in range(2):
                total = keep_ref[m, i, rows] + other_ref[i, rows, :].astype(F32)
                ref[i, rows] = (total * column).astype(BF16)
        column = row_to_column(rate[4:5])
        for i in range(2):
            rows = slice(i * 64, (i + 1) * 64)
            total = keep_q_ref[m, rows] + other_ref[i, HALF : HALF + 64, :].astype(F32)
            value = (total * column[rows]).astype(BF16)
            for z in range(4):
                q_ref[z, head, rows] = value
        for z in range(4):
            q_ref[z, m, 128:] = count_ref[z]


def finish(source, keep, keep_q, squares, first, second, counts):
    vmem = pl.BlockSpec(memory_space=pltpu.VMEM)
    half = jax.ShapeDtypeStruct((2, HALF, 128), BF16)
    return pl.pallas_call(
        finish_kernel,
        in_specs=[pl.BlockSpec(memory_space=pltpu.SMEM)] + [vmem] * 6,
        out_specs=[vmem] * 3,
        out_shape=[half, half, jax.ShapeDtypeStruct((4, 2, 192, 128), BF16)],
        name="finish",
    )(source, keep, keep_q, squares, first, second, counts)


def attend_kernel(order_ref, q_ref, near_ref, next_ref, far_ref, count_ref, out_ref, expo_ref):
    queries = jnp.concatenate([q_ref[0, 0], q_ref[0, 1]], axis=0)
    blocks = [near_ref.at[0], near_ref.at[1], next_ref.at[0], next_ref.at[1]]
    blocks += [far_ref.at[k, i] for k in range(2) for i in range(2)]
    total = jnp.zeros((4 * SPAN, 128), F32)
    for k, block in enumerate(blocks):
        lanes = slice(k * HALF, (k + 1) * HALF)
        bias = jnp.log2(count_ref[0, order_ref[k]].astype(F32))
        spread = jnp.broadcast_to(bias[:, None, :], (4, SPAN, HALF)).reshape(4 * SPAN, HALF)
        scores = dot(queries, block[0], ((1,), (1,)))
        expo = jnp.exp2(scores * SCALE + spread)
        expo_ref[:, lanes] = expo
        for i in range(HALF // 128):
            total = total + expo[:, i * 128 : (i + 1) * 128]
    total = jnp.sum(total, axis=1, keepdims=True)
    inverse = jnp.where(total > 0.0, 1.0 / total, 0.0)
    weights = (expo_ref[...] * inverse).astype(BF16)
    values = jnp.concatenate([block[1] for block in blocks], axis=0)
    part = dot(weights, values, ((1,), (0,))).astype(BF16)
    for j in range(4):
        rows = slice(j * SPAN, (j + 1) * SPAN)
        out_ref[j // 2, 0, j % 2, :SPAN, :] = part[rows]
        tail = jnp.broadcast_to(sums_to_row(total[rows]), (ROWS - SPAN, 128))
        out_ref[j // 2, 0, j % 2, SPAN:, :] = tail.astype(BF16)


def attend(order, queries, near, after, far, counts):
    block = pl.BlockSpec((2, 2, HALF, HEAD_DIM), lambda i, *_: (0, 0, 0, 0))
    return pl.pallas_call(
        attend_kernel,
        grid_spec=pltpu.PrefetchScalarGridSpec(
            num_scalar_prefetch=1,
            grid=(4,),
            in_specs=[
                pl.BlockSpec((1, 2, 128, HEAD_DIM), lambda i, *_: (i, 0, 0, 0)),
                block,
                block,
                pl.BlockSpec((2, 2, 2, HALF, HEAD_DIM), lambda i, *_: (0, 0, 0, 0, 0)),
                pl.BlockSpec((1, 8, 4, HALF), lambda i, *_: (i, 0, 0, 0)),
            ],
            out_specs=pl.BlockSpec((2, 1, 2, ROWS, HEAD_DIM), lambda i, *_: (0, i, 0, 0, 0)),
            scratch_shapes=[pltpu.VMEM((4 * SPAN, 8 * HALF), F32)],
        ),
        out_shape=jax.ShapeDtypeStruct((2, 4, 2, ROWS, HEAD_DIM), BF16),
        name="attend",
    )(order, queries, near, after, far, counts)


def merge(parts):
    sums = [row_to_sums(p[SPAN : SPAN + 1, :].astype(F32)) for p in parts]
    total = functools.reduce(jnp.add, sums)
    mixed = functools.reduce(
        jnp.add, [p[:SPAN, :].astype(F32) * (s / total) for p, s in zip(parts, sums)]
    )
    return mixed, total


def mix_kernel(place_ref, parts_ref, w0_ref, w1_ref, w2_ref, w3_ref, out_ref, att_ref):
    @pl.when(pl.program_id(0) == 0)
    def _():
        for s in range(2):
            for c in range(2):
                mixed, _ = merge([parts_ref[s, z, c] for z in range(4)])
                att_ref[2 * s + c] = mixed.astype(BF16)

    place = place_ref[0]
    acc = None
    for k, ref in enumerate((w0_ref, w1_ref, w2_ref, w3_ref)):
        term = dot(att_ref[place ^ k], ref[...], ((1,), (1,)))
        acc = term if acc is None else acc + term
    for d in range(out_ref.shape[0]):
        out_ref[d] = acc[:, d * HEAD_DIM : (d + 1) * HEAD_DIM].astype(BF16)


def mix(place, parts, weights):
    step = 8
    weight = pl.BlockSpec((step * HEAD_DIM, HEAD_DIM), lambda i, *_: (i, 0))
    return pl.pallas_call(
        mix_kernel,
        grid_spec=pltpu.PrefetchScalarGridSpec(
            num_scalar_prefetch=1,
            grid=(32 // step,),
            in_specs=[
                pl.BlockSpec((2, 4, 2, ROWS, HEAD_DIM), lambda i, *_: (0, 0, 0, 0, 0)),
                weight,
                weight,
                weight,
                weight,
            ],
            out_specs=pl.BlockSpec((step, SPAN, HEAD_DIM), lambda i, *_: (i, 0, 0)),
            scratch_shapes=[pltpu.VMEM((4, SPAN, HEAD_DIM), BF16)],
        ),
        out_shape=jax.ShapeDtypeStruct((32, SPAN, HEAD_DIM), BF16),
        name="mix",
    )(place, parts, *weights)


def swap(value, axis):
    return lax.ppermute(value, axis, [(0, 1), (1, 0)])


def multiplicities(nb_ids, nb_index):
    place = nb_ids % SHARD
    place = jnp.where(place < HALF, place, place + (2 * HALF - SHARD))
    upper = (nb_ids // SHARD) * 32 + place // 32
    one_upper = (upper[:, :, None] == jnp.arange(512)).astype(BF16)
    one_lower = ((place % 32)[:, :, None] == jnp.arange(32)).astype(BF16)
    per_block = jnp.einsum("nip,niq->npq", one_upper, one_lower, preferred_element_type=F32)
    pick = jnp.sum((nb_index[:, :, None] == jnp.arange(8)).astype(F32), axis=1)
    counts = jnp.einsum(
        "gn,npq->gpq", pick.astype(BF16), per_block.astype(BF16), preferred_element_type=F32
    )
    return counts.astype(BF16)


def half_of(table, tokens, core):
    rows = lax.dynamic_slice_in_dim(table, core * (SHARD - HALF), HALF)
    return jnp.concatenate([rows, lax.dynamic_slice_in_dim(tokens, core * 128, 128)], axis=0)


def pairs(size, turn):
    out = []
    for place in range(size):
        for core in range(2):
            spot = (place - core) % size
            other = spot ^ 1 if turn == 0 else spot + (1 if spot % 2 else -1)
            out.append((2 * place + core, 2 * ((other + core) % size) + core))
    return out


def exchange(value, axis, size, turn):
    return lax.ppermute(value, (axis, "c"), pairs(size, turn))


def after(value, *others):
    return lax.optimization_barrier((value, *others))[0]


def on_device(tokens, nb_ids, nb_index, table, norm_gains, projections):
    core, section, here = lax.axis_index("c"), lax.axis_index("s"), lax.axis_index("y")
    column = lax.axis_index("x")

    own = half_of(table, tokens, core)
    got = swap(half_of(table, tokens, 1 - core), "c")

    def feature_rows(of):
        cut = lax.dynamic_slice(projections, (0, 0, of * 2048, 0), (2, 2, 2048, 128))
        return cut.reshape(4, 2048, 128)[:3]

    away = feature_rows(1 - section)
    across = swap(away, "s")

    got = after(got, away)
    chunk = jnp.where(core == 0, jnp.stack([own, got]), jnp.stack([got, own]))
    first = exchange(chunk, "y", 8, 0)
    second = exchange(jnp.stack([chunk, first]), "y", 8, 1)
    mine = after(feature_rows(section), first)
    beside = swap(mine, "c")
    third = exchange(second, "y", 8, 0)
    fourth = exchange(third, "y", 8, 1)
    diagonal = swap(after(across, fourth), "c")

    gains = lax.dynamic_slice_in_dim(norm_gains, section * 2048, 2048, axis=1)
    gains = gains.reshape(2, 8, 2, 128).transpose(1, 2, 0, 3)
    counts = multiplicities(nb_ids, nb_index).reshape(2, 2, 4, 4 * 1024)
    counts = lax.dynamic_index_in_dim(counts, core, 0, keepdims=False)
    counts = counts.transpose(1, 0, 2).reshape(4, 64, 128)

    sign = 1 - 2 * ((here + core) % 2)
    offsets = jnp.array([0, 1, -1, -2, 2, 3, -3, -4], jnp.int32)
    source = jnp.concatenate([(here + sign * offsets) % 8, core.reshape(1)]).astype(jnp.int32)
    sign = 1 - 2 * ((column + core) % 2)
    origin = (column + sign * offsets[:4]) % 4
    order = (2 * origin[:, None] + jnp.stack([core, 1 - core])[None]).reshape(8).astype(jnp.int32)

    lhs, squares, send = project_far(
        source, (chunk, first, second, third, fourth), gains, across
    )
    mine_sum = swap(send, "s")
    beside_sum = swap(project_diagonal(lhs, diagonal), "s")
    keep, keep_q = project_near(lhs, (mine, beside))
    near, give, queries = finish(source, keep, keep_q, squares, mine_sum, beside_sum, counts)
    near = jnp.stack([near, swap(give, "c")])
    following = exchange(near, "x", 4, 0)
    beyond = exchange(jnp.stack([near, following]), "x", 4, 1)
    queries = lax.all_to_all(queries.reshape(8, 192, 128), ("zh", "c"), 0, 0)
    queries = queries.reshape(4, 2, 192, 128)
    counts = queries[:, :, 128:].reshape(4, 2, 2, 8, HALF).transpose(0, 3, 1, 2, 4)
    counts = counts.reshape(4, 8, 4, HALF)

    wo = after(projections[1, 1], near)
    wo_section = swap(wo, "s")
    wo_all = (wo, swap(wo, "c"), wo_section, None)

    parts = attend(order, queries, near, following, beyond, counts)
    wo_all = (*wo_all[:3], swap(after(wo_section, parts), "c"))
    parts = lax.all_to_all(parts.reshape(16, ROWS, HEAD_DIM), ("s", "zh", "c"), 0, 0)
    place = (section * 2 + core).astype(jnp.int32).reshape(1)
    out = mix(place, parts.reshape(2, 4, 2, ROWS, HEAD_DIM), wo_all)
    out = lax.all_to_all(out, ("s", "y", "c"), 0, 0)
    out = jnp.sum(out.reshape(2, 8, 2, SPAN, HEAD_DIM).astype(F32), axis=1)
    return out.astype(BF16).reshape(4 * SPAN, HEAD_DIM)


def solution(mesh):
    fine = Mesh(mesh.devices.reshape(2, 4, 4, 8, 2), ("s", "zh", "x", "y", "c"))
    batch, cols = ("zh", "x"), ("s", "y", "c")
    return jax.shard_map(
        on_device,
        mesh=fine,
        in_specs=(
            P(batch, cols),
            P(batch, None),
            P(batch, None),
            P(batch, cols),
            P(),
            P(None, None, None, cols),
        ),
        out_specs=P(batch, cols),
        check_vma=False,
    )
```

```python
import functools
import math

import jax
import jax.numpy as jnp
from jax import lax
from jax.experimental import pallas as pl
from jax.experimental.pallas import tpu as pltpu
from jax.sharding import Mesh
from jax.sharding import PartitionSpec as P

HEAD_DIM = 128
SPAN = 64
ROWS = 72
SHARD = 1000
HALF = 512
ROWS_IN = HALF + 128
EPS = 1e-06
SCALE = math.log2(math.e) / math.sqrt(HEAD_DIM)
F32 = jnp.float32
BF16 = jnp.bfloat16


def dot(a, b, dims):
    return lax.dot_general(a, b, (dims, ((), ())), preferred_element_type=F32)


def diagonal(shape):
    row = lax.broadcasted_iota(jnp.int32, shape, len(shape) - 2)
    lane = lax.broadcasted_iota(jnp.int32, shape, len(shape) - 1)
    return row == lane % SPAN


def sums_to_row(column):
    row = jnp.sum(jnp.where(diagonal((SPAN, 128)), column, 0.0), axis=0, keepdims=True)
    upper = row.astype(BF16).astype(F32)
    lane = lax.broadcasted_iota(jnp.int32, (1, 128), 1)
    return jnp.where(lane < SPAN, upper, row - upper)


def row_to_sums(row):
    return jnp.sum(jnp.where(diagonal((SPAN, 128)), row, 0.0), axis=1, keepdims=True)


def column_to_row(column):
    square = (128, 128)
    same = lax.broadcasted_iota(jnp.int32, square, 0) == lax.broadcasted_iota(jnp.int32, square, 1)
    return jnp.sum(jnp.where(same, column, 0.0), axis=0, keepdims=True)


def row_to_column(row):
    square = (128, 128)
    same = lax.broadcasted_iota(jnp.int32, square, 0) == lax.broadcasted_iota(jnp.int32, square, 1)
    return jnp.sum(jnp.where(same, row, 0.0), axis=1, keepdims=True)


def far_kernel(source_ref, b0_ref, b1_ref, b2_ref, b3_ref, b4_ref, gain_ref, w0_ref, w1_ref, lhs_ref, squares_ref, send_ref):
    square = jnp.zeros((ROWS_IN, 128), F32)
    pieces = [b0_ref, b1_ref]
    for ref in (b2_ref, b3_ref, b4_ref):
        pieces += [ref.at[0], ref.at[1]]
    for k, ref in enumerate(pieces):
        source = source_ref[k]
        for i in range(2):
            wide = ref[i].astype(F32)
            square = square + wide * wide
            gain = gain_ref[source, i]
            lanes = slice(i * 128, (i + 1) * 128)
            lhs_ref[source, :HALF, lanes] = (wide[:HALF] * gain[0:1]).astype(BF16)
            lhs_ref[source, HALF:, lanes] = (wide[HALF:] * gain[1:2]).astype(BF16)
    sums = jnp.sum(square, axis=1, keepdims=True)
    tail = [column_to_row(sums[k * 128 : (k + 1) * 128]) for k in range(5)]
    squares = jnp.concatenate(tail + [jnp.zeros((3, 128), F32)], axis=0)
    squares_ref[...] = squares
    upper = squares.astype(BF16)
    lower = (squares - upper.astype(F32)).astype(BF16)
    for i in range(4):
        send_ref[i, HALF + 64 :, :] = lower if i == 1 else upper
    lhs = jnp.concatenate([lhs_ref[y] for y in range(8)], axis=1)
    for m, ref in enumerate((w0_ref, w1_ref)):
        pair = jnp.concatenate([ref[0], ref[1]], axis=1)
        both = dot(lhs[:HALF], pair, ((1,), (0,)))
        query = dot(lhs[HALF:], ref[2], ((1,), (0,)))
        for i in range(2):
            send_ref[2 * m + i, :HALF, :] = both[:, i * 128 : (i + 1) * 128].astype(BF16)
            send_ref[2 * m + i, HALF : HALF + 64, :] = query[i * 64 : (i + 1) * 64].astype(BF16)


def project_far(source, blocks, gains, weights):
    vmem = pl.BlockSpec(memory_space=pltpu.VMEM)
    return pl.pallas_call(
        far_kernel,
        in_specs=[pl.BlockSpec(memory_space=pltpu.SMEM)] + [vmem] * 8,
        out_specs=[vmem] * 3,
        out_shape=[
            jax.ShapeDtypeStruct((8, ROWS_IN, 256), BF16),
            jax.ShapeDtypeStruct((8, 128), F32),
            jax.ShapeDtypeStruct((4, HALF + 72, 128), BF16),
        ],
        name="project_far",
    )(source, *blocks, gains, *weights)


def near_kernel(lhs_ref, w0_ref, w1_ref, keep_ref, keep_q_ref):
    lhs = jnp.concatenate([lhs_ref[y] for y in range(8)], axis=1)
    for m, ref in enumerate((w0_ref, w1_ref)):
        pair = jnp.concatenate([ref[0], ref[1]], axis=1)
        both = dot(lhs[:HALF], pair, ((1,), (0,)))
        keep_ref[m, 0] = both[:, :128]
        keep_ref[m, 1] = both[:, 128:]
        keep_q_ref[m] = dot(lhs[HALF:], ref[2], ((1,), (0,)))


def project_near(lhs, weights):
    vmem = pl.BlockSpec(memory_space=pltpu.VMEM)
    return pl.pallas_call(
        near_kernel,
        in_specs=[vmem] * 3,
        out_specs=[vmem] * 2,
        out_shape=[
            jax.ShapeDtypeStruct((2, 2, HALF, 128), F32),
            jax.ShapeDtypeStruct((2, 128, 128), F32),
        ],
        name="project_near",
    )(lhs, *weights)


def finish_kernel(source_ref, keep_ref, keep_q_ref, squares_ref, other_ref, count_ref, own_ref, give_ref, q_ref):
    core = source_ref[8]
    ours = squares_ref[...]
    theirs = other_ref[0, HALF + 64 :, :].astype(F32) + other_ref[1, HALF + 64 :, :].astype(F32)
    rate = lax.rsqrt((ours + theirs) * (1.0 / 4096) + EPS)
    for m, ref in enumerate((own_ref, give_ref)):
        head = core ^ m
        for k in range(4):
            rows = slice(k * 128, (k + 1) * 128)
            column = row_to_column(rate[k : k + 1])
            for i in range(2):
                total = keep_ref[m, i, rows] + other_ref[2 * m + i, rows, :].astype(F32)
                ref[i, rows] = (total * column).astype(BF16)
        column = row_to_column(rate[4:5])
        for i in range(2):
            rows = slice(i * 64, (i + 1) * 64)
            total = keep_q_ref[m, rows] + other_ref[2 * m + i, HALF : HALF + 64, :].astype(F32)
            value = (total * column[rows]).astype(BF16)
            for z in range(4):
                q_ref[z, head, rows] = value
        for z in range(4):
            q_ref[z, m, 128:] = count_ref[z]


def finish(source, keep, keep_q, squares, other, counts):
    vmem = pl.BlockSpec(memory_space=pltpu.VMEM)
    half = jax.ShapeDtypeStruct((2, HALF, 128), BF16)
    return pl.pallas_call(
        finish_kernel,
        in_specs=[pl.BlockSpec(memory_space=pltpu.SMEM)] + [vmem] * 5,
        out_specs=[vmem] * 3,
        out_shape=[half, half, jax.ShapeDtypeStruct((4, 2, 192, 128), BF16)],
        name="finish",
    )(source, keep, keep_q, squares, other, counts)


def partial(order_ref, first, queries, blocks, count_ref, expo_ref):
    total = jnp.zeros((4 * SPAN, 128), F32)
    for k, block in enumerate(blocks):
        lanes = slice(k * HALF, (k + 1) * HALF)
        bias = jnp.log2(count_ref[0, order_ref[first + k]].astype(F32))
        spread = jnp.broadcast_to(bias[:, None, :], (4, SPAN, HALF)).reshape(4 * SPAN, HALF)
        scores = dot(queries, block[0], ((1,), (1,)))
        expo = jnp.exp2(scores * SCALE + spread)
        expo_ref[:, lanes] = expo
        for i in range(HALF // 128):
            total = total + expo[:, i * 128 : (i + 1) * 128]
    total = jnp.sum(total, axis=1, keepdims=True)
    inverse = jnp.where(total > 0.0, 1.0 / total, 0.0)
    weights = (expo_ref[...] * inverse).astype(BF16)
    values = jnp.concatenate([block[1] for block in blocks], axis=0)
    return dot(weights, values, ((1,), (0,))), total


def near_attend_kernel(order_ref, q_ref, near_ref, next_ref, count_ref, part_ref, total_ref, expo_ref):
    queries = jnp.concatenate([q_ref[0, 0], q_ref[0, 1]], axis=0)
    blocks = [near_ref.at[0], near_ref.at[1], next_ref.at[0], next_ref.at[1]]
    part, total = partial(order_ref, 0, queries, blocks, count_ref, expo_ref)
    part_ref[...] = part
    total_ref[...] = jnp.broadcast_to(total, (4 * SPAN, 128))


def far_attend_kernel(order_ref, q_ref, far_ref, count_ref, part_ref, total_ref, out_ref, expo_ref):
    queries = jnp.concatenate([q_ref[0, 0], q_ref[0, 1]], axis=0)
    blocks = [far_ref.at[k, i] for k in range(2) for i in range(2)]
    part, total = partial(order_ref, 4, queries, blocks, count_ref, expo_ref)
    before = total_ref[:, 0:1]
    both = total + before
    inverse = jnp.where(both > 0.0, 1.0 / both, 0.0)
    part = (part * (total * inverse) + part_ref[...] * (before * inverse)).astype(BF16)
    for j in range(4):
        rows = slice(j * SPAN, (j + 1) * SPAN)
        out_ref[j // 2, 0, j % 2, :SPAN, :] = part[rows]
        tail = jnp.broadcast_to(sums_to_row(both[rows]), (ROWS - SPAN, 128))
        out_ref[j // 2, 0, j % 2, SPAN:, :] = tail.astype(BF16)


QUERY_SPEC = pl.BlockSpec((1, 2, 128, HEAD_DIM), lambda i, *_: (i, 0, 0, 0))
COUNT_SPEC = pl.BlockSpec((1, 8, 4, HALF), lambda i, *_: (i, 0, 0, 0))
PART_SPEC = pl.BlockSpec((4 * SPAN, HEAD_DIM), lambda i, *_: (i, 0))


def attend_near(order, queries, near, following, counts):
    block = pl.BlockSpec((2, 2, HALF, HEAD_DIM), lambda i, *_: (0, 0, 0, 0))
    return pl.pallas_call(
        near_attend_kernel,
        grid_spec=pltpu.PrefetchScalarGridSpec(
            num_scalar_prefetch=1,
            grid=(4,),
            in_specs=[QUERY_SPEC, block, block, COUNT_SPEC],
            out_specs=[PART_SPEC, PART_SPEC],
            scratch_shapes=[pltpu.VMEM((4 * SPAN, 4 * HALF), F32)],
        ),
        out_shape=[jax.ShapeDtypeStruct((16 * SPAN, HEAD_DIM), F32)] * 2,
        name="attend_near",
    )(order, queries, near, following, counts)


def attend_far(order, queries, beyond, counts, part, total):
    return pl.pallas_call(
        far_attend_kernel,
        grid_spec=pltpu.PrefetchScalarGridSpec(
            num_scalar_prefetch=1,
            grid=(4,),
            in_specs=[
                QUERY_SPEC,
                pl.BlockSpec((2, 2, 2, HALF, HEAD_DIM), lambda i, *_: (0, 0, 0, 0, 0)),
                COUNT_SPEC,
                PART_SPEC,
                PART_SPEC,
            ],
            out_specs=pl.BlockSpec((2, 1, 2, ROWS, HEAD_DIM), lambda i, *_: (0, i, 0, 0, 0)),
            scratch_shapes=[pltpu.VMEM((4 * SPAN, 4 * HALF), F32)],
        ),
        out_shape=jax.ShapeDtypeStruct((2, 4, 2, ROWS, HEAD_DIM), BF16),
        name="attend_far",
    )(order, queries, beyond, counts, part, total)


def merge(parts):
    sums = [row_to_sums(p[SPAN : SPAN + 1, :].astype(F32)) for p in parts]
    total = functools.reduce(jnp.add, sums)
    mixed = functools.reduce(
        jnp.add, [p[:SPAN, :].astype(F32) * (s / total) for p, s in zip(parts, sums)]
    )
    return mixed, total


def mix_kernel(place_ref, parts_ref, w0_ref, w1_ref, w2_ref, w3_ref, out_ref, att_ref):
    @pl.when(pl.program_id(0) == 0)
    def _():
        for s in range(2):
            for c in range(2):
                mixed, _ = merge([parts_ref[s, z, c] for z in range(4)])
                att_ref[2 * s + c] = mixed.astype(BF16)

    place = place_ref[0]
    acc = None
    for k, ref in enumerate((w0_ref, w1_ref, w2_ref, w3_ref)):
        term = dot(att_ref[place ^ k], ref[...], ((1,), (1,)))
        acc = term if acc is None else acc + term
    for d in range(out_ref.shape[0]):
        out_ref[d] = acc[:, d * HEAD_DIM : (d + 1) * HEAD_DIM].astype(BF16)


def mix(place, parts, weights):
    step = 8
    weight = pl.BlockSpec((step * HEAD_DIM, HEAD_DIM), lambda i, *_: (i, 0))
    return pl.pallas_call(
        mix_kernel,
        grid_spec=pltpu.PrefetchScalarGridSpec(
            num_scalar_prefetch=1,
            grid=(32 // step,),
            in_specs=[
                pl.BlockSpec((2, 4, 2, ROWS, HEAD_DIM), lambda i, *_: (0, 0, 0, 0, 0)),
                weight,
                weight,
                weight,
                weight,
            ],
            out_specs=pl.BlockSpec((step, SPAN, HEAD_DIM), lambda i, *_: (i, 0, 0)),
            scratch_shapes=[pltpu.VMEM((4, SPAN, HEAD_DIM), BF16)],
        ),
        out_shape=jax.ShapeDtypeStruct((32, SPAN, HEAD_DIM), BF16),
        name="mix",
    )(place, parts, *weights)


def swap(value, axis):
    return lax.ppermute(value, axis, [(0, 1), (1, 0)])


def multiplicities(nb_ids, nb_index):
    place = nb_ids % SHARD
    place = jnp.where(place < HALF, place, place + (2 * HALF - SHARD))
    upper = (nb_ids // SHARD) * 32 + place // 32
    one_upper = (upper[:, :, None] == jnp.arange(512)).astype(BF16)
    one_lower = ((place % 32)[:, :, None] == jnp.arange(32)).astype(BF16)
    per_block = jnp.einsum("nip,niq->npq", one_upper, one_lower, preferred_element_type=F32)
    pick = jnp.sum((nb_index[:, :, None] == jnp.arange(8)).astype(F32), axis=1)
    counts = jnp.einsum(
        "gn,npq->gpq", pick.astype(BF16), per_block.astype(BF16), preferred_element_type=F32
    )
    return counts.astype(BF16)


def half_of(table, tokens, core):
    rows = lax.dynamic_slice_in_dim(table, core * (SHARD - HALF), HALF)
    return jnp.concatenate([rows, lax.dynamic_slice_in_dim(tokens, core * 128, 128)], axis=0)


def pairs(size, turn):
    out = []
    for place in range(size):
        for core in range(2):
            spot = (place - core) % size
            other = spot ^ 1 if turn == 0 else spot + (1 if spot % 2 else -1)
            out.append((2 * place + core, 2 * ((other + core) % size) + core))
    return out


def exchange(value, axis, size, turn):
    return lax.ppermute(value, (axis, "c"), pairs(size, turn))


def after(value, *others):
    return lax.optimization_barrier((value, *others))[0]


def feature_rows(projections, section):
    start = section * 2048
    encoder = lax.dynamic_slice(projections, (0, 0, start, 0), (1, 2, 2048, 128))
    decoder = lax.dynamic_slice(projections, (1, 0, start, 0), (1, 1, 2048, 128))
    return jnp.concatenate([encoder[0], decoder[0]], axis=0)


def step(tokens, nb_ids, nb_index, table, norm_gains, projections):
    core, section, here = lax.axis_index("c"), lax.axis_index("s"), lax.axis_index("y")
    column = lax.axis_index("x")

    own = half_of(table, tokens, core)
    got = swap(half_of(table, tokens, 1 - core), "c")
    across = swap(feature_rows(projections, 1 - section), "s")
    chunk = jnp.where(core == 0, jnp.stack([own, got]), jnp.stack([got, own]))
    first = exchange(chunk, "y", 8, 0)
    second = exchange(jnp.stack([chunk, first]), "y", 8, 1)
    mine = after(feature_rows(projections, section), first)
    beside = swap(mine, "c")

    gains = lax.dynamic_slice_in_dim(norm_gains, section * 2048, 2048, axis=1)
    gains = gains.reshape(2, 8, 2, 128).transpose(1, 2, 0, 3)
    counts = multiplicities(nb_ids, nb_index).reshape(2, 2, 4, 4 * 1024)
    counts = lax.dynamic_index_in_dim(counts, core, 0, keepdims=False)
    counts = counts.transpose(1, 0, 2).reshape(4, 64, 128)
    sign = 1 - 2 * ((here + core) % 2)
    offsets = jnp.array([0, 1, -1, -2, 2, 3, -3, -4], jnp.int32)
    source = jnp.concatenate([(here + sign * offsets) % 8, core.reshape(1)]).astype(jnp.int32)
    sign = 1 - 2 * ((column + core) % 2)
    origin = (column + sign * offsets[:4]) % 4
    order = (2 * origin[:, None] + jnp.stack([core, 1 - core])[None]).reshape(8).astype(jnp.int32)

    third = exchange(second, "y", 8, 0)
    third, gains, counts, source, order = lax.optimization_barrier(
        (third, gains, counts, source, order)
    )
    fourth = exchange(third, "y", 8, 1)
    diagonal = swap(after(across, third), "c")

    lhs, squares, send = project_far(
        source, (chunk, first, second, third, fourth), gains, (across, diagonal)
    )
    other = swap(send, "s")
    keep, keep_q = project_near(lhs, (mine, beside))
    near, give, queries = finish(source, keep, keep_q, squares, other, counts)
    queries = queries.reshape(8, 192, 128)
    queries = lax.all_to_all(queries, ("zh", "c"), 0, 0)
    near = jnp.stack([near, swap(give, "c")])
    following = exchange(near, "x", 4, 0)
    following = after(following, queries)
    beyond = exchange(jnp.stack([near, following]), "x", 4, 1)
    queries = queries.reshape(4, 2, 192, 128)
    counts = queries[:, :, 128:].reshape(4, 2, 2, 8, HALF).transpose(0, 3, 1, 2, 4)
    counts = counts.reshape(4, 8, 4, HALF)

    wo = after(projections[1, 1], queries)
    wo_section = swap(wo, "s")
    wo_beside = swap(wo, "c")

    part, total = attend_near(order, queries, near, following, counts)
    parts = attend_far(order, queries, beyond, counts, part, total)
    wo_diagonal = swap(after(wo_section, parts), "c")
    parts = lax.all_to_all(parts.reshape(16, ROWS, HEAD_DIM), ("s", "zh", "c"), 0, 0)
    place = (section * 2 + core).astype(jnp.int32).reshape(1)
    weights = (wo, wo_beside, wo_section, wo_diagonal)
    out = mix(place, parts.reshape(2, 4, 2, ROWS, HEAD_DIM), weights)
    out = lax.all_to_all(out, ("s", "y", "c"), 0, 0)
    out = jnp.sum(out.reshape(2, 8, 2, SPAN, HEAD_DIM).astype(F32), axis=1)
    return out.astype(BF16).reshape(4 * SPAN, HEAD_DIM)


def solution(mesh):
    fine = Mesh(mesh.devices.reshape(2, 4, 4, 8, 2), ("s", "zh", "x", "y", "c"))
    batch, cols = ("zh", "x"), ("s", "y", "c")
    return jax.shard_map(
        step,
        mesh=fine,
        in_specs=(
            P(batch, cols),
            P(batch, None),
            P(batch, None),
            P(batch, cols),
            P(),
            P(None, None, None, cols),
        ),
        out_specs=P(batch, cols),
        check_vma=False,
    )
```

```python
import functools
import math

import jax
import jax.numpy as jnp
from jax import lax
from jax.experimental import pallas as pl
from jax.experimental.pallas import tpu as pltpu
from jax.sharding import Mesh
from jax.sharding import PartitionSpec as P

HEAD_DIM = 128
SPAN = 64
ROWS = 72
SHARD = 1000
HALF = 512
ROWS_IN = HALF + 128
EPS = 1e-06
SCALE = math.log2(math.e) / math.sqrt(HEAD_DIM)
F32 = jnp.float32
BF16 = jnp.bfloat16


def dot(a, b, dims):
    return lax.dot_general(a, b, (dims, ((), ())), preferred_element_type=F32)


def diagonal(shape):
    row = lax.broadcasted_iota(jnp.int32, shape, len(shape) - 2)
    lane = lax.broadcasted_iota(jnp.int32, shape, len(shape) - 1)
    return row == lane % SPAN


def sums_to_row(column):
    row = jnp.sum(jnp.where(diagonal((SPAN, 128)), column, 0.0), axis=0, keepdims=True)
    upper = row.astype(BF16).astype(F32)
    lane = lax.broadcasted_iota(jnp.int32, (1, 128), 1)
    return jnp.where(lane < SPAN, upper, row - upper)


def row_to_sums(row):
    return jnp.sum(jnp.where(diagonal((SPAN, 128)), row, 0.0), axis=1, keepdims=True)


def column_to_row(column):
    square = (128, 128)
    same = lax.broadcasted_iota(jnp.int32, square, 0) == lax.broadcasted_iota(jnp.int32, square, 1)
    return jnp.sum(jnp.where(same, column, 0.0), axis=0, keepdims=True)


def row_to_column(row):
    square = (128, 128)
    same = lax.broadcasted_iota(jnp.int32, square, 0) == lax.broadcasted_iota(jnp.int32, square, 1)
    return jnp.sum(jnp.where(same, row, 0.0), axis=1, keepdims=True)


def far_kernel(source_ref, b0_ref, b1_ref, b2_ref, b3_ref, b4_ref, gain_ref, w0_ref, w1_ref, lhs_ref, squares_ref, send_ref):
    square = jnp.zeros((ROWS_IN, 128), F32)
    pieces = [b0_ref, b1_ref]
    for ref in (b2_ref, b3_ref, b4_ref):
        pieces += [ref.at[0], ref.at[1]]
    for k, ref in enumerate(pieces):
        source = source_ref[k]
        for i in range(2):
            wide = ref[i].astype(F32)
            square = square + wide * wide
            gain = gain_ref[source, i]
            lanes = slice(i * 128, (i + 1) * 128)
            lhs_ref[source, :HALF, lanes] = (wide[:HALF] * gain[0:1]).astype(BF16)
            lhs_ref[source, HALF:, lanes] = (wide[HALF:] * gain[1:2]).astype(BF16)
    sums = jnp.sum(square, axis=1, keepdims=True)
    tail = [column_to_row(sums[k * 128 : (k + 1) * 128]) for k in range(5)]
    squares = jnp.concatenate(tail + [jnp.zeros((3, 128), F32)], axis=0)
    squares_ref[...] = squares
    upper = squares.astype(BF16)
    lower = (squares - upper.astype(F32)).astype(BF16)
    for i in range(4):
        send_ref[i, HALF + 64 :, :] = lower if i == 1 else upper
    lhs = jnp.concatenate([lhs_ref[y] for y in range(8)], axis=1)
    for m, ref in enumerate((w0_ref, w1_ref)):
        pair = jnp.concatenate([ref[0], ref[1]], axis=1)
        both = dot(lhs[:HALF], pair, ((1,), (0,)))
        query = dot(lhs[HALF:], ref[2], ((1,), (0,)))
        for i in range(2):
            send_ref[2 * m + i, :HALF, :] = both[:, i * 128 : (i + 1) * 128].astype(BF16)
            send_ref[2 * m + i, HALF : HALF + 64, :] = query[i * 64 : (i + 1) * 64].astype(BF16)


def project_far(source, blocks, gains, weights):
    vmem = pl.BlockSpec(memory_space=pltpu.VMEM)
    return pl.pallas_call(
        far_kernel,
        in_specs=[pl.BlockSpec(memory_space=pltpu.SMEM)] + [vmem] * 8,
        out_specs=[vmem] * 3,
        out_shape=[
            jax.ShapeDtypeStruct((8, ROWS_IN, 256), BF16),
            jax.ShapeDtypeStruct((8, 128), F32),
            jax.ShapeDtypeStruct((4, HALF + 72, 128), BF16),
        ],
        name="project_far",
    )(source, *blocks, gains, *weights)


def near_kernel(lhs_ref, w0_ref, w1_ref, keep_ref, keep_q_ref):
    lhs = jnp.concatenate([lhs_ref[y] for y in range(8)], axis=1)
    for m, ref in enumerate((w0_ref, w1_ref)):
        pair = jnp.concatenate([ref[0], ref[1]], axis=1)
        both = dot(lhs[:HALF], pair, ((1,), (0,)))
        keep_ref[m, 0] = both[:, :128]
        keep_ref[m, 1] = both[:, 128:]
        keep_q_ref[m] = dot(lhs[HALF:], ref[2], ((1,), (0,)))


def project_near(lhs, weights):
    vmem = pl.BlockSpec(memory_space=pltpu.VMEM)
    return pl.pallas_call(
        near_kernel,
        in_specs=[vmem] * 3,
        out_specs=[vmem] * 2,
        out_shape=[
            jax.ShapeDtypeStruct((2, 2, HALF, 128), F32),
            jax.ShapeDtypeStruct((2, 128, 128), F32),
        ],
        name="project_near",
    )(lhs, *weights)


def finish_kernel(source_ref, keep_ref, keep_q_ref, squares_ref, other_ref, count_ref, own_ref, give_ref, q_ref):
    core = source_ref[8]
    ours = squares_ref[...]
    theirs = other_ref[0, HALF + 64 :, :].astype(F32) + other_ref[1, HALF + 64 :, :].astype(F32)
    rate = lax.rsqrt((ours + theirs) * (1.0 / 4096) + EPS)
    for m, ref in enumerate((own_ref, give_ref)):
        head = core ^ m
        for k in range(4):
            rows = slice(k * 128, (k + 1) * 128)
            column = row_to_column(rate[k : k + 1])
            for i in range(2):
                total = keep_ref[m, i, rows] + other_ref[2 * m + i, rows, :].astype(F32)
                ref[i, rows] = (total * column).astype(BF16)
        column = row_to_column(rate[4:5])
        for i in range(2):
            rows = slice(i * 64, (i + 1) * 64)
            total = keep_q_ref[m, rows] + other_ref[2 * m + i, HALF : HALF + 64, :].astype(F32)
            value = (total * column[rows]).astype(BF16)
            for z in range(4):
                q_ref[z, head, rows] = value
        for z in range(4):
            q_ref[z, m, 128:] = count_ref[z]


def finish(source, keep, keep_q, squares, other, counts):
    vmem = pl.BlockSpec(memory_space=pltpu.VMEM)
    half = jax.ShapeDtypeStruct((2, HALF, 128), BF16)
    return pl.pallas_call(
        finish_kernel,
        in_specs=[pl.BlockSpec(memory_space=pltpu.SMEM)] + [vmem] * 5,
        out_specs=[vmem] * 3,
        out_shape=[half, half, jax.ShapeDtypeStruct((4, 2, 192, 128), BF16)],
        name="finish",
    )(source, keep, keep_q, squares, other, counts)


def partial(order_ref, first, queries, blocks, count_ref, expo_ref):
    total = jnp.zeros((4 * SPAN, 128), F32)
    for k, block in enumerate(blocks):
        lanes = slice(k * HALF, (k + 1) * HALF)
        bias = jnp.log2(count_ref[0, order_ref[first + k]].astype(F32))
        spread = jnp.broadcast_to(bias[:, None, :], (4, SPAN, HALF)).reshape(4 * SPAN, HALF)
        scores = dot(queries, block[0], ((1,), (1,)))
        expo = jnp.exp2(scores * SCALE + spread)
        expo_ref[:, lanes] = expo
        for i in range(HALF // 128):
            total = total + expo[:, i * 128 : (i + 1) * 128]
    total = jnp.sum(total, axis=1, keepdims=True)
    inverse = jnp.where(total > 0.0, 1.0 / total, 0.0)
    weights = (expo_ref[...] * inverse).astype(BF16)
    values = jnp.concatenate([block[1] for block in blocks], axis=0)
    return dot(weights, values, ((1,), (0,))), total


def near_attend_kernel(order_ref, q_ref, near_ref, next_ref, count_ref, part_ref, total_ref, expo_ref):
    queries = jnp.concatenate([q_ref[0, 0], q_ref[0, 1]], axis=0)
    blocks = [near_ref.at[0], near_ref.at[1], next_ref.at[0], next_ref.at[1]]
    part, total = partial(order_ref, 0, queries, blocks, count_ref, expo_ref)
    part_ref[...] = part
    total_ref[...] = jnp.broadcast_to(total, (4 * SPAN, 128))


def far_attend_kernel(order_ref, q_ref, far_ref, count_ref, part_ref, total_ref, out_ref, expo_ref):
    queries = jnp.concatenate([q_ref[0, 0], q_ref[0, 1]], axis=0)
    blocks = [far_ref.at[k, i] for k in range(2) for i in range(2)]
    part, total = partial(order_ref, 4, queries, blocks, count_ref, expo_ref)
    before = total_ref[:, 0:1]
    both = total + before
    inverse = jnp.where(both > 0.0, 1.0 / both, 0.0)
    part = (part * (total * inverse) + part_ref[...] * (before * inverse)).astype(BF16)
    for j in range(4):
        rows = slice(j * SPAN, (j + 1) * SPAN)
        out_ref[j // 2, 0, j % 2, :SPAN, :] = part[rows]
        tail = jnp.broadcast_to(sums_to_row(both[rows]), (ROWS - SPAN, 128))
        out_ref[j // 2, 0, j % 2, SPAN:, :] = tail.astype(BF16)


QUERY_SPEC = pl.BlockSpec((1, 2, 128, HEAD_DIM), lambda i, *_: (i, 0, 0, 0))
COUNT_SPEC = pl.BlockSpec((1, 8, 4, HALF), lambda i, *_: (i, 0, 0, 0))
PART_SPEC = pl.BlockSpec((4 * SPAN, HEAD_DIM), lambda i, *_: (i, 0))


def attend_near(order, queries, near, following, counts):
    block = pl.BlockSpec((2, 2, HALF, HEAD_DIM), lambda i, *_: (0, 0, 0, 0))
    return pl.pallas_call(
        near_attend_kernel,
        grid_spec=pltpu.PrefetchScalarGridSpec(
            num_scalar_prefetch=1,
            grid=(4,),
            in_specs=[QUERY_SPEC, block, block, COUNT_SPEC],
            out_specs=[PART_SPEC, PART_SPEC],
            scratch_shapes=[pltpu.VMEM((4 * SPAN, 4 * HALF), F32)],
        ),
        out_shape=[jax.ShapeDtypeStruct((16 * SPAN, HEAD_DIM), F32)] * 2,
        name="attend_near",
    )(order, queries, near, following, counts)


def attend_far(order, queries, beyond, counts, part, total):
    return pl.pallas_call(
        far_attend_kernel,
        grid_spec=pltpu.PrefetchScalarGridSpec(
            num_scalar_prefetch=1,
            grid=(4,),
            in_specs=[
                QUERY_SPEC,
                pl.BlockSpec((2, 2, 2, HALF, HEAD_DIM), lambda i, *_: (0, 0, 0, 0, 0)),
                COUNT_SPEC,
                PART_SPEC,
                PART_SPEC,
            ],
            out_specs=pl.BlockSpec((2, 1, 2, ROWS, HEAD_DIM), lambda i, *_: (0, i, 0, 0, 0)),
            scratch_shapes=[pltpu.VMEM((4 * SPAN, 4 * HALF), F32)],
        ),
        out_shape=jax.ShapeDtypeStruct((2, 4, 2, ROWS, HEAD_DIM), BF16),
        name="attend_far",
    )(order, queries, beyond, counts, part, total)


def merge(parts):
    sums = [row_to_sums(p[SPAN : SPAN + 1, :].astype(F32)) for p in parts]
    total = functools.reduce(jnp.add, sums)
    mixed = functools.reduce(
        jnp.add, [p[:SPAN, :].astype(F32) * (s / total) for p, s in zip(parts, sums)]
    )
    return mixed, total


def mix_kernel(place_ref, parts_ref, w0_ref, w1_ref, w2_ref, w3_ref, out_ref, att_ref):
    @pl.when(pl.program_id(0) == 0)
    def _():
        for s in range(2):
            for c in range(2):
                mixed, _ = merge([parts_ref[s, z, c] for z in range(4)])
                att_ref[2 * s + c] = mixed.astype(BF16)

    place = place_ref[0]
    acc = None
    for k, ref in enumerate((w0_ref, w1_ref, w2_ref, w3_ref)):
        term = dot(att_ref[place ^ k], ref[...], ((1,), (1,)))
        acc = term if acc is None else acc + term
    for d in range(out_ref.shape[0]):
        out_ref[d] = acc[:, d * HEAD_DIM : (d + 1) * HEAD_DIM].astype(BF16)


def mix(place, parts, weights):
    step = 8
    weight = pl.BlockSpec((step * HEAD_DIM, HEAD_DIM), lambda i, *_: (i, 0))
    return pl.pallas_call(
        mix_kernel,
        grid_spec=pltpu.PrefetchScalarGridSpec(
            num_scalar_prefetch=1,
            grid=(32 // step,),
            in_specs=[
                pl.BlockSpec((2, 4, 2, ROWS, HEAD_DIM), lambda i, *_: (0, 0, 0, 0, 0)),
                weight,
                weight,
                weight,
                weight,
            ],
            out_specs=pl.BlockSpec((step, SPAN, HEAD_DIM), lambda i, *_: (i, 0, 0)),
            scratch_shapes=[pltpu.VMEM((4, SPAN, HEAD_DIM), BF16)],
        ),
        out_shape=jax.ShapeDtypeStruct((32, SPAN, HEAD_DIM), BF16),
        name="mix",
    )(place, parts, *weights)


def swap(value, axis):
    return lax.ppermute(value, axis, [(0, 1), (1, 0)])


def multiplicities(nb_ids, nb_index):
    place = nb_ids % SHARD
    place = jnp.where(place < HALF, place, place + (2 * HALF - SHARD))
    upper = (nb_ids // SHARD) * 32 + place // 32
    one_upper = (upper[:, :, None] == jnp.arange(512)).astype(BF16)
    one_lower = ((place % 32)[:, :, None] == jnp.arange(32)).astype(BF16)
    per_block = jnp.einsum("nip,niq->npq", one_upper, one_lower, preferred_element_type=F32)
    pick = jnp.sum((nb_index[:, :, None] == jnp.arange(8)).astype(F32), axis=1)
    counts = jnp.einsum(
        "gn,npq->gpq", pick.astype(BF16), per_block.astype(BF16), preferred_element_type=F32
    )
    return counts.astype(BF16)


def half_of(table, tokens, core):
    rows = lax.dynamic_slice_in_dim(table, core * (SHARD - HALF), HALF)
    return jnp.concatenate([rows, lax.dynamic_slice_in_dim(tokens, core * 128, 128)], axis=0)


def pairs(size, turn):
    out = []
    for place in range(size):
        for core in range(2):
            spot = (place - core) % size
            other = spot ^ 1 if turn == 0 else spot + (1 if spot % 2 else -1)
            out.append((2 * place + core, 2 * ((other + core) % size) + core))
    return out


def exchange(value, axis, size, turn):
    return lax.ppermute(value, (axis, "c"), pairs(size, turn))


def after(value, *others):
    return lax.optimization_barrier((value, *others))[0]


def feature_rows(projections, section):
    start = section * 2048
    encoder = lax.dynamic_slice(projections, (0, 0, start, 0), (1, 2, 2048, 128))
    decoder = lax.dynamic_slice(projections, (1, 0, start, 0), (1, 1, 2048, 128))
    return jnp.concatenate([encoder[0], decoder[0]], axis=0)


def step(tokens, nb_ids, nb_index, table, norm_gains, projections):
    core, section, here = lax.axis_index("c"), lax.axis_index("s"), lax.axis_index("y")
    column = lax.axis_index("x")

    own = half_of(table, tokens, core)
    got = swap(half_of(table, tokens, 1 - core), "c")
    across = swap(feature_rows(projections, 1 - section), "s")
    chunk = jnp.where(core == 0, jnp.stack([own, got]), jnp.stack([got, own]))
    first = exchange(chunk, "y", 8, 0)
    second = exchange(jnp.stack([chunk, first]), "y", 8, 1)
    mine = feature_rows(after(projections, first), section)
    beside = swap(mine, "c")

    gains = lax.dynamic_slice_in_dim(norm_gains, section * 2048, 2048, axis=1)
    gains = gains.reshape(2, 8, 2, 128).transpose(1, 2, 0, 3)
    counts = multiplicities(after(nb_ids, first), nb_index).reshape(2, 2, 4, 4 * 1024)
    counts = lax.dynamic_index_in_dim(counts, core, 0, keepdims=False)
    counts = counts.transpose(1, 0, 2).reshape(4, 64, 128)
    sign = 1 - 2 * ((here + core) % 2)
    offsets = after(jnp.array([0, 1, -1, -2, 2, 3, -3, -4], jnp.int32), first)
    source = jnp.concatenate([(here + sign * offsets) % 8, core.reshape(1)]).astype(jnp.int32)
    sign = 1 - 2 * ((column + core) % 2)
    origin = (column + sign * offsets[:4]) % 4
    order = (2 * origin[:, None] + jnp.stack([core, 1 - core])[None]).reshape(8).astype(jnp.int32)

    third = exchange(second, "y", 8, 0)
    third, gains, counts, source, order = lax.optimization_barrier(
        (third, gains, counts, source, order)
    )
    fourth = exchange(third, "y", 8, 1)
    diagonal = swap(after(across, third), "c")

    lhs, squares, send = project_far(
        source, (chunk, first, second, third, fourth), gains, (across, diagonal)
    )
    wo = after(projections[1, 1], third)
    wo_section = swap(wo, "s")
    other = swap(send, "s")
    keep, keep_q = project_near(lhs, (mine, beside))
    near, give, queries = finish(source, keep, keep_q, squares, other, counts)
    queries = queries.reshape(8, 192, 128)
    queries = lax.all_to_all(queries, ("zh", "c"), 0, 0)
    near = jnp.stack([near, swap(give, "c")])
    following = exchange(near, "x", 4, 0)
    beyond = exchange(jnp.stack([near, following]), "x", 4, 1)
    queries = queries.reshape(4, 2, 192, 128)
    counts = queries[:, :, 128:].reshape(4, 2, 2, 8, HALF).transpose(0, 3, 1, 2, 4)
    counts = counts.reshape(4, 8, 4, HALF)

    wo_beside = swap(wo, "c")
    wo_diagonal = swap(wo_section, "c")

    part, total = attend_near(order, queries, near, following, counts)
    parts = attend_far(order, queries, beyond, counts, part, total)
    parts = lax.all_to_all(parts.reshape(16, ROWS, HEAD_DIM), ("s", "zh", "c"), 0, 0)
    place = (section * 2 + core).astype(jnp.int32).reshape(1)
    weights = (wo, wo_beside, wo_section, wo_diagonal)
    out = mix(place, parts.reshape(2, 4, 2, ROWS, HEAD_DIM), weights)
    out = lax.all_to_all(out, ("s", "y", "c"), 0, 0)
    out = jnp.sum(out.reshape(2, 8, 2, SPAN, HEAD_DIM).astype(F32), axis=1)
    return out.astype(BF16).reshape(4 * SPAN, HEAD_DIM)


def solution(mesh):
    fine = Mesh(mesh.devices.reshape(2, 4, 4, 8, 2), ("s", "zh", "x", "y", "c"))
    batch, cols = ("zh", "x"), ("s", "y", "c")
    return jax.shard_map(
        step,
        mesh=fine,
        in_specs=(
            P(batch, cols),
            P(batch, None),
            P(batch, None),
            P(batch, cols),
            P(),
            P(None, None, None, cols),
        ),
        out_specs=P(batch, cols),
        check_vma=False,
    )
```

```python
import functools
import math

import jax
import jax.numpy as jnp
from jax import lax
from jax.experimental import pallas as pl
from jax.experimental.pallas import tpu as pltpu
from jax.sharding import Mesh
from jax.sharding import PartitionSpec as P

HEAD_DIM = 128
SPAN = 64
ROWS = 72
SHARD = 1000
HALF = 512
ROWS_IN = HALF + 128
EPS = 1e-06
SCALE = math.log2(math.e) / math.sqrt(HEAD_DIM)
F32 = jnp.float32
BF16 = jnp.bfloat16


def dot(a, b, dims):
    return lax.dot_general(a, b, (dims, ((), ())), preferred_element_type=F32)


def diagonal(shape):
    row = lax.broadcasted_iota(jnp.int32, shape, len(shape) - 2)
    lane = lax.broadcasted_iota(jnp.int32, shape, len(shape) - 1)
    return row == lane % SPAN


def sums_to_row(column):
    row = jnp.sum(jnp.where(diagonal((SPAN, 128)), column, 0.0), axis=0, keepdims=True)
    upper = row.astype(BF16).astype(F32)
    lane = lax.broadcasted_iota(jnp.int32, (1, 128), 1)
    return jnp.where(lane < SPAN, upper, row - upper)


def row_to_sums(row):
    return jnp.sum(jnp.where(diagonal((SPAN, 128)), row, 0.0), axis=1, keepdims=True)


def column_to_row(column):
    square = (128, 128)
    same = lax.broadcasted_iota(jnp.int32, square, 0) == lax.broadcasted_iota(jnp.int32, square, 1)
    return jnp.sum(jnp.where(same, column, 0.0), axis=0, keepdims=True)


def row_to_column(row):
    square = (128, 128)
    same = lax.broadcasted_iota(jnp.int32, square, 0) == lax.broadcasted_iota(jnp.int32, square, 1)
    return jnp.sum(jnp.where(same, row, 0.0), axis=1, keepdims=True)


def normed(ref, gain, lhs_ref, slot, square):
    for i in range(2):
        wide = ref[i].astype(F32)
        square = square + wide * wide
        lanes = slice(i * 128, (i + 1) * 128)
        lhs_ref[slot, :HALF, lanes] = (wide[:HALF] * gain[i, 0:1]).astype(BF16)
        lhs_ref[slot, HALF:, lanes] = (wide[HALF:] * gain[i, 1:2]).astype(BF16)
    return square


def columns(pieces):
    return jnp.concatenate(pieces, axis=1)


def rows_of(ref, which, source_ref, slots):
    picked = [
        ref[which, pl.ds(pl.multiple_of(source_ref[k] * 256, 256), 256), :] for k in slots
    ]
    return jnp.concatenate(picked, axis=0)


def early_kernel(source_ref, b0_ref, b1_ref, b2_ref, b3_ref, gain_ref, w0_ref, w1_ref, lhs_ref, square_ref, kv_ref, q_ref):
    square = jnp.zeros((ROWS_IN, 128), F32)
    pieces = [b0_ref, b1_ref, b2_ref.at[0], b2_ref.at[1], b3_ref.at[0], b3_ref.at[1]]
    for k, ref in enumerate(pieces):
        square = normed(ref, gain_ref[source_ref[k]], lhs_ref, k, square)
    square_ref[...] = square
    lhs = columns([lhs_ref[k] for k in range(6)])
    for m, ref in enumerate((w0_ref, w1_ref)):
        pair = columns([rows_of(ref, i, source_ref, range(6)) for i in range(2)])
        kv_ref[m] = dot(lhs[:HALF], pair, ((1,), (0,)))
        q_ref[m] = dot(lhs[HALF:], rows_of(ref, 2, source_ref, range(6)), ((1,), (0,)))


def project_early(source, blocks, gains, weights):
    vmem = pl.BlockSpec(memory_space=pltpu.VMEM)
    return pl.pallas_call(
        early_kernel,
        in_specs=[pl.BlockSpec(memory_space=pltpu.SMEM)] + [vmem] * 7,
        out_specs=[vmem] * 4,
        out_shape=[
            jax.ShapeDtypeStruct((6, ROWS_IN, 256), BF16),
            jax.ShapeDtypeStruct((ROWS_IN, 128), F32),
            jax.ShapeDtypeStruct((2, HALF, 256), F32),
            jax.ShapeDtypeStruct((2, 128, 128), F32),
        ],
        name="project_early",
    )(source, *blocks, gains, *weights)


def late_kernel(source_ref, b4_ref, gain_ref, w00_ref, w01_ref, w10_ref, w11_ref, square_ref, kv_ref, q_ref, lhs_ref, squares_ref, send_ref):
    square = square_ref[...]
    for k in range(2):
        square = normed(b4_ref.at[k], gain_ref[source_ref[6 + k]], lhs_ref, k, square)
    sums = jnp.sum(square, axis=1, keepdims=True)
    tail = [column_to_row(sums[k * 128 : (k + 1) * 128]) for k in range(5)]
    squares = jnp.concatenate(tail + [jnp.zeros((3, 128), F32)], axis=0)
    squares_ref[...] = squares
    upper = squares.astype(BF16)
    lower = (squares - upper.astype(F32)).astype(BF16)
    for i in range(4):
        send_ref[i, HALF + 64 :, :] = lower if i == 1 else upper
    lhs = columns([lhs_ref[k] for k in range(2)])
    for m, (one, two) in enumerate(((w00_ref, w01_ref), (w10_ref, w11_ref))):
        rows = [jnp.concatenate([one[i], two[i]], axis=0) for i in range(3)]
        both = kv_ref[m] + dot(lhs[:HALF], columns(rows[:2]), ((1,), (0,)))
        query = q_ref[m] + dot(lhs[HALF:], rows[2], ((1,), (0,)))
        for i in range(2):
            send_ref[2 * m + i, :HALF, :] = both[:, i * 128 : (i + 1) * 128].astype(BF16)
            send_ref[2 * m + i, HALF : HALF + 64, :] = query[i * 64 : (i + 1) * 64].astype(BF16)


def whole_spec(*shape):
    return pl.BlockSpec(shape, lambda i, *_: (0,) * len(shape))


def project_late(source, block, gains, weights, square, kv, query):
    picked = [pl.BlockSpec((3, 256, 128), lambda i, s, k=k: (0, s[6 + k], 0)) for k in range(2)]
    return pl.pallas_call(
        late_kernel,
        grid_spec=pltpu.PrefetchScalarGridSpec(
            num_scalar_prefetch=1,
            grid=(1,),
            in_specs=[
                whole_spec(2, 2, ROWS_IN, 128),
                whole_spec(8, 2, 2, 128),
                *picked,
                *picked,
                whole_spec(ROWS_IN, 128),
                whole_spec(2, HALF, 256),
                whole_spec(2, 128, 128),
            ],
            out_specs=[
                whole_spec(2, ROWS_IN, 256),
                whole_spec(8, 128),
                whole_spec(4, HALF + 72, 128),
            ],
        ),
        out_shape=[
            jax.ShapeDtypeStruct((2, ROWS_IN, 256), BF16),
            jax.ShapeDtypeStruct((8, 128), F32),
            jax.ShapeDtypeStruct((4, HALF + 72, 128), BF16),
        ],
        name="project_late",
    )(source, block, gains, weights[0], weights[0], weights[1], weights[1], square, kv, query)


def near_kernel(source_ref, early_ref, late_ref, w0_ref, w1_ref, keep_ref, keep_q_ref):
    lhs = columns([early_ref[k] for k in range(6)] + [late_ref[k] for k in range(2)])
    for m, ref in enumerate((w0_ref, w1_ref)):
        pair = columns([rows_of(ref, i, source_ref, range(8)) for i in range(2)])
        both = dot(lhs[:HALF], pair, ((1,), (0,)))
        keep_ref[m, 0] = both[:, :128]
        keep_ref[m, 1] = both[:, 128:]
        keep_q_ref[m] = dot(lhs[HALF:], rows_of(ref, 2, source_ref, range(8)), ((1,), (0,)))


def project_near(source, early, late, weights):
    vmem = pl.BlockSpec(memory_space=pltpu.VMEM)
    return pl.pallas_call(
        near_kernel,
        in_specs=[pl.BlockSpec(memory_space=pltpu.SMEM)] + [vmem] * 4,
        out_specs=[vmem] * 2,
        out_shape=[
            jax.ShapeDtypeStruct((2, 2, HALF, 128), F32),
            jax.ShapeDtypeStruct((2, 128, 128), F32),
        ],
        name="project_near",
    )(source, early, late, *weights)


def finish_kernel(source_ref, keep_ref, keep_q_ref, squares_ref, other_ref, count_ref, own_ref, give_ref, q_ref):
    core = source_ref[8]
    ours = squares_ref[...]
    theirs = other_ref[0, HALF + 64 :, :].astype(F32) + other_ref[1, HALF + 64 :, :].astype(F32)
    rate = lax.rsqrt((ours + theirs) * (1.0 / 4096) + EPS)
    for m, ref in enumerate((own_ref, give_ref)):
        head = core ^ m
        for k in range(4):
            rows = slice(k * 128, (k + 1) * 128)
            column = row_to_column(rate[k : k + 1])
            for i in range(2):
                total = keep_ref[m, i, rows] + other_ref[2 * m + i, rows, :].astype(F32)
                ref[i, rows] = (total * column).astype(BF16)
        column = row_to_column(rate[4:5])
        for i in range(2):
            rows = slice(i * 64, (i + 1) * 64)
            total = keep_q_ref[m, rows] + other_ref[2 * m + i, HALF : HALF + 64, :].astype(F32)
            value = (total * column[rows]).astype(BF16)
            for z in range(4):
                q_ref[z, head, rows] = value
        for z in range(4):
            q_ref[z, m, 128:] = count_ref[z]


def finish(source, keep, keep_q, squares, other, counts):
    vmem = pl.BlockSpec(memory_space=pltpu.VMEM)
    half = jax.ShapeDtypeStruct((2, HALF, 128), BF16)
    return pl.pallas_call(
        finish_kernel,
        in_specs=[pl.BlockSpec(memory_space=pltpu.SMEM)] + [vmem] * 5,
        out_specs=[vmem] * 3,
        out_shape=[half, half, jax.ShapeDtypeStruct((4, 2, 192, 128), BF16)],
        name="finish",
    )(source, keep, keep_q, squares, other, counts)


def partial(order_ref, first, queries, blocks, count_ref, expo_ref):
    total = jnp.zeros((4 * SPAN, 128), F32)
    for k, block in enumerate(blocks):
        lanes = slice(k * HALF, (k + 1) * HALF)
        bias = jnp.log2(count_ref[0, order_ref[first + k]].astype(F32))
        spread = jnp.broadcast_to(bias[:, None, :], (4, SPAN, HALF)).reshape(4 * SPAN, HALF)
        scores = dot(queries, block[0], ((1,), (1,)))
        expo = jnp.exp2(scores * SCALE + spread)
        expo_ref[:, lanes] = expo
        for i in range(HALF // 128):
            total = total + expo[:, i * 128 : (i + 1) * 128]
    total = jnp.sum(total, axis=1, keepdims=True)
    inverse = jnp.where(total > 0.0, 1.0 / total, 0.0)
    weights = (expo_ref[...] * inverse).astype(BF16)
    values = jnp.concatenate([block[1] for block in blocks], axis=0)
    return dot(weights, values, ((1,), (0,))), total


def near_attend_kernel(order_ref, q_ref, near_ref, next_ref, count_ref, part_ref, total_ref, expo_ref):
    queries = jnp.concatenate([q_ref[0, 0], q_ref[0, 1]], axis=0)
    blocks = [near_ref.at[0], near_ref.at[1], next_ref.at[0], next_ref.at[1]]
    part, total = partial(order_ref, 0, queries, blocks, count_ref, expo_ref)
    part_ref[...] = part
    total_ref[...] = jnp.broadcast_to(total, (4 * SPAN, 128))


def far_attend_kernel(order_ref, q_ref, far_ref, count_ref, part_ref, total_ref, out_ref, expo_ref):
    queries = jnp.concatenate([q_ref[0, 0], q_ref[0, 1]], axis=0)
    blocks = [far_ref.at[k, i] for k in range(2) for i in range(2)]
    part, total = partial(order_ref, 4, queries, blocks, count_ref, expo_ref)
    before = total_ref[:, 0:1]
    both = total + before
    inverse = jnp.where(both > 0.0, 1.0 / both, 0.0)
    part = (part * (total * inverse) + part_ref[...] * (before * inverse)).astype(BF16)
    for j in range(4):
        rows = slice(j * SPAN, (j + 1) * SPAN)
        out_ref[j // 2, 0, j % 2, :SPAN, :] = part[rows]
        tail = jnp.broadcast_to(sums_to_row(both[rows]), (ROWS - SPAN, 128))
        out_ref[j // 2, 0, j % 2, SPAN:, :] = tail.astype(BF16)


QUERY_SPEC = pl.BlockSpec((1, 2, 128, HEAD_DIM), lambda i, *_: (i, 0, 0, 0))
COUNT_SPEC = pl.BlockSpec((1, 8, 4, HALF), lambda i, *_: (i, 0, 0, 0))
PART_SPEC = pl.BlockSpec((4 * SPAN, HEAD_DIM), lambda i, *_: (i, 0))


def attend_near(order, queries, near, following, counts):
    block = pl.BlockSpec((2, 2, HALF, HEAD_DIM), lambda i, *_: (0, 0, 0, 0))
    return pl.pallas_call(
        near_attend_kernel,
        grid_spec=pltpu.PrefetchScalarGridSpec(
            num_scalar_prefetch=1,
            grid=(4,),
            in_specs=[QUERY_SPEC, block, block, COUNT_SPEC],
            out_specs=[PART_SPEC, PART_SPEC],
            scratch_shapes=[pltpu.VMEM((4 * SPAN, 4 * HALF), F32)],
        ),
        out_shape=[jax.ShapeDtypeStruct((16 * SPAN, HEAD_DIM), F32)] * 2,
        name="attend_near",
    )(order, queries, near, following, counts)


def attend_far(order, queries, beyond, counts, part, total):
    return pl.pallas_call(
        far_attend_kernel,
        grid_spec=pltpu.PrefetchScalarGridSpec(
            num_scalar_prefetch=1,
            grid=(4,),
            in_specs=[
                QUERY_SPEC,
                pl.BlockSpec((2, 2, 2, HALF, HEAD_DIM), lambda i, *_: (0, 0, 0, 0, 0)),
                COUNT_SPEC,
                PART_SPEC,
                PART_SPEC,
            ],
            out_specs=pl.BlockSpec((2, 1, 2, ROWS, HEAD_DIM), lambda i, *_: (0, i, 0, 0, 0)),
            scratch_shapes=[pltpu.VMEM((4 * SPAN, 4 * HALF), F32)],
        ),
        out_shape=jax.ShapeDtypeStruct((2, 4, 2, ROWS, HEAD_DIM), BF16),
        name="attend_far",
    )(order, queries, beyond, counts, part, total)


def merge(parts):
    sums = [row_to_sums(p[SPAN : SPAN + 1, :].astype(F32)) for p in parts]
    total = functools.reduce(jnp.add, sums)
    mixed = functools.reduce(
        jnp.add, [p[:SPAN, :].astype(F32) * (s / total) for p, s in zip(parts, sums)]
    )
    return mixed, total


def mix_kernel(place_ref, parts_ref, w0_ref, w1_ref, w2_ref, w3_ref, out_ref, att_ref):
    @pl.when(pl.program_id(0) == 0)
    def _():
        for s in range(2):
            for c in range(2):
                mixed, _ = merge([parts_ref[s, z, c] for z in range(4)])
                att_ref[2 * s + c] = mixed.astype(BF16)

    place = place_ref[0]
    acc = None
    for k, ref in enumerate((w0_ref, w1_ref, w2_ref, w3_ref)):
        term = dot(att_ref[place ^ k], ref[...], ((1,), (1,)))
        acc = term if acc is None else acc + term
    for d in range(out_ref.shape[0]):
        out_ref[d] = acc[:, d * HEAD_DIM : (d + 1) * HEAD_DIM].astype(BF16)


def mix(place, parts, weights):
    step = 8
    weight = pl.BlockSpec((step * HEAD_DIM, HEAD_DIM), lambda i, *_: (i, 0))
    return pl.pallas_call(
        mix_kernel,
        grid_spec=pltpu.PrefetchScalarGridSpec(
            num_scalar_prefetch=1,
            grid=(32 // step,),
            in_specs=[
                pl.BlockSpec((2, 4, 2, ROWS, HEAD_DIM), lambda i, *_: (0, 0, 0, 0, 0)),
                weight,
                weight,
                weight,
                weight,
            ],
            out_specs=pl.BlockSpec((step, SPAN, HEAD_DIM), lambda i, *_: (i, 0, 0)),
            scratch_shapes=[pltpu.VMEM((4, SPAN, HEAD_DIM), BF16)],
        ),
        out_shape=jax.ShapeDtypeStruct((32, SPAN, HEAD_DIM), BF16),
        name="mix",
    )(place, parts, *weights)


def swap(value, axis):
    return lax.ppermute(value, axis, [(0, 1), (1, 0)])


def multiplicities(nb_ids, nb_index):
    place = nb_ids % SHARD
    place = jnp.where(place < HALF, place, place + (2 * HALF - SHARD))
    upper = (nb_ids // SHARD) * 32 + place // 32
    one_upper = (upper[:, :, None] == jnp.arange(512)).astype(BF16)
    one_lower = ((place % 32)[:, :, None] == jnp.arange(32)).astype(BF16)
    per_block = jnp.einsum("nip,niq->npq", one_upper, one_lower, preferred_element_type=F32)
    pick = jnp.sum((nb_index[:, :, None] == jnp.arange(8)).astype(F32), axis=1)
    counts = jnp.einsum(
        "gn,npq->gpq", pick.astype(BF16), per_block.astype(BF16), preferred_element_type=F32
    )
    return counts.astype(BF16)


def half_of(table, tokens, core):
    rows = lax.dynamic_slice_in_dim(table, core * (SHARD - HALF), HALF)
    return jnp.concatenate([rows, lax.dynamic_slice_in_dim(tokens, core * 128, 128)], axis=0)


def pairs(size, turn):
    out = []
    for place in range(size):
        for core in range(2):
            spot = (place - core) % size
            other = spot ^ 1 if turn == 0 else spot + (1 if spot % 2 else -1)
            out.append((2 * place + core, 2 * ((other + core) % size) + core))
    return out


def exchange(value, axis, size, turn):
    return lax.ppermute(value, (axis, "c"), pairs(size, turn))


def after(value, *others):
    return lax.optimization_barrier((value, *others))[0]


def feature_rows(projections, section):
    start = section * 2048
    encoder = lax.dynamic_slice(projections, (0, 0, start, 0), (1, 2, 2048, 128))
    decoder = lax.dynamic_slice(projections, (1, 0, start, 0), (1, 1, 2048, 128))
    return jnp.concatenate([encoder[0], decoder[0]], axis=0)


def step(tokens, nb_ids, nb_index, table, norm_gains, projections):
    core, section, here = lax.axis_index("c"), lax.axis_index("s"), lax.axis_index("y")
    column = lax.axis_index("x")

    own = half_of(table, tokens, core)
    got = swap(half_of(table, tokens, 1 - core), "c")
    across = swap(feature_rows(projections, 1 - section), "s")
    chunk = jnp.where(core == 0, jnp.stack([own, got]), jnp.stack([got, own]))
    first = exchange(chunk, "y", 8, 0)
    second = exchange(jnp.stack([chunk, first]), "y", 8, 1)
    mine = feature_rows(after(projections, first), section)
    beside = swap(mine, "c")

    gains = lax.dynamic_slice_in_dim(norm_gains, section * 2048, 2048, axis=1)
    gains = gains.reshape(2, 8, 2, 128).transpose(1, 2, 0, 3)
    counts = multiplicities(after(nb_ids, first), nb_index).reshape(2, 2, 4, 4 * 1024)
    counts = lax.dynamic_index_in_dim(counts, core, 0, keepdims=False)
    counts = counts.transpose(1, 0, 2).reshape(4, 64, 128)
    sign = 1 - 2 * ((here + core) % 2)
    offsets = after(jnp.array([0, 1, -1, -2, 2, 3, -3, -4], jnp.int32), first)
    source = jnp.concatenate([(here + sign * offsets) % 8, core.reshape(1)]).astype(jnp.int32)
    sign = 1 - 2 * ((column + core) % 2)
    origin = (column + sign * offsets[:4]) % 4
    order = (2 * origin[:, None] + jnp.stack([core, 1 - core])[None]).reshape(8).astype(jnp.int32)

    third = exchange(second, "y", 8, 0)
    third, gains, counts, source, order = lax.optimization_barrier(
        (third, gains, counts, source, order)
    )
    fourth = exchange(third, "y", 8, 1)
    diagonal = swap(after(across, third), "c")

    far = (across, diagonal)
    early, square, kv, query = project_early(source, (chunk, first, second, third), gains, far)
    late, squares, send = project_late(source, fourth, gains, far, square, kv, query)
    other = swap(send, "s")
    keep, keep_q = project_near(source, early, late, (mine, beside))
    near, give, queries = finish(source, keep, keep_q, squares, other, counts)
    queries = queries.reshape(8, 192, 128)
    queries = lax.all_to_all(queries, ("zh", "c"), 0, 0)
    near = jnp.stack([near, swap(give, "c")])
    following = exchange(near, "x", 4, 0)
    following = after(following, queries)
    beyond = exchange(jnp.stack([near, following]), "x", 4, 1)
    queries = queries.reshape(4, 2, 192, 128)
    counts = queries[:, :, 128:].reshape(4, 2, 2, 8, HALF).transpose(0, 3, 1, 2, 4)
    counts = counts.reshape(4, 8, 4, HALF)

    wo = after(projections[1, 1], first)
    wo_section = swap(after(wo, queries), "s")
    wo_beside = swap(wo, "c")
    wo_diagonal = swap(wo_section, "c")

    part, total = attend_near(order, queries, near, following, counts)
    parts = attend_far(order, queries, beyond, counts, part, total)
    parts = parts.reshape(16, ROWS, HEAD_DIM)
    parts = lax.all_to_all(parts, ("s", "zh", "c"), 0, 0)
    place = (section * 2 + core).astype(jnp.int32).reshape(1)
    weights = (wo, wo_beside, wo_section, wo_diagonal)
    out = mix(place, parts.reshape(2, 4, 2, ROWS, HEAD_DIM), weights)
    out = lax.all_to_all(out, ("s", "y", "c"), 0, 0)
    out = jnp.sum(out.reshape(2, 8, 2, SPAN, HEAD_DIM).astype(F32), axis=1)
    return out.astype(BF16).reshape(4 * SPAN, HEAD_DIM)


def solution(mesh):
    fine = Mesh(mesh.devices.reshape(2, 4, 4, 8, 2), ("s", "zh", "x", "y", "c"))
    batch, cols = ("zh", "x"), ("s", "y", "c")
    return jax.shard_map(
        step,
        mesh=fine,
        in_specs=(
            P(batch, cols),
            P(batch, None),
            P(batch, None),
            P(batch, cols),
            P(),
            P(None, None, None, cols),
        ),
        out_specs=P(batch, cols),
        check_vma=False,
    )
```

```python
import functools
import math

import jax
import jax.numpy as jnp
from jax import lax
from jax.experimental import pallas as pl
from jax.experimental.pallas import tpu as pltpu
from jax.sharding import Mesh
from jax.sharding import PartitionSpec as P

HEAD_DIM = 128
SPAN = 64
ROWS = 72
SHARD = 1000
HALF = 512
ROWS_IN = HALF + 128
EPS = 1e-06
SCALE = math.log2(math.e) / math.sqrt(HEAD_DIM)
F32 = jnp.float32
BF16 = jnp.bfloat16


def dot(a, b, dims):
    return lax.dot_general(a, b, (dims, ((), ())), preferred_element_type=F32)


def diagonal(shape):
    row = lax.broadcasted_iota(jnp.int32, shape, len(shape) - 2)
    lane = lax.broadcasted_iota(jnp.int32, shape, len(shape) - 1)
    return row == lane % SPAN


def sums_to_row(column):
    row = jnp.sum(jnp.where(diagonal((SPAN, 128)), column, 0.0), axis=0, keepdims=True)
    upper = row.astype(BF16).astype(F32)
    lane = lax.broadcasted_iota(jnp.int32, (1, 128), 1)
    return jnp.where(lane < SPAN, upper, row - upper)


def row_to_sums(row):
    return jnp.sum(jnp.where(diagonal((SPAN, 128)), row, 0.0), axis=1, keepdims=True)


def column_to_row(column):
    square = (128, 128)
    same = lax.broadcasted_iota(jnp.int32, square, 0) == lax.broadcasted_iota(jnp.int32, square, 1)
    return jnp.sum(jnp.where(same, column, 0.0), axis=0, keepdims=True)


def row_to_column(row):
    square = (128, 128)
    same = lax.broadcasted_iota(jnp.int32, square, 0) == lax.broadcasted_iota(jnp.int32, square, 1)
    return jnp.sum(jnp.where(same, row, 0.0), axis=1, keepdims=True)


def normed(ref, gain, lhs_ref, slot, square):
    for i in range(2):
        wide = ref[i].astype(F32)
        square = square + wide * wide
        lanes = slice(i * 128, (i + 1) * 128)
        lhs_ref[slot, :HALF, lanes] = (wide[:HALF] * gain[i, 0:1]).astype(BF16)
        lhs_ref[slot, HALF:, lanes] = (wide[HALF:] * gain[i, 1:2]).astype(BF16)
    return square


def columns(pieces):
    return jnp.concatenate(pieces, axis=1)


def rows_of(ref, which, source_ref, slots):
    picked = [
        ref[which, pl.ds(pl.multiple_of(source_ref[k] * 256, 256), 256), :] for k in slots
    ]
    return jnp.concatenate(picked, axis=0)


def early_kernel(source_ref, b0_ref, b1_ref, b2_ref, b3_ref, gain_ref, w0_ref, w1_ref, lhs_ref, square_ref, kv_ref, q_ref):
    square = jnp.zeros((ROWS_IN, 128), F32)
    pieces = [b0_ref, b1_ref, b2_ref.at[0], b2_ref.at[1], b3_ref.at[0], b3_ref.at[1]]
    for k, ref in enumerate(pieces):
        square = normed(ref, gain_ref[source_ref[k]], lhs_ref, k, square)
    square_ref[...] = square
    lhs = columns([lhs_ref[k] for k in range(6)])
    for m, ref in enumerate((w0_ref, w1_ref)):
        pair = columns([rows_of(ref, i, source_ref, range(6)) for i in range(2)])
        kv_ref[m] = dot(lhs[:HALF], pair, ((1,), (0,)))
        q_ref[m] = dot(lhs[HALF:], rows_of(ref, 2, source_ref, range(6)), ((1,), (0,)))


def project_early(source, blocks, gains, weights):
    vmem = pl.BlockSpec(memory_space=pltpu.VMEM)
    return pl.pallas_call(
        early_kernel,
        in_specs=[pl.BlockSpec(memory_space=pltpu.SMEM)] + [vmem] * 7,
        out_specs=[vmem] * 4,
        out_shape=[
            jax.ShapeDtypeStruct((6, ROWS_IN, 256), BF16),
            jax.ShapeDtypeStruct((ROWS_IN, 128), F32),
            jax.ShapeDtypeStruct((2, HALF, 256), F32),
            jax.ShapeDtypeStruct((2, 128, 128), F32),
        ],
        name="project_early",
    )(source, *blocks, gains, *weights)


def late_kernel(source_ref, b4_ref, gain_ref, w00_ref, w01_ref, w10_ref, w11_ref, square_ref, kv_ref, q_ref, lhs_ref, squares_ref, send_ref, send_q_ref):
    square = square_ref[...]
    for k in range(2):
        square = normed(b4_ref.at[k], gain_ref[source_ref[6 + k]], lhs_ref, k, square)
    sums = jnp.sum(square, axis=1, keepdims=True)
    tail = [column_to_row(sums[k * 128 : (k + 1) * 128]) for k in range(5)]
    squares = jnp.concatenate(tail + [jnp.zeros((3, 128), F32)], axis=0)
    squares_ref[...] = squares
    upper = squares.astype(BF16)
    lower = (squares - upper.astype(F32)).astype(BF16)
    send_q_ref[256:264] = upper
    send_q_ref[264:272] = lower
    lhs = columns([lhs_ref[k] for k in range(2)])
    for m, (one, two) in enumerate(((w00_ref, w01_ref), (w10_ref, w11_ref))):
        rows = [jnp.concatenate([one[i], two[i]], axis=0) for i in range(3)]
        both = kv_ref[m] + dot(lhs[:HALF], columns(rows[:2]), ((1,), (0,)))
        query = q_ref[m] + dot(lhs[HALF:], rows[2], ((1,), (0,)))
        send_q_ref[m * 128 : (m + 1) * 128] = query.astype(BF16)
        for i in range(2):
            send_ref[2 * m + i] = both[:, i * 128 : (i + 1) * 128].astype(BF16)


def whole_spec(*shape):
    return pl.BlockSpec(shape, lambda i, *_: (0,) * len(shape))


def project_late(source, block, gains, weights, square, kv, query):
    picked = [pl.BlockSpec((3, 256, 128), lambda i, s, k=k: (0, s[6 + k], 0)) for k in range(2)]
    return pl.pallas_call(
        late_kernel,
        grid_spec=pltpu.PrefetchScalarGridSpec(
            num_scalar_prefetch=1,
            grid=(1,),
            in_specs=[
                whole_spec(2, 2, ROWS_IN, 128),
                whole_spec(8, 2, 2, 128),
                *picked,
                *picked,
                whole_spec(ROWS_IN, 128),
                whole_spec(2, HALF, 256),
                whole_spec(2, 128, 128),
            ],
            out_specs=[
                whole_spec(2, ROWS_IN, 256),
                whole_spec(8, 128),
                whole_spec(4, HALF, 128),
                whole_spec(272, 128),
            ],
        ),
        out_shape=[
            jax.ShapeDtypeStruct((2, ROWS_IN, 256), BF16),
            jax.ShapeDtypeStruct((8, 128), F32),
            jax.ShapeDtypeStruct((4, HALF, 128), BF16),
            jax.ShapeDtypeStruct((272, 128), BF16),
        ],
        name="project_late",
    )(source, block, gains, weights[0], weights[0], weights[1], weights[1], square, kv, query)


def rate_of(squares_ref, other_ref):
    theirs = other_ref[256:264].astype(F32) + other_ref[264:272].astype(F32)
    return lax.rsqrt((squares_ref[...] + theirs) * (1.0 / 4096) + EPS)


def query_kernel(source_ref, early_ref, late_ref, w0_ref, w1_ref, squares_ref, other_ref, count_ref, q_ref):
    core = source_ref[8]
    column = row_to_column(rate_of(squares_ref, other_ref)[4:5])
    lhs = columns([early_ref[k] for k in range(6)] + [late_ref[k] for k in range(2)])
    for m, ref in enumerate((w0_ref, w1_ref)):
        near = dot(lhs, rows_of(ref, 0, source_ref, range(8)), ((1,), (0,)))
        total = near + other_ref[m * 128 : (m + 1) * 128].astype(F32)
        value = (total * column).astype(BF16)
        for z in range(4):
            q_ref[z, core ^ m, :128] = value
            q_ref[z, m, 128:] = count_ref[z]


def finish_queries(source, early, late, weights, squares, other, counts):
    last = lambda i, *_: (0, HALF // 128, 0)
    weight = pl.BlockSpec((1, 2048, 128), lambda i, *_: (2, 0, 0))
    return pl.pallas_call(
        query_kernel,
        grid_spec=pltpu.PrefetchScalarGridSpec(
            num_scalar_prefetch=1,
            grid=(1,),
            in_specs=[
                pl.BlockSpec((6, 128, 256), last),
                pl.BlockSpec((2, 128, 256), last),
                weight,
                weight,
                whole_spec(8, 128),
                whole_spec(272, 128),
                whole_spec(4, 64, 128),
            ],
            out_specs=whole_spec(4, 2, 192, 128),
        ),
        out_shape=jax.ShapeDtypeStruct((4, 2, 192, 128), BF16),
        name="finish_queries",
    )(source, early, late, *weights, squares, other, counts)


def near_kernel(source_ref, early_ref, late_ref, w0_ref, w1_ref, keep_ref):
    lhs = columns([early_ref[k] for k in range(6)] + [late_ref[k] for k in range(2)])
    for m, ref in enumerate((w0_ref, w1_ref)):
        pair = columns([rows_of(ref, i, source_ref, range(8)) for i in range(2)])
        both = dot(lhs, pair, ((1,), (0,)))
        keep_ref[m, 0] = both[:, :128]
        keep_ref[m, 1] = both[:, 128:]


def project_near(source, early, late, weights):
    return pl.pallas_call(
        near_kernel,
        grid_spec=pltpu.PrefetchScalarGridSpec(
            num_scalar_prefetch=1,
            grid=(1,),
            in_specs=[
                whole_spec(6, HALF, 256),
                whole_spec(2, HALF, 256),
                whole_spec(2, 2048, 128),
                whole_spec(2, 2048, 128),
            ],
            out_specs=whole_spec(2, 2, HALF, 128),
        ),
        out_shape=jax.ShapeDtypeStruct((2, 2, HALF, 128), F32),
        name="project_near",
    )(source, early, late, *weights)


def finish_kernel(keep_ref, squares_ref, other_q_ref, other_ref, own_ref, give_ref):
    rate = rate_of(squares_ref, other_q_ref)
    for k in range(4):
        rows = slice(k * 128, (k + 1) * 128)
        column = row_to_column(rate[k : k + 1])
        for m, ref in enumerate((own_ref, give_ref)):
            for i in range(2):
                total = keep_ref[m, i, rows] + other_ref[2 * m + i, rows, :].astype(F32)
                ref[i, rows] = (total * column).astype(BF16)


def finish(keep, squares, other_q, other):
    vmem = pl.BlockSpec(memory_space=pltpu.VMEM)
    half = jax.ShapeDtypeStruct((2, HALF, 128), BF16)
    return pl.pallas_call(
        finish_kernel,
        in_specs=[vmem] * 4,
        out_specs=[vmem] * 2,
        out_shape=[half, half],
        name="finish",
    )(keep, squares, other_q, other)


def partial(order_ref, first, queries, blocks, count_ref, expo_ref):
    total = jnp.zeros((4 * SPAN, 128), F32)
    for k, block in enumerate(blocks):
        lanes = slice(k * HALF, (k + 1) * HALF)
        bias = jnp.log2(count_ref[0, order_ref[first + k]].astype(F32))
        spread = jnp.broadcast_to(bias[:, None, :], (4, SPAN, HALF)).reshape(4 * SPAN, HALF)
        scores = dot(queries, block[0], ((1,), (1,)))
        expo = jnp.exp2(scores * SCALE + spread)
        expo_ref[:, lanes] = expo
        for i in range(HALF // 128):
            total = total + expo[:, i * 128 : (i + 1) * 128]
    total = jnp.sum(total, axis=1, keepdims=True)
    inverse = jnp.where(total > 0.0, 1.0 / total, 0.0)
    weights = (expo_ref[...] * inverse).astype(BF16)
    values = jnp.concatenate([block[1] for block in blocks], axis=0)
    return dot(weights, values, ((1,), (0,))), total


def near_attend_kernel(order_ref, q_ref, near_ref, next_ref, count_ref, part_ref, total_ref, expo_ref):
    queries = jnp.concatenate([q_ref[0, 0], q_ref[0, 1]], axis=0)
    blocks = [near_ref.at[0], near_ref.at[1], next_ref.at[0], next_ref.at[1]]
    part, total = partial(order_ref, 0, queries, blocks, count_ref, expo_ref)
    part_ref[...] = part
    total_ref[...] = jnp.broadcast_to(total, (4 * SPAN, 128))


def far_attend_kernel(order_ref, q_ref, far_ref, count_ref, part_ref, total_ref, out_ref, expo_ref):
    queries = jnp.concatenate([q_ref[0, 0], q_ref[0, 1]], axis=0)
    blocks = [far_ref.at[k, i] for k in range(2) for i in range(2)]
    part, total = partial(order_ref, 4, queries, blocks, count_ref, expo_ref)
    before = total_ref[:, 0:1]
    both = total + before
    inverse = jnp.where(both > 0.0, 1.0 / both, 0.0)
    part = (part * (total * inverse) + part_ref[...] * (before * inverse)).astype(BF16)
    for j in range(4):
        rows = slice(j * SPAN, (j + 1) * SPAN)
        out_ref[j // 2, 0, j % 2, :SPAN, :] = part[rows]
        tail = jnp.broadcast_to(sums_to_row(both[rows]), (ROWS - SPAN, 128))
        out_ref[j // 2, 0, j % 2, SPAN:, :] = tail.astype(BF16)


QUERY_SPEC = pl.BlockSpec((1, 2, 128, HEAD_DIM), lambda i, *_: (i, 0, 0, 0))
COUNT_SPEC = pl.BlockSpec((1, 8, 4, HALF), lambda i, *_: (i, 0, 0, 0))
PART_SPEC = pl.BlockSpec((4 * SPAN, HEAD_DIM), lambda i, *_: (i, 0))


def attend_near(order, queries, near, following, counts):
    block = pl.BlockSpec((2, 2, HALF, HEAD_DIM), lambda i, *_: (0, 0, 0, 0))
    return pl.pallas_call(
        near_attend_kernel,
        grid_spec=pltpu.PrefetchScalarGridSpec(
            num_scalar_prefetch=1,
            grid=(4,),
            in_specs=[QUERY_SPEC, block, block, COUNT_SPEC],
            out_specs=[PART_SPEC, PART_SPEC],
            scratch_shapes=[pltpu.VMEM((4 * SPAN, 4 * HALF), F32)],
        ),
        out_shape=[jax.ShapeDtypeStruct((16 * SPAN, HEAD_DIM), F32)] * 2,
        name="attend_near",
    )(order, queries, near, following, counts)


def attend_far(order, queries, beyond, counts, part, total):
    return pl.pallas_call(
        far_attend_kernel,
        grid_spec=pltpu.PrefetchScalarGridSpec(
            num_scalar_prefetch=1,
            grid=(4,),
            in_specs=[
                QUERY_SPEC,
                pl.BlockSpec((2, 2, 2, HALF, HEAD_DIM), lambda i, *_: (0, 0, 0, 0, 0)),
                COUNT_SPEC,
                PART_SPEC,
                PART_SPEC,
            ],
            out_specs=pl.BlockSpec((2, 1, 2, ROWS, HEAD_DIM), lambda i, *_: (0, i, 0, 0, 0)),
            scratch_shapes=[pltpu.VMEM((4 * SPAN, 4 * HALF), F32)],
        ),
        out_shape=jax.ShapeDtypeStruct((2, 4, 2, ROWS, HEAD_DIM), BF16),
        name="attend_far",
    )(order, queries, beyond, counts, part, total)


def merge(parts):
    sums = [row_to_sums(p[SPAN : SPAN + 1, :].astype(F32)) for p in parts]
    total = functools.reduce(jnp.add, sums)
    mixed = functools.reduce(
        jnp.add, [p[:SPAN, :].astype(F32) * (s / total) for p, s in zip(parts, sums)]
    )
    return mixed, total


def mix_kernel(place_ref, parts_ref, w0_ref, w1_ref, w2_ref, w3_ref, out_ref, att_ref):
    @pl.when(pl.program_id(0) == 0)
    def _():
        for s in range(2):
            for c in range(2):
                mixed, _ = merge([parts_ref[s, z, c] for z in range(4)])
                att_ref[2 * s + c] = mixed.astype(BF16)

    place = place_ref[0]
    acc = None
    for k, ref in enumerate((w0_ref, w1_ref, w2_ref, w3_ref)):
        term = dot(att_ref[place ^ k], ref[...], ((1,), (1,)))
        acc = term if acc is None else acc + term
    for d in range(out_ref.shape[0]):
        out_ref[d] = acc[:, d * HEAD_DIM : (d + 1) * HEAD_DIM].astype(BF16)


def mix(place, parts, weights):
    step = 8
    weight = pl.BlockSpec((step * HEAD_DIM, HEAD_DIM), lambda i, *_: (i, 0))
    return pl.pallas_call(
        mix_kernel,
        grid_spec=pltpu.PrefetchScalarGridSpec(
            num_scalar_prefetch=1,
            grid=(32 // step,),
            in_specs=[
                pl.BlockSpec((2, 4, 2, ROWS, HEAD_DIM), lambda i, *_: (0, 0, 0, 0, 0)),
                weight,
                weight,
                weight,
                weight,
            ],
            out_specs=pl.BlockSpec((step, SPAN, HEAD_DIM), lambda i, *_: (i, 0, 0)),
            scratch_shapes=[pltpu.VMEM((4, SPAN, HEAD_DIM), BF16)],
        ),
        out_shape=jax.ShapeDtypeStruct((32, SPAN, HEAD_DIM), BF16),
        name="mix",
    )(place, parts, *weights)


def swap(value, axis):
    return lax.ppermute(value, axis, [(0, 1), (1, 0)])


def multiplicities(nb_ids, nb_index):
    place = nb_ids % SHARD
    place = jnp.where(place < HALF, place, place + (2 * HALF - SHARD))
    upper = (nb_ids // SHARD) * 32 + place // 32
    one_upper = (upper[:, :, None] == jnp.arange(512)).astype(BF16)
    one_lower = ((place % 32)[:, :, None] == jnp.arange(32)).astype(BF16)
    per_block = jnp.einsum("nip,niq->npq", one_upper, one_lower, preferred_element_type=F32)
    pick = jnp.sum((nb_index[:, :, None] == jnp.arange(8)).astype(F32), axis=1)
    counts = jnp.einsum(
        "gn,npq->gpq", pick.astype(BF16), per_block.astype(BF16), preferred_element_type=F32
    )
    return counts.astype(BF16)


def half_of(table, tokens, core):
    rows = lax.dynamic_slice_in_dim(table, core * (SHARD - HALF), HALF)
    return jnp.concatenate([rows, lax.dynamic_slice_in_dim(tokens, core * 128, 128)], axis=0)


def pairs(size, turn):
    out = []
    for place in range(size):
        for core in range(2):
            spot = (place - core) % size
            other = spot ^ 1 if turn == 0 else spot + (1 if spot % 2 else -1)
            out.append((2 * place + core, 2 * ((other + core) % size) + core))
    return out


def exchange(value, axis, size, turn):
    return lax.ppermute(value, (axis, "c"), pairs(size, turn))


def after(value, *others):
    return lax.optimization_barrier((value, *others))[0]


def feature_rows(projections, section):
    start = section * 2048
    encoder = lax.dynamic_slice(projections, (0, 0, start, 0), (1, 2, 2048, 128))
    decoder = lax.dynamic_slice(projections, (1, 0, start, 0), (1, 1, 2048, 128))
    return jnp.concatenate([encoder[0], decoder[0]], axis=0)


def step(tokens, nb_ids, nb_index, table, norm_gains, projections):
    core, section, here = lax.axis_index("c"), lax.axis_index("s"), lax.axis_index("y")
    column = lax.axis_index("x")

    own = half_of(table, tokens, core)
    got = swap(half_of(table, tokens, 1 - core), "c")
    away = feature_rows(after(projections, got), 1 - section)
    across = swap(away, "s")
    chunk = jnp.where(core == 0, jnp.stack([own, got]), jnp.stack([got, own]))
    first = exchange(chunk, "y", 8, 0)
    second = exchange(jnp.stack([chunk, first]), "y", 8, 1)
    later = after(projections, first)
    wo = later[1, 1]
    wo_section = swap(wo, "s")
    wo_beside = swap(wo, "c")
    mine = feature_rows(later, section)
    beside = swap(mine, "c")

    gains = lax.dynamic_slice_in_dim(norm_gains, section * 2048, 2048, axis=1)
    gains = gains.reshape(2, 8, 2, 128).transpose(1, 2, 0, 3)
    counts = multiplicities(after(nb_ids, first), nb_index).reshape(2, 2, 4, 4 * 1024)
    counts = lax.dynamic_index_in_dim(counts, core, 0, keepdims=False)
    counts = counts.transpose(1, 0, 2).reshape(4, 64, 128)
    sign = 1 - 2 * ((here + core) % 2)
    offsets = after(jnp.array([0, 1, -1, -2, 2, 3, -3, -4], jnp.int32), first)
    source = jnp.concatenate([(here + sign * offsets) % 8, core.reshape(1)]).astype(jnp.int32)
    sign = 1 - 2 * ((column + core) % 2)
    origin = (column + sign * offsets[:4]) % 4
    order = (2 * origin[:, None] + jnp.stack([core, 1 - core])[None]).reshape(8).astype(jnp.int32)

    third = exchange(second, "y", 8, 0)
    third, gains, counts, source, order = lax.optimization_barrier(
        (third, gains, counts, source, order)
    )
    fourth = exchange(third, "y", 8, 1)
    diagonal = swap(after(across, third), "c")

    far = (across, diagonal)
    early, square, kv, query = project_early(source, (chunk, first, second, third), gains, far)
    late, squares, send, send_q = project_late(source, fourth, gains, far, square, kv, query)
    other_q = swap(send_q, "s")
    other = swap(send, "s")
    beside = (mine, beside)
    queries = finish_queries(source, early, late, beside, squares, other_q, counts)
    queries = queries.reshape(8, 192, 128)
    queries = lax.all_to_all(queries, ("zh", "c"), 0, 0)
    keep = project_near(source, early, late, beside)
    near, give = finish(keep, squares, other_q, other)
    wo_diagonal = swap(wo_section, "c")
    near = jnp.stack([near, swap(give, "c")])
    following = exchange(near, "x", 4, 0)
    beyond = exchange(jnp.stack([near, following]), "x", 4, 1)
    queries = queries.reshape(4, 2, 192, 128)
    counts = queries[:, :, 128:].reshape(4, 2, 2, 8, HALF).transpose(0, 3, 1, 2, 4)
    counts = counts.reshape(4, 8, 4, HALF)

    part, total = attend_near(order, queries, near, following, counts)
    parts = attend_far(order, queries, beyond, counts, part, total)
    parts = parts.reshape(16, ROWS, HEAD_DIM)
    parts = lax.all_to_all(parts, ("s", "zh", "c"), 0, 0)
    place = (section * 2 + core).astype(jnp.int32).reshape(1)
    weights = (wo, wo_beside, wo_section, wo_diagonal)
    out = mix(place, parts.reshape(2, 4, 2, ROWS, HEAD_DIM), weights)
    out = lax.all_to_all(out, ("s", "y", "c"), 0, 0)
    out = jnp.sum(out.reshape(2, 8, 2, SPAN, HEAD_DIM).astype(F32), axis=1)
    return out.astype(BF16).reshape(4 * SPAN, HEAD_DIM)


def solution(mesh):
    fine = Mesh(mesh.devices.reshape(2, 4, 4, 8, 2), ("s", "zh", "x", "y", "c"))
    batch, cols = ("zh", "x"), ("s", "y", "c")
    return jax.shard_map(
        step,
        mesh=fine,
        in_specs=(
            P(batch, cols),
            P(batch, None),
            P(batch, None),
            P(batch, cols),
            P(),
            P(None, None, None, cols),
        ),
        out_specs=P(batch, cols),
        check_vma=False,
    )
```

```python
import functools
import math

import jax
import jax.numpy as jnp
from jax import lax
from jax.experimental import pallas as pl
from jax.experimental.pallas import tpu as pltpu
from jax.sharding import Mesh
from jax.sharding import PartitionSpec as P

HEAD_DIM = 128
SPAN = 64
ROWS = 72
SHARD = 1000
HALF = 512
ROWS_IN = HALF + 128
EPS = 1e-06
SCALE = math.log2(math.e) / math.sqrt(HEAD_DIM)
F32 = jnp.float32
BF16 = jnp.bfloat16


def dot(a, b, dims):
    return lax.dot_general(a, b, (dims, ((), ())), preferred_element_type=F32)


def diagonal(shape):
    row = lax.broadcasted_iota(jnp.int32, shape, len(shape) - 2)
    lane = lax.broadcasted_iota(jnp.int32, shape, len(shape) - 1)
    return row == lane % SPAN


def sums_to_row(column):
    row = jnp.sum(jnp.where(diagonal((SPAN, 128)), column, 0.0), axis=0, keepdims=True)
    upper = row.astype(BF16).astype(F32)
    lane = lax.broadcasted_iota(jnp.int32, (1, 128), 1)
    return jnp.where(lane < SPAN, upper, row - upper)


def row_to_sums(row):
    return jnp.sum(jnp.where(diagonal((SPAN, 128)), row, 0.0), axis=1, keepdims=True)


def column_to_row(column):
    square = (128, 128)
    same = lax.broadcasted_iota(jnp.int32, square, 0) == lax.broadcasted_iota(jnp.int32, square, 1)
    return jnp.sum(jnp.where(same, column, 0.0), axis=0, keepdims=True)


def row_to_column(row):
    square = (128, 128)
    same = lax.broadcasted_iota(jnp.int32, square, 0) == lax.broadcasted_iota(jnp.int32, square, 1)
    return jnp.sum(jnp.where(same, row, 0.0), axis=1, keepdims=True)


def normed(ref, gain, lhs_ref, slot, square):
    for i in range(2):
        wide = ref[i].astype(F32)
        square = square + wide * wide
        lanes = slice(i * 128, (i + 1) * 128)
        lhs_ref[slot, :HALF, lanes] = (wide[:HALF] * gain[i, 0:1]).astype(BF16)
        lhs_ref[slot, HALF:, lanes] = (wide[HALF:] * gain[i, 1:2]).astype(BF16)
    return square


def columns(pieces):
    return jnp.concatenate(pieces, axis=1)


def rows_of(ref, which, source_ref, slots):
    picked = [
        ref[which, pl.ds(pl.multiple_of(source_ref[k] * 256, 256), 256), :] for k in slots
    ]
    return jnp.concatenate(picked, axis=0)


def early_kernel(source_ref, b0_ref, b1_ref, b2_ref, b3_ref, gain_ref, w0_ref, w1_ref, lhs_ref, square_ref, kv_ref, q_ref):
    square = jnp.zeros((ROWS_IN, 128), F32)
    pieces = [b0_ref, b1_ref, b2_ref.at[0], b2_ref.at[1], b3_ref.at[0], b3_ref.at[1]]
    for k, ref in enumerate(pieces):
        square = normed(ref, gain_ref[source_ref[k]], lhs_ref, k, square)
    square_ref[...] = square
    lhs = columns([lhs_ref[k] for k in range(6)])
    for m, ref in enumerate((w0_ref, w1_ref)):
        pair = columns([rows_of(ref, i, source_ref, range(6)) for i in range(2)])
        kv_ref[m] = dot(lhs[:HALF], pair, ((1,), (0,)))
        q_ref[m] = dot(lhs[HALF:], rows_of(ref, 2, source_ref, range(6)), ((1,), (0,)))


def project_early(source, blocks, gains, weights):
    vmem = pl.BlockSpec(memory_space=pltpu.VMEM)
    return pl.pallas_call(
        early_kernel,
        in_specs=[pl.BlockSpec(memory_space=pltpu.SMEM)] + [vmem] * 7,
        out_specs=[vmem] * 4,
        out_shape=[
            jax.ShapeDtypeStruct((6, ROWS_IN, 256), BF16),
            jax.ShapeDtypeStruct((ROWS_IN, 128), F32),
            jax.ShapeDtypeStruct((2, HALF, 256), F32),
            jax.ShapeDtypeStruct((2, 128, 128), F32),
        ],
        name="project_early",
    )(source, *blocks, gains, *weights)


def late_kernel(source_ref, b4_ref, gain_ref, early_ref, w0_ref, w1_ref, square_ref, lhs_ref, squares_ref, send_ref, send_q_ref):
    square = square_ref[...]
    for k in range(2):
        square = normed(b4_ref.at[k], gain_ref[source_ref[6 + k]], lhs_ref, k, square)
    sums = jnp.sum(square, axis=1, keepdims=True)
    tail = [column_to_row(sums[k * 128 : (k + 1) * 128]) for k in range(5)]
    squares = jnp.concatenate(tail + [jnp.zeros((3, 128), F32)], axis=0)
    squares_ref[...] = squares
    upper = squares.astype(BF16)
    send_q_ref[256:264] = upper
    send_q_ref[264:272] = (squares - upper.astype(F32)).astype(BF16)
    lhs = columns([early_ref[k] for k in range(6)] + [lhs_ref[k] for k in range(2)])
    for m, ref in enumerate((w0_ref, w1_ref)):
        pair = columns([rows_of(ref, i, source_ref, range(8)) for i in range(2)])
        both = dot(lhs[:HALF], pair, ((1,), (0,)))
        query = dot(lhs[HALF:], rows_of(ref, 2, source_ref, range(8)), ((1,), (0,)))
        send_q_ref[m * 128 : (m + 1) * 128] = query.astype(BF16)
        for i in range(2):
            send_ref[2 * m + i] = both[:, i * 128 : (i + 1) * 128].astype(BF16)


def whole_spec(*shape):
    return pl.BlockSpec(shape, lambda i, *_: (0,) * len(shape))


def picked_specs(depth, first):
    return [
        pl.BlockSpec((depth, 256, 128), lambda i, s, k=k: (first, s[6 + k], 0)) for k in range(2)
    ]


def project_late(source, block, gains, early, weights, square):
    return pl.pallas_call(
        late_kernel,
        grid_spec=pltpu.PrefetchScalarGridSpec(
            num_scalar_prefetch=1,
            grid=(1,),
            in_specs=[
                whole_spec(2, 2, ROWS_IN, 128),
                whole_spec(8, 2, 2, 128),
                whole_spec(6, ROWS_IN, 256),
                whole_spec(3, 2048, 128),
                whole_spec(3, 2048, 128),
                whole_spec(ROWS_IN, 128),
            ],
            out_specs=[
                whole_spec(2, ROWS_IN, 256),
                whole_spec(8, 128),
                whole_spec(4, HALF, 128),
                whole_spec(272, 128),
            ],
        ),
        out_shape=[
            jax.ShapeDtypeStruct((2, ROWS_IN, 256), BF16),
            jax.ShapeDtypeStruct((8, 128), F32),
            jax.ShapeDtypeStruct((4, HALF, 128), BF16),
            jax.ShapeDtypeStruct((272, 128), BF16),
        ],
        name="project_late",
    )(source, block, gains, early, *weights, square)


def rate_of(squares_ref, other_ref):
    theirs = other_ref[256:264].astype(F32) + other_ref[264:272].astype(F32)
    return lax.rsqrt((squares_ref[...] + theirs) * (1.0 / 4096) + EPS)


def query_kernel(source_ref, late_ref, w00_ref, w01_ref, w10_ref, w11_ref, near_ref, squares_ref, other_ref, count_ref, q_ref):
    core = source_ref[8]
    column = row_to_column(rate_of(squares_ref, other_ref)[4:5])
    lhs = columns([late_ref[k] for k in range(2)])
    for m, (one, two) in enumerate(((w00_ref, w01_ref), (w10_ref, w11_ref))):
        rows = jnp.concatenate([one[0], two[0]], axis=0)
        near = near_ref[m] + dot(lhs, rows, ((1,), (0,)))
        total = near + other_ref[m * 128 : (m + 1) * 128].astype(F32)
        value = (total * column).astype(BF16)
        for z in range(4):
            q_ref[z, core ^ m, :128] = value
            q_ref[z, m, 128:] = count_ref[z]


def finish_queries(source, late, weights, near, squares, other, counts):
    picked = picked_specs(1, 2)
    return pl.pallas_call(
        query_kernel,
        grid_spec=pltpu.PrefetchScalarGridSpec(
            num_scalar_prefetch=1,
            grid=(1,),
            in_specs=[
                pl.BlockSpec((2, 128, 256), lambda i, *_: (0, HALF // 128, 0)),
                *picked,
                *picked,
                whole_spec(2, 128, 128),
                whole_spec(8, 128),
                whole_spec(272, 128),
                whole_spec(4, 64, 128),
            ],
            out_specs=whole_spec(4, 2, 192, 128),
        ),
        out_shape=jax.ShapeDtypeStruct((4, 2, 192, 128), BF16),
        name="finish_queries",
    )(source, late, weights[0], weights[0], weights[1], weights[1], near, squares, other, counts)


def near_kernel(source_ref, late_ref, w00_ref, w01_ref, w10_ref, w11_ref, kv_ref, keep_ref):
    lhs = columns([late_ref[k] for k in range(2)])
    for m, (one, two) in enumerate(((w00_ref, w01_ref), (w10_ref, w11_ref))):
        rows = [jnp.concatenate([one[i], two[i]], axis=0) for i in range(2)]
        both = kv_ref[m] + dot(lhs, columns(rows), ((1,), (0,)))
        keep_ref[m, 0] = both[:, :128]
        keep_ref[m, 1] = both[:, 128:]


def project_near(source, late, weights, kv):
    picked = picked_specs(2, 0)
    return pl.pallas_call(
        near_kernel,
        grid_spec=pltpu.PrefetchScalarGridSpec(
            num_scalar_prefetch=1,
            grid=(1,),
            in_specs=[whole_spec(2, HALF, 256), *picked, *picked, whole_spec(2, HALF, 256)],
            out_specs=whole_spec(2, 2, HALF, 128),
        ),
        out_shape=jax.ShapeDtypeStruct((2, 2, HALF, 128), F32),
        name="project_near",
    )(source, late, weights[0], weights[0], weights[1], weights[1], kv)


def finish_kernel(keep_ref, squares_ref, other_q_ref, other_ref, own_ref, give_ref):
    rate = rate_of(squares_ref, other_q_ref)
    for k in range(4):
        rows = slice(k * 128, (k + 1) * 128)
        column = row_to_column(rate[k : k + 1])
        for m, ref in enumerate((own_ref, give_ref)):
            for i in range(2):
                total = keep_ref[m, i, rows] + other_ref[2 * m + i, rows, :].astype(F32)
                ref[i, rows] = (total * column).astype(BF16)


def finish(keep, squares, other_q, other):
    vmem = pl.BlockSpec(memory_space=pltpu.VMEM)
    half = jax.ShapeDtypeStruct((2, HALF, 128), BF16)
    return pl.pallas_call(
        finish_kernel,
        in_specs=[vmem] * 4,
        out_specs=[vmem] * 2,
        out_shape=[half, half],
        name="finish",
    )(keep, squares, other_q, other)


def partial(order_ref, first, queries, blocks, count_ref, expo_ref):
    total = jnp.zeros((4 * SPAN, 128), F32)
    for k, block in enumerate(blocks):
        lanes = slice(k * HALF, (k + 1) * HALF)
        bias = jnp.log2(count_ref[0, order_ref[first + k]].astype(F32))
        spread = jnp.broadcast_to(bias[:, None, :], (4, SPAN, HALF)).reshape(4 * SPAN, HALF)
        scores = dot(queries, block[0], ((1,), (1,)))
        expo = jnp.exp2(scores * SCALE + spread)
        expo_ref[:, lanes] = expo
        for i in range(HALF // 128):
            total = total + expo[:, i * 128 : (i + 1) * 128]
    total = jnp.sum(total, axis=1, keepdims=True)
    inverse = jnp.where(total > 0.0, 1.0 / total, 0.0)
    weights = (expo_ref[...] * inverse).astype(BF16)
    values = jnp.concatenate([block[1] for block in blocks], axis=0)
    return dot(weights, values, ((1,), (0,))), total


def near_attend_kernel(order_ref, q_ref, near_ref, next_ref, count_ref, part_ref, total_ref, expo_ref):
    queries = jnp.concatenate([q_ref[0, 0], q_ref[0, 1]], axis=0)
    blocks = [near_ref.at[0], near_ref.at[1], next_ref.at[0], next_ref.at[1]]
    part, total = partial(order_ref, 0, queries, blocks, count_ref, expo_ref)
    part_ref[...] = part
    total_ref[...] = jnp.broadcast_to(total, (4 * SPAN, 128))


def far_attend_kernel(order_ref, q_ref, far_ref, count_ref, part_ref, total_ref, out_ref, expo_ref):
    queries = jnp.concatenate([q_ref[0, 0], q_ref[0, 1]], axis=0)
    blocks = [far_ref.at[k, i] for k in range(2) for i in range(2)]
    part, total = partial(order_ref, 4, queries, blocks, count_ref, expo_ref)
    before = total_ref[:, 0:1]
    both = total + before
    inverse = jnp.where(both > 0.0, 1.0 / both, 0.0)
    part = (part * (total * inverse) + part_ref[...] * (before * inverse)).astype(BF16)
    for j in range(4):
        rows = slice(j * SPAN, (j + 1) * SPAN)
        out_ref[j // 2, 0, j % 2, :SPAN, :] = part[rows]
        tail = jnp.broadcast_to(sums_to_row(both[rows]), (ROWS - SPAN, 128))
        out_ref[j // 2, 0, j % 2, SPAN:, :] = tail.astype(BF16)


QUERY_SPEC = pl.BlockSpec((1, 2, 128, HEAD_DIM), lambda i, *_: (i, 0, 0, 0))
COUNT_SPEC = pl.BlockSpec((1, 8, 4, HALF), lambda i, *_: (i, 0, 0, 0))
PART_SPEC = pl.BlockSpec((4 * SPAN, HEAD_DIM), lambda i, *_: (i, 0))


def attend_near(order, queries, near, following, counts):
    block = pl.BlockSpec((2, 2, HALF, HEAD_DIM), lambda i, *_: (0, 0, 0, 0))
    return pl.pallas_call(
        near_attend_kernel,
        grid_spec=pltpu.PrefetchScalarGridSpec(
            num_scalar_prefetch=1,
            grid=(4,),
            in_specs=[QUERY_SPEC, block, block, COUNT_SPEC],
            out_specs=[PART_SPEC, PART_SPEC],
            scratch_shapes=[pltpu.VMEM((4 * SPAN, 4 * HALF), F32)],
        ),
        out_shape=[jax.ShapeDtypeStruct((16 * SPAN, HEAD_DIM), F32)] * 2,
        name="attend_near",
    )(order, queries, near, following, counts)


def attend_far(order, queries, beyond, counts, part, total):
    return pl.pallas_call(
        far_attend_kernel,
        grid_spec=pltpu.PrefetchScalarGridSpec(
            num_scalar_prefetch=1,
            grid=(4,),
            in_specs=[
                QUERY_SPEC,
                pl.BlockSpec((2, 2, 2, HALF, HEAD_DIM), lambda i, *_: (0, 0, 0, 0, 0)),
                COUNT_SPEC,
                PART_SPEC,
                PART_SPEC,
            ],
            out_specs=pl.BlockSpec((2, 1, 2, ROWS, HEAD_DIM), lambda i, *_: (0, i, 0, 0, 0)),
            scratch_shapes=[pltpu.VMEM((4 * SPAN, 4 * HALF), F32)],
        ),
        out_shape=jax.ShapeDtypeStruct((2, 4, 2, ROWS, HEAD_DIM), BF16),
        name="attend_far",
    )(order, queries, beyond, counts, part, total)


def merge(parts):
    sums = [row_to_sums(p[SPAN : SPAN + 1, :].astype(F32)) for p in parts]
    total = functools.reduce(jnp.add, sums)
    mixed = functools.reduce(
        jnp.add, [p[:SPAN, :].astype(F32) * (s / total) for p, s in zip(parts, sums)]
    )
    return mixed, total


def mix_kernel(place_ref, parts_ref, w0_ref, w1_ref, w2_ref, w3_ref, out_ref, att_ref):
    @pl.when(pl.program_id(0) == 0)
    def _():
        for s in range(2):
            for c in range(2):
                mixed, _ = merge([parts_ref[s, z, c] for z in range(4)])
                att_ref[2 * s + c] = mixed.astype(BF16)

    place = place_ref[0]
    acc = None
    for k, ref in enumerate((w0_ref, w1_ref, w2_ref, w3_ref)):
        term = dot(att_ref[place ^ k], ref[...], ((1,), (1,)))
        acc = term if acc is None else acc + term
    for d in range(out_ref.shape[0]):
        out_ref[d] = acc[:, d * HEAD_DIM : (d + 1) * HEAD_DIM].astype(BF16)


def mix(place, parts, weights):
    step = 8
    weight = pl.BlockSpec((step * HEAD_DIM, HEAD_DIM), lambda i, *_: (i, 0))
    return pl.pallas_call(
        mix_kernel,
        grid_spec=pltpu.PrefetchScalarGridSpec(
            num_scalar_prefetch=1,
            grid=(32 // step,),
            in_specs=[
                pl.BlockSpec((2, 4, 2, ROWS, HEAD_DIM), lambda i, *_: (0, 0, 0, 0, 0)),
                weight,
                weight,
                weight,
                weight,
            ],
            out_specs=pl.BlockSpec((step, SPAN, HEAD_DIM), lambda i, *_: (i, 0, 0)),
            scratch_shapes=[pltpu.VMEM((4, SPAN, HEAD_DIM), BF16)],
        ),
        out_shape=jax.ShapeDtypeStruct((32, SPAN, HEAD_DIM), BF16),
        name="mix",
    )(place, parts, *weights)


def swap(value, axis):
    return lax.ppermute(value, axis, [(0, 1), (1, 0)])


def multiplicities(nb_ids, nb_index):
    place = nb_ids % SHARD
    place = jnp.where(place < HALF, place, place + (2 * HALF - SHARD))
    upper = (nb_ids // SHARD) * 32 + place // 32
    one_upper = (upper[:, :, None] == jnp.arange(512)).astype(BF16)
    one_lower = ((place % 32)[:, :, None] == jnp.arange(32)).astype(BF16)
    per_block = jnp.einsum("nip,niq->npq", one_upper, one_lower, preferred_element_type=F32)
    pick = jnp.sum((nb_index[:, :, None] == jnp.arange(8)).astype(F32), axis=1)
    counts = jnp.einsum(
        "gn,npq->gpq", pick.astype(BF16), per_block.astype(BF16), preferred_element_type=F32
    )
    return counts.astype(BF16)


def half_of(table, tokens, core):
    rows = lax.dynamic_slice_in_dim(table, core * (SHARD - HALF), HALF)
    return jnp.concatenate([rows, lax.dynamic_slice_in_dim(tokens, core * 128, 128)], axis=0)


def pairs(size, turn):
    out = []
    for place in range(size):
        for core in range(2):
            spot = (place - core) % size
            other = spot ^ 1 if turn == 0 else spot + (1 if spot % 2 else -1)
            out.append((2 * place + core, 2 * ((other + core) % size) + core))
    return out


def exchange(value, axis, size, turn):
    return lax.ppermute(value, (axis, "c"), pairs(size, turn))


def after(value, *others):
    return lax.optimization_barrier((value, *others))[0]


def feature_rows(projections, section):
    start = section * 2048
    encoder = lax.dynamic_slice(projections, (0, 0, start, 0), (1, 2, 2048, 128))
    decoder = lax.dynamic_slice(projections, (1, 0, start, 0), (1, 1, 2048, 128))
    return jnp.concatenate([encoder[0], decoder[0]], axis=0)


def block_order(column, core):
    sign = 1 - 2 * ((column + core) % 2)
    offsets = jnp.array([0, 0, 1, 1, -1, -1, -2, -2], jnp.int32)
    origin = (column + sign * offsets) % 4
    half = (core + jnp.arange(8)) % 2
    return (2 * origin + half).astype(jnp.int32)


def step(tokens, nb_ids, nb_index, table, norm_gains, projections):
    core, section, here = lax.axis_index("c"), lax.axis_index("s"), lax.axis_index("y")
    column = lax.axis_index("x")

    own = half_of(table, tokens, core)
    got = swap(half_of(table, tokens, 1 - core), "c")
    away = feature_rows(after(projections, got), 1 - section)
    across = swap(away, "s")
    chunk = jnp.where(core == 0, jnp.stack([own, got]), jnp.stack([got, own]))
    first = exchange(chunk, "y", 8, 0)
    second = exchange(jnp.stack([chunk, first]), "y", 8, 1)
    later = after(projections, first)
    wo = later[1, 1]
    wo_section = swap(wo, "s")
    wo_beside = swap(wo, "c")
    mine = feature_rows(later, section)
    beside = swap(mine, "c")

    gains = lax.dynamic_slice_in_dim(norm_gains, section * 2048, 2048, axis=1)
    gains = gains.reshape(2, 8, 2, 128).transpose(1, 2, 0, 3)
    counts = multiplicities(after(nb_ids, first), nb_index).reshape(2, 2, 4, 4 * 1024)
    counts = lax.dynamic_index_in_dim(counts, core, 0, keepdims=False)
    counts = counts.transpose(1, 0, 2).reshape(4, 64, 128)
    sign = 1 - 2 * ((here + core) % 2)
    offsets = after(jnp.array([0, 1, -1, -2, 2, 3, -3, -4], jnp.int32), first)
    source = jnp.concatenate([(here + sign * offsets) % 8, core.reshape(1)]).astype(jnp.int32)
    third = exchange(second, "y", 8, 0)
    third, gains, counts, source = lax.optimization_barrier((third, gains, counts, source))
    fourth = exchange(third, "y", 8, 1)
    beside = (mine, beside)
    early, square, kv, query = project_early(source, (chunk, first, second, third), gains, beside)
    across = after(across, square)
    diagonal = swap(across, "c")
    far = (across, diagonal)
    late, squares, send, send_q = project_late(source, fourth, gains, early, far, square)
    other_q = swap(send_q, "s")
    other = swap(send, "s")
    queries = finish_queries(source, late, beside, query, squares, other_q, counts)
    queries = queries.reshape(8, 192, 128)
    queries = lax.all_to_all(queries, ("zh", "c"), 0, 0)
    keep = project_near(source, late, beside, kv)
    near, give = finish(keep, squares, other_q, other)
    order = block_order(column, core)
    wo_diagonal = swap(wo_section, "c")
    near = jnp.stack([near, swap(give, "c")])
    following = exchange(near, "x", 4, 0)
    beyond = exchange(jnp.stack([near, following]), "x", 4, 1)
    queries = queries.reshape(4, 2, 192, 128)
    counts = queries[:, :, 128:].reshape(4, 2, 2, 8, HALF).transpose(0, 3, 1, 2, 4)
    counts = counts.reshape(4, 8, 4, HALF)

    part, total = attend_near(order, queries, near, following, counts)
    parts = attend_far(order, queries, beyond, counts, part, total)
    parts = parts.reshape(16, ROWS, HEAD_DIM)
    parts = lax.all_to_all(parts, ("s", "zh", "c"), 0, 0)
    place = (section * 2 + core).astype(jnp.int32).reshape(1)
    weights = (wo, wo_beside, wo_section, wo_diagonal)
    out = mix(place, parts.reshape(2, 4, 2, ROWS, HEAD_DIM), weights)
    out = lax.all_to_all(out, ("s", "y", "c"), 0, 0)
    out = jnp.sum(out.reshape(2, 8, 2, SPAN, HEAD_DIM).astype(F32), axis=1)
    return out.astype(BF16).reshape(4 * SPAN, HEAD_DIM)


def solution(mesh):
    fine = Mesh(mesh.devices.reshape(2, 4, 4, 8, 2), ("s", "zh", "x", "y", "c"))
    batch, cols = ("zh", "x"), ("s", "y", "c")
    return jax.shard_map(
        step,
        mesh=fine,
        in_specs=(
            P(batch, cols),
            P(batch, None),
            P(batch, None),
            P(batch, cols),
            P(),
            P(None, None, None, cols),
        ),
        out_specs=P(batch, cols),
        check_vma=False,
    )
```

```python
import functools
import math

import jax
import jax.numpy as jnp
from jax import lax
from jax.experimental import pallas as pl
from jax.experimental.pallas import tpu as pltpu
from jax.sharding import Mesh
from jax.sharding import PartitionSpec as P

HEAD_DIM = 128
SPAN = 64
ROWS = 72
SHARD = 1000
HALF = 512
ROWS_IN = HALF + 128
EPS = 1e-06
SCALE = math.log2(math.e) / math.sqrt(HEAD_DIM)
F32 = jnp.float32
BF16 = jnp.bfloat16


def dot(a, b, dims):
    return lax.dot_general(a, b, (dims, ((), ())), preferred_element_type=F32)


def diagonal(shape):
    row = lax.broadcasted_iota(jnp.int32, shape, len(shape) - 2)
    lane = lax.broadcasted_iota(jnp.int32, shape, len(shape) - 1)
    return row == lane % SPAN


def sums_to_row(column):
    row = jnp.sum(jnp.where(diagonal((SPAN, 128)), column, 0.0), axis=0, keepdims=True)
    upper = row.astype(BF16).astype(F32)
    lane = lax.broadcasted_iota(jnp.int32, (1, 128), 1)
    return jnp.where(lane < SPAN, upper, row - upper)


def row_to_sums(row):
    return jnp.sum(jnp.where(diagonal((SPAN, 128)), row, 0.0), axis=1, keepdims=True)


def column_to_row(column):
    square = (128, 128)
    same = lax.broadcasted_iota(jnp.int32, square, 0) == lax.broadcasted_iota(jnp.int32, square, 1)
    return jnp.sum(jnp.where(same, column, 0.0), axis=0, keepdims=True)


def row_to_column(row):
    square = (128, 128)
    same = lax.broadcasted_iota(jnp.int32, square, 0) == lax.broadcasted_iota(jnp.int32, square, 1)
    return jnp.sum(jnp.where(same, row, 0.0), axis=1, keepdims=True)


def normed(ref, gain, lhs_ref, slot, square):
    for i in range(2):
        wide = ref[i].astype(F32)
        square = square + wide * wide
        lanes = slice(i * 128, (i + 1) * 128)
        lhs_ref[slot, :HALF, lanes] = (wide[:HALF] * gain[i, 0:1]).astype(BF16)
        lhs_ref[slot, HALF:, lanes] = (wide[HALF:] * gain[i, 1:2]).astype(BF16)
    return square


def columns(pieces):
    return jnp.concatenate(pieces, axis=1)


def rows_of(ref, which, source_ref, slots):
    picked = [
        ref[which, pl.ds(pl.multiple_of(source_ref[k] * 256, 256), 256), :] for k in slots
    ]
    return jnp.concatenate(picked, axis=0)


def early_kernel(source_ref, b0_ref, b1_ref, b2_ref, b3_ref, gain_ref, w0_ref, w1_ref, lhs_ref, square_ref, kv_ref, q_ref):
    square = jnp.zeros((ROWS_IN, 128), F32)
    pieces = [b0_ref, b1_ref, b2_ref.at[0], b2_ref.at[1], b3_ref.at[0], b3_ref.at[1]]
    for k, ref in enumerate(pieces):
        square = normed(ref, gain_ref[source_ref[k]], lhs_ref, k, square)
    square_ref[...] = square
    lhs = columns([lhs_ref[k] for k in range(6)])
    for m, ref in enumerate((w0_ref, w1_ref)):
        pair = columns([rows_of(ref, i, source_ref, range(6)) for i in range(2)])
        kv_ref[m] = dot(lhs[:HALF], pair, ((1,), (0,)))
        q_ref[m] = dot(lhs[HALF:], rows_of(ref, 2, source_ref, range(6)), ((1,), (0,)))


def project_early(source, blocks, gains, weights):
    vmem = pl.BlockSpec(memory_space=pltpu.VMEM)
    return pl.pallas_call(
        early_kernel,
        in_specs=[pl.BlockSpec(memory_space=pltpu.SMEM)] + [vmem] * 7,
        out_specs=[vmem] * 4,
        out_shape=[
            jax.ShapeDtypeStruct((6, ROWS_IN, 256), BF16),
            jax.ShapeDtypeStruct((ROWS_IN, 128), F32),
            jax.ShapeDtypeStruct((2, HALF, 256), F32),
            jax.ShapeDtypeStruct((2, 128, 128), F32),
        ],
        name="project_early",
    )(source, *blocks, gains, *weights)


def late_kernel(source_ref, b4_ref, gain_ref, early_ref, w0_ref, w1_ref, square_ref, lhs_ref, squares_ref, send_ref, send_q_ref):
    square = square_ref[...]
    for k in range(2):
        square = normed(b4_ref.at[k], gain_ref[source_ref[6 + k]], lhs_ref, k, square)
    sums = jnp.sum(square, axis=1, keepdims=True)
    tail = [column_to_row(sums[k * 128 : (k + 1) * 128]) for k in range(5)]
    squares = jnp.concatenate(tail + [jnp.zeros((3, 128), F32)], axis=0)
    squares_ref[...] = squares
    upper = squares.astype(BF16)
    send_q_ref[256:264] = upper
    send_q_ref[264:272] = (squares - upper.astype(F32)).astype(BF16)
    lhs = columns([early_ref[k] for k in range(6)] + [lhs_ref[k] for k in range(2)])
    for m, ref in enumerate((w0_ref, w1_ref)):
        pair = columns([rows_of(ref, i, source_ref, range(8)) for i in range(2)])
        both = dot(lhs[:HALF], pair, ((1,), (0,)))
        query = dot(lhs[HALF:], rows_of(ref, 2, source_ref, range(8)), ((1,), (0,)))
        send_q_ref[m * 128 : (m + 1) * 128] = query.astype(BF16)
        for i in range(2):
            send_ref[2 * m + i] = both[:, i * 128 : (i + 1) * 128].astype(BF16)


def whole_spec(*shape):
    return pl.BlockSpec(shape, lambda i, *_: (0,) * len(shape))


def picked_specs(depth, first):
    return [
        pl.BlockSpec((depth, 256, 128), lambda i, s, k=k: (first, s[6 + k], 0)) for k in range(2)
    ]


def project_late(source, block, gains, early, weights, square):
    return pl.pallas_call(
        late_kernel,
        grid_spec=pltpu.PrefetchScalarGridSpec(
            num_scalar_prefetch=1,
            grid=(1,),
            in_specs=[
                whole_spec(2, 2, ROWS_IN, 128),
                whole_spec(8, 2, 2, 128),
                whole_spec(6, ROWS_IN, 256),
                whole_spec(3, 2048, 128),
                whole_spec(3, 2048, 128),
                whole_spec(ROWS_IN, 128),
            ],
            out_specs=[
                whole_spec(2, ROWS_IN, 256),
                whole_spec(8, 128),
                whole_spec(4, HALF, 128),
                whole_spec(272, 128),
            ],
        ),
        out_shape=[
            jax.ShapeDtypeStruct((2, ROWS_IN, 256), BF16),
            jax.ShapeDtypeStruct((8, 128), F32),
            jax.ShapeDtypeStruct((4, HALF, 128), BF16),
            jax.ShapeDtypeStruct((272, 128), BF16),
        ],
        name="project_late",
    )(source, block, gains, early, *weights, square)


def rate_of(squares_ref, other_ref):
    theirs = other_ref[256:264].astype(F32) + other_ref[264:272].astype(F32)
    return lax.rsqrt((squares_ref[...] + theirs) * (1.0 / 4096) + EPS)


def query_kernel(source_ref, late_ref, w00_ref, w01_ref, w10_ref, w11_ref, near_ref, squares_ref, other_ref, count_ref, q_ref):
    core = source_ref[8]
    column = row_to_column(rate_of(squares_ref, other_ref)[4:5])
    lhs = columns([late_ref[k] for k in range(2)])
    for m, (one, two) in enumerate(((w00_ref, w01_ref), (w10_ref, w11_ref))):
        rows = jnp.concatenate([one[0], two[0]], axis=0)
        near = near_ref[m] + dot(lhs, rows, ((1,), (0,)))
        total = near + other_ref[m * 128 : (m + 1) * 128].astype(F32)
        value = (total * column).astype(BF16)
        for z in range(4):
            q_ref[z, core ^ m, :128] = value
            q_ref[z, m, 128:] = count_ref[z]


def finish_queries(source, late, weights, near, squares, other, counts):
    picked = picked_specs(1, 2)
    return pl.pallas_call(
        query_kernel,
        grid_spec=pltpu.PrefetchScalarGridSpec(
            num_scalar_prefetch=1,
            grid=(1,),
            in_specs=[
                pl.BlockSpec((2, 128, 256), lambda i, *_: (0, HALF // 128, 0)),
                *picked,
                *picked,
                whole_spec(2, 128, 128),
                whole_spec(8, 128),
                whole_spec(272, 128),
                whole_spec(4, 64, 128),
            ],
            out_specs=whole_spec(4, 2, 192, 128),
        ),
        out_shape=jax.ShapeDtypeStruct((4, 2, 192, 128), BF16),
        name="finish_queries",
    )(source, late, weights[0], weights[0], weights[1], weights[1], near, squares, other, counts)


def near_kernel(source_ref, late_ref, w00_ref, w01_ref, w10_ref, w11_ref, kv_ref, keep_ref):
    lhs = columns([late_ref[k] for k in range(2)])
    for m, (one, two) in enumerate(((w00_ref, w01_ref), (w10_ref, w11_ref))):
        rows = [jnp.concatenate([one[i], two[i]], axis=0) for i in range(2)]
        both = kv_ref[m] + dot(lhs, columns(rows), ((1,), (0,)))
        keep_ref[m, 0] = both[:, :128]
        keep_ref[m, 1] = both[:, 128:]


def project_near(source, late, weights, kv):
    picked = picked_specs(2, 0)
    return pl.pallas_call(
        near_kernel,
        grid_spec=pltpu.PrefetchScalarGridSpec(
            num_scalar_prefetch=1,
            grid=(1,),
            in_specs=[whole_spec(2, HALF, 256), *picked, *picked, whole_spec(2, HALF, 256)],
            out_specs=whole_spec(2, 2, HALF, 128),
        ),
        out_shape=jax.ShapeDtypeStruct((2, 2, HALF, 128), F32),
        name="project_near",
    )(source, late, weights[0], weights[0], weights[1], weights[1], kv)


def finish_kernel(keep_ref, squares_ref, other_q_ref, other_ref, own_ref, give_ref):
    rate = rate_of(squares_ref, other_q_ref)
    for k in range(4):
        rows = slice(k * 128, (k + 1) * 128)
        column = row_to_column(rate[k : k + 1])
        for m, ref in enumerate((own_ref, give_ref)):
            for i in range(2):
                total = keep_ref[m, i, rows] + other_ref[2 * m + i, rows, :].astype(F32)
                ref[i, rows] = (total * column).astype(BF16)


def finish(keep, squares, other_q, other):
    vmem = pl.BlockSpec(memory_space=pltpu.VMEM)
    half = jax.ShapeDtypeStruct((2, HALF, 128), BF16)
    return pl.pallas_call(
        finish_kernel,
        in_specs=[vmem] * 4,
        out_specs=[vmem] * 2,
        out_shape=[half, half],
        name="finish",
    )(keep, squares, other_q, other)


def partial(order_ref, first, queries, blocks, count_ref, expo_ref):
    total = jnp.zeros((4 * SPAN, 128), F32)
    for k, block in enumerate(blocks):
        lanes = slice(k * HALF, (k + 1) * HALF)
        bias = jnp.log2(count_ref[0, order_ref[first + k]].astype(F32))
        spread = jnp.broadcast_to(bias[:, None, :], (4, SPAN, HALF)).reshape(4 * SPAN, HALF)
        scores = dot(queries, block[0], ((1,), (1,)))
        expo = jnp.exp2(scores * SCALE + spread)
        expo_ref[:, lanes] = expo
        for i in range(HALF // 128):
            total = total + expo[:, i * 128 : (i + 1) * 128]
    total = jnp.sum(total, axis=1, keepdims=True)
    inverse = jnp.where(total > 0.0, 1.0 / total, 0.0)
    weights = (expo_ref[...] * inverse).astype(BF16)
    values = jnp.concatenate([block[1] for block in blocks], axis=0)
    return dot(weights, values, ((1,), (0,))), total


def near_attend_kernel(order_ref, q_ref, near_ref, up_ref, down_ref, count_ref, part_ref, total_ref, expo_ref):
    queries = jnp.concatenate([q_ref[0, 0], q_ref[0, 1]], axis=0)
    blocks = [ref.at[i] for ref in (near_ref, up_ref, down_ref) for i in range(2)]
    part, total = partial(order_ref, 0, queries, blocks, count_ref, expo_ref)
    part_ref[...] = part
    total_ref[...] = jnp.broadcast_to(total, (4 * SPAN, 128))


def far_attend_kernel(order_ref, q_ref, first_ref, second_ref, count_ref, part_ref, total_ref, out_ref, expo_ref):
    queries = jnp.concatenate([q_ref[0, 0], q_ref[0, 1]], axis=0)
    part, total = partial(order_ref, 6, queries, [first_ref, second_ref], count_ref, expo_ref)
    before = total_ref[:, 0:1]
    both = total + before
    inverse = jnp.where(both > 0.0, 1.0 / both, 0.0)
    part = (part * (total * inverse) + part_ref[...] * (before * inverse)).astype(BF16)
    for j in range(4):
        rows = slice(j * SPAN, (j + 1) * SPAN)
        out_ref[j // 2, 0, j % 2, :SPAN, :] = part[rows]
        tail = jnp.broadcast_to(sums_to_row(both[rows]), (ROWS - SPAN, 128))
        out_ref[j // 2, 0, j % 2, SPAN:, :] = tail.astype(BF16)


QUERY_SPEC = pl.BlockSpec((1, 2, 128, HEAD_DIM), lambda i, *_: (i, 0, 0, 0))
COUNT_SPEC = pl.BlockSpec((1, 8, 4, HALF), lambda i, *_: (i, 0, 0, 0))
PART_SPEC = pl.BlockSpec((4 * SPAN, HEAD_DIM), lambda i, *_: (i, 0))


def attend_near(order, queries, near, up, down, counts):
    block = pl.BlockSpec((2, 2, HALF, HEAD_DIM), lambda i, *_: (0, 0, 0, 0))
    return pl.pallas_call(
        near_attend_kernel,
        grid_spec=pltpu.PrefetchScalarGridSpec(
            num_scalar_prefetch=1,
            grid=(4,),
            in_specs=[QUERY_SPEC, block, block, block, COUNT_SPEC],
            out_specs=[PART_SPEC, PART_SPEC],
            scratch_shapes=[pltpu.VMEM((4 * SPAN, 6 * HALF), F32)],
        ),
        out_shape=[jax.ShapeDtypeStruct((16 * SPAN, HEAD_DIM), F32)] * 2,
        name="attend_near",
    )(order, queries, near, up, down, counts)


def attend_far(order, queries, first, second, counts, part, total):
    half = pl.BlockSpec((2, HALF, HEAD_DIM), lambda i, *_: (0, 0, 0))
    return pl.pallas_call(
        far_attend_kernel,
        grid_spec=pltpu.PrefetchScalarGridSpec(
            num_scalar_prefetch=1,
            grid=(4,),
            in_specs=[QUERY_SPEC, half, half, COUNT_SPEC, PART_SPEC, PART_SPEC],
            out_specs=pl.BlockSpec((2, 1, 2, ROWS, HEAD_DIM), lambda i, *_: (0, i, 0, 0, 0)),
            scratch_shapes=[pltpu.VMEM((4 * SPAN, 2 * HALF), F32)],
        ),
        out_shape=jax.ShapeDtypeStruct((2, 4, 2, ROWS, HEAD_DIM), BF16),
        name="attend_far",
    )(order, queries, first, second, counts, part, total)


def merge(parts):
    sums = [row_to_sums(p[SPAN : SPAN + 1, :].astype(F32)) for p in parts]
    total = functools.reduce(jnp.add, sums)
    mixed = functools.reduce(
        jnp.add, [p[:SPAN, :].astype(F32) * (s / total) for p, s in zip(parts, sums)]
    )
    return mixed, total


def mix_kernel(place_ref, parts_ref, w0_ref, w1_ref, w2_ref, w3_ref, out_ref, att_ref):
    @pl.when(pl.program_id(0) == 0)
    def _():
        for s in range(2):
            for c in range(2):
                mixed, _ = merge([parts_ref[s, z, c] for z in range(4)])
                att_ref[2 * s + c] = mixed.astype(BF16)

    place = place_ref[0]
    acc = None
    for k, ref in enumerate((w0_ref, w1_ref, w2_ref, w3_ref)):
        term = dot(att_ref[place ^ k], ref[...], ((1,), (1,)))
        acc = term if acc is None else acc + term
    for d in range(out_ref.shape[0]):
        out_ref[d] = acc[:, d * HEAD_DIM : (d + 1) * HEAD_DIM].astype(BF16)


def mix(place, parts, weights):
    step = 8
    weight = pl.BlockSpec((step * HEAD_DIM, HEAD_DIM), lambda i, *_: (i, 0))
    return pl.pallas_call(
        mix_kernel,
        grid_spec=pltpu.PrefetchScalarGridSpec(
            num_scalar_prefetch=1,
            grid=(32 // step,),
            in_specs=[
                pl.BlockSpec((2, 4, 2, ROWS, HEAD_DIM), lambda i, *_: (0, 0, 0, 0, 0)),
                weight,
                weight,
                weight,
                weight,
            ],
            out_specs=pl.BlockSpec((step, SPAN, HEAD_DIM), lambda i, *_: (i, 0, 0)),
            scratch_shapes=[pltpu.VMEM((4, SPAN, HEAD_DIM), BF16)],
        ),
        out_shape=jax.ShapeDtypeStruct((32, SPAN, HEAD_DIM), BF16),
        name="mix",
    )(place, parts, *weights)


def swap(value, axis):
    return lax.ppermute(value, axis, [(0, 1), (1, 0)])


def multiplicities(nb_ids, nb_index):
    place = nb_ids % SHARD
    place = jnp.where(place < HALF, place, place + (2 * HALF - SHARD))
    upper = (nb_ids // SHARD) * 32 + place // 32
    one_upper = (upper[:, :, None] == jnp.arange(512)).astype(BF16)
    one_lower = ((place % 32)[:, :, None] == jnp.arange(32)).astype(BF16)
    per_block = jnp.einsum("nip,niq->npq", one_upper, one_lower, preferred_element_type=F32)
    pick = jnp.sum((nb_index[:, :, None] == jnp.arange(8)).astype(F32), axis=1)
    counts = jnp.einsum(
        "gn,npq->gpq", pick.astype(BF16), per_block.astype(BF16), preferred_element_type=F32
    )
    return counts.astype(BF16)


def half_of(table, tokens, core):
    rows = lax.dynamic_slice_in_dim(table, core * (SHARD - HALF), HALF)
    return jnp.concatenate([rows, lax.dynamic_slice_in_dim(tokens, core * 128, 128)], axis=0)


def pairs(size, turn):
    out = []
    for place in range(size):
        for core in range(2):
            spot = (place - core) % size
            other = spot ^ 1 if turn == 0 else spot + (1 if spot % 2 else -1)
            out.append((2 * place + core, 2 * ((other + core) % size) + core))
    return out


def exchange(value, axis, size, turn):
    return lax.ppermute(value, (axis, "c"), pairs(size, turn))


def after(value, *others):
    return lax.optimization_barrier((value, *others))[0]


def feature_rows(projections, section):
    start = section * 2048
    encoder = lax.dynamic_slice(projections, (0, 0, start, 0), (1, 2, 2048, 128))
    decoder = lax.dynamic_slice(projections, (1, 0, start, 0), (1, 1, 2048, 128))
    return jnp.concatenate([encoder[0], decoder[0]], axis=0)


def block_order(column, core):
    offsets = jnp.array([0, 0, -1, -1, 1, 1, 2, 2], jnp.int32)
    origin = (column + offsets) % 4
    half = (core + jnp.arange(8)) % 2
    return (2 * origin + half).astype(jnp.int32)


def step(tokens, nb_ids, nb_index, table, norm_gains, projections):
    core, section, here = lax.axis_index("c"), lax.axis_index("s"), lax.axis_index("y")
    column = lax.axis_index("x")

    own = half_of(table, tokens, core)
    got = swap(half_of(table, tokens, 1 - core), "c")
    away = feature_rows(after(projections, got), 1 - section)
    across = swap(away, "s")
    chunk = jnp.where(core == 0, jnp.stack([own, got]), jnp.stack([got, own]))
    first = exchange(chunk, "y", 8, 0)
    second = exchange(jnp.stack([chunk, first]), "y", 8, 1)
    later = after(projections, first)
    wo = later[1, 1]
    wo_section = swap(wo, "s")
    wo_beside = swap(wo, "c")
    mine = feature_rows(later, section)
    beside = swap(mine, "c")

    gains = lax.dynamic_slice_in_dim(norm_gains, section * 2048, 2048, axis=1)
    gains = gains.reshape(2, 8, 2, 128).transpose(1, 2, 0, 3)
    counts = multiplicities(after(nb_ids, first), nb_index).reshape(2, 2, 4, 4 * 1024)
    counts = lax.dynamic_index_in_dim(counts, core, 0, keepdims=False)
    counts = counts.transpose(1, 0, 2).reshape(4, 64, 128)
    sign = 1 - 2 * ((here + core) % 2)
    offsets = after(jnp.array([0, 1, -1, -2, 2, 3, -3, -4], jnp.int32), first)
    source = jnp.concatenate([(here + sign * offsets) % 8, core.reshape(1)]).astype(jnp.int32)
    third = exchange(second, "y", 8, 0)
    third, gains, counts, source = lax.optimization_barrier((third, gains, counts, source))
    fourth = exchange(third, "y", 8, 1)
    beside = (mine, beside)
    early, square, kv, query = project_early(source, (chunk, first, second, third), gains, beside)
    across = after(across, square)
    diagonal = swap(across, "c")
    far = (across, diagonal)
    late, squares, send, send_q = project_late(source, fourth, gains, early, far, square)
    other_q = swap(send_q, "s")
    other = swap(send, "s")
    queries = finish_queries(source, late, beside, query, squares, other_q, counts)
    queries = queries.reshape(8, 192, 128)
    queries = lax.all_to_all(queries, ("zh", "c"), 0, 0)
    keep = project_near(source, late, beside, kv)
    near, give = finish(keep, squares, other_q, other)
    order = block_order(column, core)
    wo_diagonal = swap(wo_section, "c")
    near = jnp.stack([near, swap(give, "c")])
    ahead = [(i, (i + 1) % 4) for i in range(4)]
    back = [(i, (i - 1) % 4) for i in range(4)]
    up = lax.ppermute(near, "x", ahead)
    down = lax.ppermute(near, "x", back)
    up_far = lax.ppermute(up[0], "x", ahead)
    down_far = lax.ppermute(down[1], "x", back)
    queries = queries.reshape(4, 2, 192, 128)
    counts = queries[:, :, 128:].reshape(4, 2, 2, 8, HALF).transpose(0, 3, 1, 2, 4)
    counts = counts.reshape(4, 8, 4, HALF)

    part, total = attend_near(order, queries, near, up, down, counts)
    parts = attend_far(order, queries, up_far, down_far, counts, part, total)
    parts = parts.reshape(16, ROWS, HEAD_DIM)
    parts = lax.all_to_all(parts, ("s", "zh", "c"), 0, 0)
    place = (section * 2 + core).astype(jnp.int32).reshape(1)
    weights = (wo, wo_beside, wo_section, wo_diagonal)
    out = mix(place, parts.reshape(2, 4, 2, ROWS, HEAD_DIM), weights)
    out = lax.all_to_all(out, ("s", "y", "c"), 0, 0)
    out = jnp.sum(out.reshape(2, 8, 2, SPAN, HEAD_DIM).astype(F32), axis=1)
    return out.astype(BF16).reshape(4 * SPAN, HEAD_DIM)


def solution(mesh):
    fine = Mesh(mesh.devices.reshape(2, 4, 4, 8, 2), ("s", "zh", "x", "y", "c"))
    batch, cols = ("zh", "x"), ("s", "y", "c")
    return jax.shard_map(
        step,
        mesh=fine,
        in_specs=(
            P(batch, cols),
            P(batch, None),
            P(batch, None),
            P(batch, cols),
            P(),
            P(None, None, None, cols),
        ),
        out_specs=P(batch, cols),
        check_vma=False,
    )
```

```python
import functools
import math

import jax
import jax.numpy as jnp
from jax import lax
from jax.experimental import pallas as pl
from jax.experimental.pallas import tpu as pltpu
from jax.sharding import Mesh
from jax.sharding import PartitionSpec as P

HEAD_DIM = 128
SPAN = 64
ROWS = 72
SHARD = 1000
HALF = 512
ROWS_IN = HALF + 128
EPS = 1e-06
SCALE = math.log2(math.e) / math.sqrt(HEAD_DIM)
F32 = jnp.float32
BF16 = jnp.bfloat16


def dot(a, b, dims):
    return lax.dot_general(a, b, (dims, ((), ())), preferred_element_type=F32)


def diagonal(shape):
    row = lax.broadcasted_iota(jnp.int32, shape, len(shape) - 2)
    lane = lax.broadcasted_iota(jnp.int32, shape, len(shape) - 1)
    return row == lane % SPAN


def sums_to_row(column):
    row = jnp.sum(jnp.where(diagonal((SPAN, 128)), column, 0.0), axis=0, keepdims=True)
    upper = row.astype(BF16).astype(F32)
    lane = lax.broadcasted_iota(jnp.int32, (1, 128), 1)
    return jnp.where(lane < SPAN, upper, row - upper)


def row_to_sums(row):
    return jnp.sum(jnp.where(diagonal((SPAN, 128)), row, 0.0), axis=1, keepdims=True)


def column_to_row(column):
    square = (128, 128)
    same = lax.broadcasted_iota(jnp.int32, square, 0) == lax.broadcasted_iota(jnp.int32, square, 1)
    return jnp.sum(jnp.where(same, column, 0.0), axis=0, keepdims=True)


def row_to_column(row):
    square = (128, 128)
    same = lax.broadcasted_iota(jnp.int32, square, 0) == lax.broadcasted_iota(jnp.int32, square, 1)
    return jnp.sum(jnp.where(same, row, 0.0), axis=1, keepdims=True)


def normed(ref, gain, lhs_ref, slot, square):
    for i in range(2):
        wide = ref[i].astype(F32)
        square = square + wide * wide
        lanes = slice(i * 128, (i + 1) * 128)
        lhs_ref[slot, :HALF, lanes] = (wide[:HALF] * gain[i, 0:1]).astype(BF16)
        lhs_ref[slot, HALF:, lanes] = (wide[HALF:] * gain[i, 1:2]).astype(BF16)
    return square


def columns(pieces):
    return jnp.concatenate(pieces, axis=1)


def rows_of(ref, which, source_ref, slots):
    picked = [
        ref[which, pl.ds(pl.multiple_of(source_ref[k] * 256, 256), 256), :] for k in slots
    ]
    return jnp.concatenate(picked, axis=0)


def early_kernel(source_ref, b0_ref, b1_ref, b2_ref, b3_ref, gain_ref, w0_ref, w1_ref, lhs_ref, square_ref, kv_ref, q_ref):
    square = jnp.zeros((ROWS_IN, 128), F32)
    pieces = [b0_ref, b1_ref, b2_ref.at[0], b2_ref.at[1], b3_ref.at[0], b3_ref.at[1]]
    for k, ref in enumerate(pieces):
        square = normed(ref, gain_ref[source_ref[k]], lhs_ref, k, square)
    square_ref[...] = square
    lhs = columns([lhs_ref[k] for k in range(6)])
    for m, ref in enumerate((w0_ref, w1_ref)):
        pair = columns([rows_of(ref, i, source_ref, range(6)) for i in range(2)])
        kv_ref[m] = dot(lhs[:HALF], pair, ((1,), (0,)))
        q_ref[m] = dot(lhs[HALF:], rows_of(ref, 2, source_ref, range(6)), ((1,), (0,)))


def project_early(source, blocks, gains, weights):
    vmem = pl.BlockSpec(memory_space=pltpu.VMEM)
    return pl.pallas_call(
        early_kernel,
        in_specs=[pl.BlockSpec(memory_space=pltpu.SMEM)] + [vmem] * 7,
        out_specs=[vmem] * 4,
        out_shape=[
            jax.ShapeDtypeStruct((6, ROWS_IN, 256), BF16),
            jax.ShapeDtypeStruct((ROWS_IN, 128), F32),
            jax.ShapeDtypeStruct((2, HALF, 256), F32),
            jax.ShapeDtypeStruct((2, 128, 128), F32),
        ],
        name="project_early",
    )(source, *blocks, gains, *weights)


def late_kernel(source_ref, b4_ref, gain_ref, early_ref, w0_ref, w1_ref, square_ref, lhs_ref, squares_ref, send_ref, send_q_ref):
    square = square_ref[...]
    for k in range(2):
        square = normed(b4_ref.at[k], gain_ref[source_ref[6 + k]], lhs_ref, k, square)
    sums = jnp.sum(square, axis=1, keepdims=True)
    tail = [column_to_row(sums[k * 128 : (k + 1) * 128]) for k in range(5)]
    squares = jnp.concatenate(tail + [jnp.zeros((3, 128), F32)], axis=0)
    squares_ref[...] = squares
    upper = squares.astype(BF16)
    send_q_ref[256:264] = upper
    send_q_ref[264:272] = (squares - upper.astype(F32)).astype(BF16)
    lhs = columns([early_ref[k] for k in range(6)] + [lhs_ref[k] for k in range(2)])
    for m, ref in enumerate((w0_ref, w1_ref)):
        pair = columns([rows_of(ref, i, source_ref, range(8)) for i in range(2)])
        both = dot(lhs[:HALF], pair, ((1,), (0,)))
        query = dot(lhs[HALF:], rows_of(ref, 2, source_ref, range(8)), ((1,), (0,)))
        send_q_ref[m * 128 : (m + 1) * 128] = query.astype(BF16)
        for i in range(2):
            send_ref[2 * m + i] = both[:, i * 128 : (i + 1) * 128].astype(BF16)


def whole_spec(*shape):
    return pl.BlockSpec(shape, lambda i, *_: (0,) * len(shape))


def picked_specs(depth, first):
    return [
        pl.BlockSpec((depth, 256, 128), lambda i, s, k=k: (first, s[6 + k], 0)) for k in range(2)
    ]


def project_late(source, block, gains, early, weights, square):
    return pl.pallas_call(
        late_kernel,
        grid_spec=pltpu.PrefetchScalarGridSpec(
            num_scalar_prefetch=1,
            grid=(1,),
            in_specs=[
                whole_spec(2, 2, ROWS_IN, 128),
                whole_spec(8, 2, 2, 128),
                whole_spec(6, ROWS_IN, 256),
                whole_spec(3, 2048, 128),
                whole_spec(3, 2048, 128),
                whole_spec(ROWS_IN, 128),
            ],
            out_specs=[
                whole_spec(2, ROWS_IN, 256),
                whole_spec(8, 128),
                whole_spec(4, HALF, 128),
                whole_spec(272, 128),
            ],
        ),
        out_shape=[
            jax.ShapeDtypeStruct((2, ROWS_IN, 256), BF16),
            jax.ShapeDtypeStruct((8, 128), F32),
            jax.ShapeDtypeStruct((4, HALF, 128), BF16),
            jax.ShapeDtypeStruct((272, 128), BF16),
        ],
        name="project_late",
    )(source, block, gains, early, *weights, square)


def rate_of(squares_ref, other_ref):
    theirs = other_ref[256:264].astype(F32) + other_ref[264:272].astype(F32)
    return lax.rsqrt((squares_ref[...] + theirs) * (1.0 / 4096) + EPS)


def query_kernel(source_ref, late_ref, w00_ref, w01_ref, w10_ref, w11_ref, near_ref, squares_ref, other_ref, count_ref, q_ref):
    core = source_ref[8]
    column = row_to_column(rate_of(squares_ref, other_ref)[4:5])
    lhs = columns([late_ref[k] for k in range(2)])
    for m, (one, two) in enumerate(((w00_ref, w01_ref), (w10_ref, w11_ref))):
        rows = jnp.concatenate([one[0], two[0]], axis=0)
        near = near_ref[m] + dot(lhs, rows, ((1,), (0,)))
        total = near + other_ref[m * 128 : (m + 1) * 128].astype(F32)
        value = (total * column).astype(BF16)
        for z in range(4):
            q_ref[z, core ^ m, :128] = value
            q_ref[z, m, 128:] = count_ref[z]


def finish_queries(source, late, weights, near, squares, other, counts):
    picked = picked_specs(1, 2)
    return pl.pallas_call(
        query_kernel,
        grid_spec=pltpu.PrefetchScalarGridSpec(
            num_scalar_prefetch=1,
            grid=(1,),
            in_specs=[
                pl.BlockSpec((2, 128, 256), lambda i, *_: (0, HALF // 128, 0)),
                *picked,
                *picked,
                whole_spec(2, 128, 128),
                whole_spec(8, 128),
                whole_spec(272, 128),
                whole_spec(4, 64, 128),
            ],
            out_specs=whole_spec(4, 2, 192, 128),
        ),
        out_shape=jax.ShapeDtypeStruct((4, 2, 192, 128), BF16),
        name="finish_queries",
    )(source, late, weights[0], weights[0], weights[1], weights[1], near, squares, other, counts)


def near_kernel(source_ref, late_ref, w00_ref, w01_ref, w10_ref, w11_ref, kv_ref, keep_ref):
    lhs = columns([late_ref[k] for k in range(2)])
    for m, (one, two) in enumerate(((w00_ref, w01_ref), (w10_ref, w11_ref))):
        rows = [jnp.concatenate([one[i], two[i]], axis=0) for i in range(2)]
        both = kv_ref[m] + dot(lhs, columns(rows), ((1,), (0,)))
        keep_ref[m, 0] = both[:, :128]
        keep_ref[m, 1] = both[:, 128:]


def project_near(source, late, weights, kv):
    picked = picked_specs(2, 0)
    return pl.pallas_call(
        near_kernel,
        grid_spec=pltpu.PrefetchScalarGridSpec(
            num_scalar_prefetch=1,
            grid=(1,),
            in_specs=[whole_spec(2, HALF, 256), *picked, *picked, whole_spec(2, HALF, 256)],
            out_specs=whole_spec(2, 2, HALF, 128),
        ),
        out_shape=jax.ShapeDtypeStruct((2, 2, HALF, 128), F32),
        name="project_near",
    )(source, late, weights[0], weights[0], weights[1], weights[1], kv)


def finish_kernel(keep_ref, squares_ref, other_q_ref, other_ref, own_ref, give_ref):
    rate = rate_of(squares_ref, other_q_ref)
    for k in range(4):
        rows = slice(k * 128, (k + 1) * 128)
        column = row_to_column(rate[k : k + 1])
        for m, ref in enumerate((own_ref, give_ref)):
            for i in range(2):
                total = keep_ref[m, i, rows] + other_ref[2 * m + i, rows, :].astype(F32)
                ref[i, rows] = (total * column).astype(BF16)


def finish(keep, squares, other_q, other):
    vmem = pl.BlockSpec(memory_space=pltpu.VMEM)
    half = jax.ShapeDtypeStruct((2, HALF, 128), BF16)
    return pl.pallas_call(
        finish_kernel,
        in_specs=[vmem] * 4,
        out_specs=[vmem] * 2,
        out_shape=[half, half],
        name="finish",
    )(keep, squares, other_q, other)


def partial(order_ref, first, queries, blocks, count_ref, expo_ref):
    total = jnp.zeros((4 * SPAN, 128), F32)
    for k, block in enumerate(blocks):
        lanes = slice(k * HALF, (k + 1) * HALF)
        bias = jnp.log2(count_ref[0, order_ref[first + k]].astype(F32))
        spread = jnp.broadcast_to(bias[:, None, :], (4, SPAN, HALF)).reshape(4 * SPAN, HALF)
        scores = dot(queries, block[0], ((1,), (1,)))
        expo = jnp.exp2(scores * SCALE + spread)
        expo_ref[:, lanes] = expo
        for i in range(HALF // 128):
            total = total + expo[:, i * 128 : (i + 1) * 128]
    total = jnp.sum(total, axis=1, keepdims=True)
    inverse = jnp.where(total > 0.0, 1.0 / total, 0.0)
    weights = (expo_ref[...] * inverse).astype(BF16)
    values = jnp.concatenate([block[1] for block in blocks], axis=0)
    return dot(weights, values, ((1,), (0,))), total


def near_attend_kernel(order_ref, q_ref, near_ref, up_ref, down_ref, count_ref, part_ref, total_ref, expo_ref):
    queries = jnp.concatenate([q_ref[0, 0], q_ref[0, 1]], axis=0)
    blocks = [ref.at[i] for ref in (near_ref, up_ref, down_ref) for i in range(2)]
    part, total = partial(order_ref, 0, queries, blocks, count_ref, expo_ref)
    part_ref[...] = part
    total_ref[...] = jnp.broadcast_to(total, (4 * SPAN, 128))


def far_attend_kernel(order_ref, q_ref, far_ref, count_ref, part_ref, total_ref, out_ref, expo_ref):
    queries = jnp.concatenate([q_ref[0, 0], q_ref[0, 1]], axis=0)
    part, total = partial(order_ref, 6, queries, [far_ref.at[0], far_ref.at[1]], count_ref, expo_ref)
    before = total_ref[:, 0:1]
    both = total + before
    inverse = jnp.where(both > 0.0, 1.0 / both, 0.0)
    part = (part * (total * inverse) + part_ref[...] * (before * inverse)).astype(BF16)
    for j in range(4):
        rows = slice(j * SPAN, (j + 1) * SPAN)
        out_ref[j // 2, 0, j % 2, :SPAN, :] = part[rows]
        tail = jnp.broadcast_to(sums_to_row(both[rows]), (ROWS - SPAN, 128))
        out_ref[j // 2, 0, j % 2, SPAN:, :] = tail.astype(BF16)


QUERY_SPEC = pl.BlockSpec((1, 2, 128, HEAD_DIM), lambda i, *_: (i, 0, 0, 0))
COUNT_SPEC = pl.BlockSpec((1, 8, 4, HALF), lambda i, *_: (i, 0, 0, 0))
PART_SPEC = pl.BlockSpec((4 * SPAN, HEAD_DIM), lambda i, *_: (i, 0))


def attend_near(order, queries, near, up, down, counts):
    block = pl.BlockSpec((2, 2, HALF, HEAD_DIM), lambda i, *_: (0, 0, 0, 0))
    return pl.pallas_call(
        near_attend_kernel,
        grid_spec=pltpu.PrefetchScalarGridSpec(
            num_scalar_prefetch=1,
            grid=(4,),
            in_specs=[QUERY_SPEC, block, block, block, COUNT_SPEC],
            out_specs=[PART_SPEC, PART_SPEC],
            scratch_shapes=[pltpu.VMEM((4 * SPAN, 6 * HALF), F32)],
        ),
        out_shape=[jax.ShapeDtypeStruct((16 * SPAN, HEAD_DIM), F32)] * 2,
        name="attend_near",
    )(order, queries, near, up, down, counts)


def attend_far(order, queries, far, counts, part, total):
    block = pl.BlockSpec((2, 2, HALF, HEAD_DIM), lambda i, *_: (0, 0, 0, 0))
    return pl.pallas_call(
        far_attend_kernel,
        grid_spec=pltpu.PrefetchScalarGridSpec(
            num_scalar_prefetch=1,
            grid=(4,),
            in_specs=[QUERY_SPEC, block, COUNT_SPEC, PART_SPEC, PART_SPEC],
            out_specs=pl.BlockSpec((2, 1, 2, ROWS, HEAD_DIM), lambda i, *_: (0, i, 0, 0, 0)),
            scratch_shapes=[pltpu.VMEM((4 * SPAN, 2 * HALF), F32)],
        ),
        out_shape=jax.ShapeDtypeStruct((2, 4, 2, ROWS, HEAD_DIM), BF16),
        name="attend_far",
    )(order, queries, far, counts, part, total)


def merge(parts):
    sums = [row_to_sums(p[SPAN : SPAN + 1, :].astype(F32)) for p in parts]
    total = functools.reduce(jnp.add, sums)
    mixed = functools.reduce(
        jnp.add, [p[:SPAN, :].astype(F32) * (s / total) for p, s in zip(parts, sums)]
    )
    return mixed, total


def mix_kernel(place_ref, parts_ref, w0_ref, w1_ref, w2_ref, w3_ref, out_ref, att_ref):
    @pl.when(pl.program_id(0) == 0)
    def _():
        for s in range(2):
            for c in range(2):
                mixed, _ = merge([parts_ref[s, z, c] for z in range(4)])
                att_ref[2 * s + c] = mixed.astype(BF16)

    place = place_ref[0]
    acc = None
    for k, ref in enumerate((w0_ref, w1_ref, w2_ref, w3_ref)):
        term = dot(att_ref[place ^ k], ref[...], ((1,), (1,)))
        acc = term if acc is None else acc + term
    for d in range(out_ref.shape[0]):
        out_ref[d] = acc[:, d * HEAD_DIM : (d + 1) * HEAD_DIM].astype(BF16)


def mix(place, parts, weights):
    step = 8
    weight = pl.BlockSpec((step * HEAD_DIM, HEAD_DIM), lambda i, *_: (i, 0))
    return pl.pallas_call(
        mix_kernel,
        grid_spec=pltpu.PrefetchScalarGridSpec(
            num_scalar_prefetch=1,
            grid=(32 // step,),
            in_specs=[
                pl.BlockSpec((2, 4, 2, ROWS, HEAD_DIM), lambda i, *_: (0, 0, 0, 0, 0)),
                weight,
                weight,
                weight,
                weight,
            ],
            out_specs=pl.BlockSpec((step, SPAN, HEAD_DIM), lambda i, *_: (i, 0, 0)),
            scratch_shapes=[pltpu.VMEM((4, SPAN, HEAD_DIM), BF16)],
        ),
        out_shape=jax.ShapeDtypeStruct((32, SPAN, HEAD_DIM), BF16),
        name="mix",
    )(place, parts, *weights)


def swap(value, axis):
    return lax.ppermute(value, axis, [(0, 1), (1, 0)])


def multiplicities(nb_ids, nb_index):
    place = nb_ids % SHARD
    place = jnp.where(place < HALF, place, place + (2 * HALF - SHARD))
    upper = (nb_ids // SHARD) * 32 + place // 32
    one_upper = (upper[:, :, None] == jnp.arange(512)).astype(BF16)
    one_lower = ((place % 32)[:, :, None] == jnp.arange(32)).astype(BF16)
    per_block = jnp.einsum("nip,niq->npq", one_upper, one_lower, preferred_element_type=F32)
    pick = jnp.sum((nb_index[:, :, None] == jnp.arange(8)).astype(F32), axis=1)
    counts = jnp.einsum(
        "gn,npq->gpq", pick.astype(BF16), per_block.astype(BF16), preferred_element_type=F32
    )
    return counts.astype(BF16)


def half_of(table, tokens, core):
    rows = lax.dynamic_slice_in_dim(table, core * (SHARD - HALF), HALF)
    return jnp.concatenate([rows, lax.dynamic_slice_in_dim(tokens, core * 128, 128)], axis=0)


def pairs(size, turn):
    out = []
    for place in range(size):
        for core in range(2):
            spot = (place - core) % size
            other = spot ^ 1 if turn == 0 else spot + (1 if spot % 2 else -1)
            out.append((2 * place + core, 2 * ((other + core) % size) + core))
    return out


def exchange(value, axis, size, turn):
    return lax.ppermute(value, (axis, "c"), pairs(size, turn))


def after(value, *others):
    return lax.optimization_barrier((value, *others))[0]


def feature_rows(projections, section):
    start = section * 2048
    encoder = lax.dynamic_slice(projections, (0, 0, start, 0), (1, 2, 2048, 128))
    decoder = lax.dynamic_slice(projections, (1, 0, start, 0), (1, 1, 2048, 128))
    return jnp.concatenate([encoder[0], decoder[0]], axis=0)


def block_order(column, core):
    sign = 1 - 2 * ((column + core) % 2)
    offsets = jnp.array([0, 0, 1, 1, -1, -1, -2, -2], jnp.int32)
    origin = (column + sign * offsets) % 4
    half = (core + jnp.arange(8)) % 2
    return (2 * origin + half).astype(jnp.int32)


def step(tokens, nb_ids, nb_index, table, norm_gains, projections):
    core, section, here = lax.axis_index("c"), lax.axis_index("s"), lax.axis_index("y")
    column = lax.axis_index("x")

    own = half_of(table, tokens, core)
    got = swap(half_of(table, tokens, 1 - core), "c")
    away = feature_rows(after(projections, got), 1 - section)
    across = swap(away, "s")
    chunk = jnp.where(core == 0, jnp.stack([own, got]), jnp.stack([got, own]))
    first = exchange(chunk, "y", 8, 0)
    second = exchange(jnp.stack([chunk, first]), "y", 8, 1)
    later = after(projections, first)
    wo = later[1, 1]
    wo_section = swap(wo, "s")
    wo_beside = swap(wo, "c")
    mine = feature_rows(later, section)
    beside = swap(mine, "c")

    gains = lax.dynamic_slice_in_dim(norm_gains, section * 2048, 2048, axis=1)
    gains = gains.reshape(2, 8, 2, 128).transpose(1, 2, 0, 3)
    counts = multiplicities(after(nb_ids, first), nb_index).reshape(2, 2, 4, 4 * 1024)
    counts = lax.dynamic_index_in_dim(counts, core, 0, keepdims=False)
    counts = counts.transpose(1, 0, 2).reshape(4, 64, 128)
    sign = 1 - 2 * ((here + core) % 2)
    offsets = after(jnp.array([0, 1, -1, -2, 2, 3, -3, -4], jnp.int32), first)
    source = jnp.concatenate([(here + sign * offsets) % 8, core.reshape(1)]).astype(jnp.int32)
    third = exchange(second, "y", 8, 0)
    third, gains, counts, source = lax.optimization_barrier((third, gains, counts, source))
    fourth = exchange(third, "y", 8, 1)
    beside = (mine, beside)
    early, square, kv, query = project_early(source, (chunk, first, second, third), gains, beside)
    across = after(across, square)
    diagonal = swap(across, "c")
    far = (across, diagonal)
    late, squares, send, send_q = project_late(source, fourth, gains, early, far, square)
    other_q = swap(send_q, "s")
    other = swap(send, "s")
    queries = finish_queries(source, late, beside, query, squares, other_q, counts)
    queries = queries.reshape(8, 192, 128)
    queries = lax.all_to_all(queries, ("zh", "c"), 0, 0)
    keep = project_near(source, late, beside, kv)
    near, give = finish(keep, squares, other_q, other)
    order = block_order(column, core)
    wo_diagonal = swap(wo_section, "c")
    near = jnp.stack([near, swap(give, "c")])
    following = exchange(near, "x", 4, 0)
    preceding = exchange(near, "x", 4, 1)
    beyond = exchange(following, "x", 4, 1)
    queries = queries.reshape(4, 2, 192, 128)
    counts = queries[:, :, 128:].reshape(4, 2, 2, 8, HALF).transpose(0, 3, 1, 2, 4)
    counts = counts.reshape(4, 8, 4, HALF)

    part, total = attend_near(order, queries, near, following, preceding, counts)
    parts = attend_far(order, queries, beyond, counts, part, total)
    parts = parts.reshape(16, ROWS, HEAD_DIM)
    parts = lax.all_to_all(parts, ("s", "zh", "c"), 0, 0)
    place = (section * 2 + core).astype(jnp.int32).reshape(1)
    weights = (wo, wo_beside, wo_section, wo_diagonal)
    out = mix(place, parts.reshape(2, 4, 2, ROWS, HEAD_DIM), weights)
    out = lax.all_to_all(out, ("s", "y", "c"), 0, 0)
    out = jnp.sum(out.reshape(2, 8, 2, SPAN, HEAD_DIM).astype(F32), axis=1)
    return out.astype(BF16).reshape(4 * SPAN, HEAD_DIM)


def solution(mesh):
    fine = Mesh(mesh.devices.reshape(2, 4, 4, 8, 2), ("s", "zh", "x", "y", "c"))
    batch, cols = ("zh", "x"), ("s", "y", "c")
    return jax.shard_map(
        step,
        mesh=fine,
        in_specs=(
            P(batch, cols),
            P(batch, None),
            P(batch, None),
            P(batch, cols),
            P(),
            P(None, None, None, cols),
        ),
        out_specs=P(batch, cols),
        check_vma=False,
    )
```
